32 devices in a mesh: seq: 8 (over z, y), tp: 4 (over x, core).
Axes of the slice: x: 2, y: 2, z: 4, core: 2. Of those that a mesh axis runs over, the one named last changes fastest.
Arguments:
- tokens: bfloat16 [16384, 1024], P(('seq', 'tp')), may hold values from -6 to 6
- doc_flags: int32 [16384], P('seq'), may hold values 0 or 1
- reset_flags: int32 [32], P('seq'), may hold values 0 or 1
- state_init: float32 [512, 1024], P(None, 'tp'), may hold values from -6 to 6
- gain_attn: float32 [1024], replicated, may hold values from 0.5 to 1.5
- w_query: bfloat16 [1024, 1024], P(None, 'tp'), may hold values from -0.1875 to 0.1875
- w_key: bfloat16 [1024, 1024], P(None, 'tp'), may hold values from -0.1875 to 0.1875
- w_value: bfloat16 [1024, 1024], P(None, 'tp'), may hold values from -0.1875 to 0.1875
- w_output: bfloat16 [1024, 1024], P('tp'), may hold values from -2 to 2
- bias_table: float32 [8, 32], P('tp'), may hold values from -4 to 4
- state_queries: bfloat16 [512, 1024], P(None, 'tp'), may hold values from -8 to 8
- gate_logits: float32 [1024], P('tp'), may hold values from -1 to 5
- gain_mlp: float32 [1024], replicated, may hold values from 0.5 to 1.5
- w_hidden: bfloat16 [1024, 4096], P(None, 'tp'), may hold values from -0.1875 to 0.1875
- w_return: bfloat16 [4096, 1024], P('tp'), may hold values from -0.09375 to 0.09375
- cotangent: bfloat16 [16384, 1024], P(('seq', 'tp')), may hold values from -6 to 6
Outputs:
- out_tokens: bfloat16 [16384, 1024], P(('seq', 'tp'))
- block_states: float32 [32, 512, 1024], P('seq', None, 'tp')
- grad_tokens: float32 [16384, 1024], P(('seq', 'tp'))
- grad_state: float32 [512, 1024], P('seq', 'tp')
- grad_gain_attn: float32 [1024], replicated
- grad_query: float32 [1024, 1024], P('seq', 'tp')
- grad_key: float32 [1024, 1024], P('seq', 'tp')
- grad_value: float32 [1024, 1024], P('seq', 'tp')
- grad_output: float32 [1024, 1024], P('tp', 'seq')
- grad_bias: float32 [8, 32], replicated
- grad_state_queries: float32 [512, 1024], P('seq', 'tp')
- grad_gate: float32 [1024], replicated
- grad_gain_mlp: float32 [1024], replicated
- grad_hidden: float32 [1024, 4096], P('seq', 'tp')
- grad_return: float32 [4096, 1024], P('tp', 'seq')
The draws below stay inside these ranges and needn't reach their ends.
Inputs may be any that keep to these rules, and one draw needn't show every extreme that they name: `doc_flags`: 1 marks the first token of a document.
All inputs are finite; a program needn't handle non-finite values. No bound on the sum of `doc_flags` on one device may be relied on, other than what follows from the above.
Results may differ from the reference program's by a relative error of at most 0.02.
Values may be sent and summed in bfloat16 or wider, within the bound.
No kernel may reach another device: no remote copies, remote signals or barrier semaphores. Data moves between devices by JAX's collectives and lax.ppermute only.
A program may use at most 320 MiB of HBM per device.

```python
import math
import jax
import jax.numpy as jnp
from jax import lax

D = 1024
H = 8
FF = 4096
NS = 512
BLOCK = 512
BUCKETS = 32
FAR = 128
NBLK = 32
TOKENS = 16384


def place_ends(drawn, own_key, low, top_value):
    shape = drawn.shape
    index_at = [jax.random.randint(jax.random.fold_in(own_key, axis), (), 0, shape[axis]) for axis in range(len(shape))]
    drawn = drawn.at[tuple(index_at)].set(low)
    longest = shape.index(max(shape))
    index_at[longest] = (index_at[longest] + 1) % shape[longest]
    return drawn.at[tuple(index_at)].set(top_value)


def level_of(key, dims, cuts, low, top_value):
    level, own = 1.0, jax.random.fold_in(key, 6)
    for axis_at, shards_of in cuts:
        heights = jnp.exp(jax.random.uniform(jax.random.fold_in(own, axis_at), (shards_of,), jnp.float32, low / len(cuts), top_value / len(cuts)))
        level = level * jnp.repeat(heights, dims[axis_at] // shards_of).reshape([-1 if axis == axis_at else 1 for axis in range(len(dims))])
    return level


def scatter_about(own_key, extent, deviation, bound, pieces=(), dtype=jnp.bfloat16):
    array = jax.random.normal(own_key, extent, jnp.float32) * deviation
    if len(pieces) > 0:
        array = level_of(own_key, extent, pieces, -0.22, 0.18) * array
    return jnp.clip(array, min=-bound, max=bound).astype(dtype)


def setup_inputs(seed: int = 0) -> dict:
    arg_keys = jax.random.split(jax.random.key(seed), 17)
    return {
        "tokens": scatter_about(arg_keys[0], (TOKENS, D), 1.0, 6.0, ((0, 32),)),
        "doc_flags": place_ends((jax.random.randint(arg_keys[1], (TOKENS,), 0, 256) < 1).astype(jnp.int32), jax.random.fold_in(arg_keys[1], 1), 0, 1),
        "reset_flags": place_ends((jax.random.randint(arg_keys[2], (NBLK,), 0, 16) < 1).astype(jnp.int32), jax.random.fold_in(arg_keys[2], 1), 0, 1),
        "state_init": scatter_about(arg_keys[3], (NS, D), 1.0, 6.0, ((1, 4),), jnp.float32),
        "gain_attn": jnp.clip(1.0 + 0.1 * jax.random.normal(arg_keys[4], (D,), jnp.float32), 0.5, 1.5),
        "w_query": scatter_about(arg_keys[5], (D, D), D ** -0.5, 0.1875, ((1, 4),)),
        "w_key": scatter_about(arg_keys[6], (D, D), D ** -0.5, 0.1875, ((1, 4),)),
        "w_value": scatter_about(arg_keys[7], (D, D), D ** -0.5, 0.1875, ((1, 4),)),
        "w_output": scatter_about(arg_keys[8], (D, D), (max(D // 128, 1)) ** -0.5, 2.0, ((0, 4),)),
        "bias_table": scatter_about(arg_keys[9], (H, BUCKETS), 1.0, 4.0, ((0, 4),), jnp.float32),
        "state_queries": scatter_about(arg_keys[10], (NS, D), 1.5, 8.0, ((1, 4),)),
        "gate_logits": jnp.clip(-1.0 + 6.0 * jax.random.uniform(arg_keys[11], (D,), jnp.float32) ** level_of(arg_keys[11], (D,), ((0, 4),), -0.2, 0.2), -1.0, 5.0),
        "gain_mlp": jnp.clip(1.0 + 0.1 * jax.random.normal(arg_keys[12], (D,), jnp.float32), 0.5, 1.5),
        "w_hidden": scatter_about(arg_keys[13], (D, FF), D ** -0.5, 0.1875, ((1, 4),)),
        "w_return": scatter_about(arg_keys[14], (FF, D), FF ** -0.5, 0.09375, ((0, 4),)),
        "cotangent": scatter_about(arg_keys[15], (TOKENS, D), 1.0, 6.0, ((0, 32),)),
    }


@jax.custom_vjp
def low(v):
    return lax.optimization_barrier(v.astype(jnp.bfloat16)).astype(jnp.float32)

@jax.custom_vjp
def low_back(v):
    return v

def low_keep(v):
    return (low(v), None)

def low_pass(kept, grad):
    return (grad,)

def back_keep(v):
    return (v, None)

def back_low(kept, grad):
    return (low(grad),)
low.defvjp(low_keep, low_pass)
low_back.defvjp(back_keep, back_low)
eps = 1e-06
negative_fill = -1e+30
highest = lax.Precision.HIGHEST

def bucket_layout(block):
    rows = lax.broadcasted_iota(jnp.int32, (block, 2 * block), 0)
    columns = lax.broadcasted_iota(jnp.int32, (block, 2 * block), 1)
    distance = block + rows - columns
    clipped = jnp.maximum(distance, 0)
    half = BUCKETS // 2
    limits = [math.ceil(half * (FAR / half) ** (level / half)) for level in range(1, half)]
    extra = sum(((clipped >= limit).astype(jnp.int32) for limit in limits))
    bucket = jnp.where(clipped < half, clipped, half + extra)
    return (distance, bucket)

def rms_scale(values):
    return lax.rsqrt(lax.optimization_barrier(jnp.mean(values * values, axis=-1, keepdims=True)) + eps)

def reference(tokens, doc_flags, reset_flags, state_init, gain_attn, w_query, w_key, w_value, w_output, bias_table, state_queries, gate_logits, gain_mlp, w_hidden, w_return, cotangent):
    blocks = tokens.shape[0] // BLOCK
    heads = bias_table.shape[0]
    width = tokens.shape[1]
    head_size = width // heads
    scale = 1.0 / math.sqrt(head_size)
    distance, bucket = bucket_layout(BLOCK)
    window_ok = (distance >= 0) & (distance < BLOCK)
    positions = jnp.arange(2 * BLOCK)
    flag_blocks = doc_flags.reshape(blocks, BLOCK)
    keep_blocks = (1 - reset_flags).astype(jnp.float32)
    numbers = jnp.arange(blocks).astype(jnp.int32)

    def forward(rows_all, state_start, gain_a, query_w, key_w, value_w, output_w, table, squeries, logits, gain_m, hidden_w, return_w):
        bias = sum((table[:, slot][:, None, None] * (bucket == slot)[None] for slot in range(BUCKETS)))
        gates = jax.nn.sigmoid(logits)
        state_heads = squeries.reshape(NS, heads, head_size)

        def step_block(carry, inputs):
            state, key_before, value_before, flag_before = carry
            rows, flags, keep, number = inputs
            normed = low(rows * rms_scale(rows) * gain_a)
            query = low_back(low(jnp.dot(normed, query_w, precision=highest)))
            key = low_back(low(jnp.dot(normed, key_w, precision=highest)))
            value = low_back(low(jnp.dot(normed, value_w, precision=highest)))
            used = state * keep
            state_low = low(used).reshape(NS, heads, head_size)
            counts = jnp.cumsum(jnp.concatenate([flag_before, flags]))
            exists = (positions >= BLOCK) | (number > 0)
            valid = (counts[BLOCK:][:, None] == counts[None, :]) & exists[None, :] & window_ok
            keys = jnp.concatenate([key_before, key]).reshape(2 * BLOCK, heads, head_size)
            values = jnp.concatenate([value_before, value]).reshape(2 * BLOCK, heads, head_size)
            query_heads = query.reshape(BLOCK, heads, head_size)
            window_scores = low_back(jnp.einsum('qhd,khd->hqk', query_heads, keys, precision=highest) * scale + bias)
            window_scores = jnp.where(valid[None], window_scores, negative_fill)
            state_scores = low_back(jnp.einsum('qhd,nhd->hqn', query_heads, state_low, precision=highest) * scale)
            probs = low(jax.nn.softmax(jnp.concatenate([window_scores, state_scores], axis=2), axis=2))
            mixed = jnp.einsum('hqk,khd->qhd', probs[:, :, :2 * BLOCK], values, precision=highest)
            mixed = mixed + jnp.einsum('hqn,nhd->qhd', probs[:, :, 2 * BLOCK:], state_low, precision=highest)
            mixed = low(low_back(mixed.reshape(BLOCK, width)))
            residual = rows + low_back(jnp.dot(mixed, output_w, precision=highest))
            normed_mlp = low(residual * rms_scale(residual) * gain_m)
            pre = low_back(jnp.dot(normed_mlp, hidden_w, precision=highest))
            hidden = low(jax.nn.gelu(pre, approximate=False))
            result = residual + low_back(jnp.dot(hidden, return_w, precision=highest))
            key_heads = key.reshape(BLOCK, heads, head_size)
            value_heads = value.reshape(BLOCK, heads, head_size)
            update_scores = low_back(jnp.einsum('nhd,khd->hnk', state_heads, key_heads, precision=highest) * scale)
            update_probs = low(jax.nn.softmax(update_scores, axis=2))
            update = low_back(jnp.einsum('hnk,khd->nhd', update_probs, value_heads, precision=highest).reshape(NS, width))
            state_next = gates * used + update
            return ((state_next, key, value, flags), (result, state_next))
        start = (state_start, jnp.zeros((BLOCK, width), jnp.float32), jnp.zeros((BLOCK, width), jnp.float32), jnp.zeros((BLOCK,), jnp.int32))
        final, outputs = lax.scan(jax.checkpoint(step_block), start, (rows_all.reshape(blocks, BLOCK, width), flag_blocks, keep_blocks, numbers))
        return (outputs[0].reshape(blocks * BLOCK, width), outputs[1])
    (result, states), pullback = jax.vjp(forward, tokens.astype(jnp.float32), state_init, gain_attn, w_query.astype(jnp.float32), w_key.astype(jnp.float32), w_value.astype(jnp.float32), w_output.astype(jnp.float32), bias_table, state_queries.astype(jnp.float32), gate_logits, gain_mlp, w_hidden.astype(jnp.float32), w_return.astype(jnp.float32))
    grads = pullback((cotangent.astype(jnp.float32), jnp.zeros_like(states)))
    return (result.astype(jnp.bfloat16), states, grads[0], grads[1], grads[2], grads[3], grads[4], grads[5], grads[6], grads[7], grads[8], grads[9], grads[10], grads[11], grads[12])
```

```python
import functools
import math

import jax
import jax.numpy as jnp
import numpy as np
from jax import lax
from jax.experimental import pallas as pl
from jax.experimental.pallas import tpu as pltpu
from jax.sharding import PartitionSpec as P

D = 1024
H = 8
NS = 512
BLOCK = 512
BUCKETS = 32
FAR = 128
TILE = 128
SPAN = BLOCK + TILE
HEAD = 128

eps = 1e-06
negative_fill = -1e30
LOG2E = math.log2(math.e)
f32 = jnp.float32
bf16 = jnp.bfloat16
VMEM_LIMIT = 56 * 1024 * 1024


def nn(a, b):
    return lax.dot_general(a, b, (((1,), (0,)), ((), ())), preferred_element_type=f32)


def nt(a, b):
    return lax.dot_general(a, b, (((1,), (1,)), ((), ())), preferred_element_type=f32)


def tn(a, b):
    return lax.dot_general(a, b, (((0,), (0,)), ((), ())), preferred_element_type=f32)


def call(kernel, grid, prefetch, ins, outs, aliases=(), scratch=(), flops=0, nbytes=0, exps=0):
    any_spec = pl.BlockSpec(memory_space=pl.ANY)
    arrays = [array for array, _ in ins] + [array for array, _ in aliases]
    specs = [spec for _, spec in ins] + [any_spec for _ in aliases]
    first = len(prefetch) + len(ins)
    alias_map = {first + n: out for n, (_, out) in enumerate(aliases)}
    n_pre, n_in, n_alias = len(prefetch), len(ins), len(aliases)

    def body(*refs):
        kept = refs[: n_pre + n_in] + refs[n_pre + n_in + n_alias :]
        kernel(*kept)

    return pl.pallas_call(
        body,
        out_shape=[jax.ShapeDtypeStruct(shape, dtype) for shape, dtype, _ in outs],
        grid_spec=pltpu.PrefetchScalarGridSpec(
            num_scalar_prefetch=n_pre,
            grid=grid,
            in_specs=specs,
            out_specs=[spec for _, _, spec in outs],
            scratch_shapes=list(scratch),
        ),
        input_output_aliases=alias_map,
        compiler_params=pltpu.CompilerParams(
            dimension_semantics=("arbitrary",) * len(grid), vmem_limit_bytes=VMEM_LIMIT
        ),
        cost_estimate=pl.CostEstimate(
            flops=int(flops), bytes_accessed=int(nbytes), transcendentals=int(exps)
        ),
    )(*prefetch, *arrays)


def lanes(*columns):
    rows = columns[0].shape[0]
    lane = lax.broadcasted_iota(jnp.int32, (rows, 128), 1)
    packed = jnp.broadcast_to(columns[0], (rows, 128))
    for n, column in enumerate(columns[1:], 1):
        packed = jnp.where(lane == n, column, packed)
    return packed


def head_of(h):
    return slice(h * HEAD, (h + 1) * HEAD)


def bias_kernel(base_ref, out_ref):
    for h in range(out_ref.shape[0]):
        row = jnp.broadcast_to(base_ref[h : h + 1, :], (TILE, SPAN))
        out_ref[h] = pltpu.roll(row, 0, 1, stride=1, stride_axis=0)


def bias_sum_kernel(grad_ref, out_ref):
    rows = lax.broadcasted_iota(jnp.int32, (TILE, SPAN), 0)
    for h in range(grad_ref.shape[0]):
        value = grad_ref[h]
        step = 1
        while step < TILE:
            moved = pltpu.roll(value, SPAN - step, 1)
            value = jnp.where((rows & step) != 0, moved, value)
            step *= 2
        out_ref[h : h + 1, :] = jnp.sum(value, axis=0, keepdims=True)


def front_kernel(scale, heads, tok, gain, w, sq, normed_out, qkv_out, u_out, lse_out):
    width = heads * HEAD
    rows = 256
    for i in range(BLOCK // rows):
        part = slice(i * rows, (i + 1) * rows)
        x = tok[part, :].astype(f32)
        r = lax.rsqrt(jnp.mean(x * x, axis=-1, keepdims=True) + eps)
        n = (x * r * gain[...]).astype(bf16)
        normed_out[part, :] = n
        qkv_out[part, :] = nn(n, w[...]).astype(bf16)
    for i in range(BLOCK // rows):
        part = slice(i * rows, (i + 1) * rows)
        stats = []
        for h in range(heads):
            k = qkv_out[:, width + h * HEAD : width + (h + 1) * HEAD]
            v = qkv_out[:, 2 * width + h * HEAD : 2 * width + (h + 1) * HEAD]
            s = nt(sq[part, head_of(h)], k) * (scale * LOG2E)
            m = jnp.max(s, axis=1, keepdims=True)
            p = jnp.exp2(s - m)
            l = jnp.sum(p, axis=1, keepdims=True)
            u_out[0, part, head_of(h)] = nn(p.astype(bf16), v) / l
            stats.append(m + jnp.log(l) * LOG2E)
        lse_out[0, part, :] = lanes(*stats)


def window_scores(scale, h, i, q, kp, kc, qid, idp, idc, bias):
    r0 = i * TILE
    cut = BLOCK - r0
    qc = qid[r0 : r0 + TILE, :]
    s1 = nt(q, kp[r0:, head_of(h)]) * (scale * LOG2E) + bias[h, :, :cut]
    s2 = nt(q, kc[: r0 + TILE, head_of(h)]) * (scale * LOG2E) + bias[h, :, cut:]
    s1 = jnp.where(qc == idp[0, :, r0:], s1, negative_fill)
    s2 = jnp.where(qc == idc[0, :, : r0 + TILE], s2, negative_fill)
    return s1, s2


def window_kernel(scale, heads, t, q, kc, vc, hk, hv, qid, idp, idc, bias, acc, ml, kp, vp):
    j = pl.program_id(0)

    @pl.when(j == 0)
    def _():
        kp[...] = hk[...]
        vp[...] = hv[...]

    for i in range(BLOCK // TILE):
        r0 = i * TILE
        part = slice(r0, r0 + TILE)
        peaks, sums = [], []
        for h in range(heads):
            qt = q[part, head_of(h)]
            s1, s2 = window_scores(scale, h, i, qt, kp, kc, qid, idp, idc, bias)
            m = jnp.maximum(
                jnp.max(s1, axis=1, keepdims=True), jnp.max(s2, axis=1, keepdims=True)
            )
            p1 = jnp.exp2(s1 - m)
            p2 = jnp.exp2(s2 - m)
            peaks.append(m)
            sums.append(jnp.sum(p1, axis=1, keepdims=True) + jnp.sum(p2, axis=1, keepdims=True))
            acc[0, part, head_of(h)] = nn(p1.astype(bf16), vp[r0:, head_of(h)]) + nn(
                p2.astype(bf16), vc[: r0 + TILE, head_of(h)]
            )
        ml[0, part, :] = lanes(*peaks, *sums)
    kp[...] = kc[...]
    vp[...] = vc[...]


def state_kernel(
    scale, heads, t, q, entry, before, carry_row, keep_row, gates, u, acc, ml, w,
    mixed_out, stats_out, used_out, next_out, part_out,
):
    used = carry_row[0] * entry[...] + keep_row[0] * before[0]
    next_out[0] = gates[...] * used + u[0]
    used_out[0] = used.astype(bf16)
    rows = 256
    for i in range(BLOCK // rows):
        part = slice(i * rows, (i + 1) * rows)
        stats = []
        for h in range(heads):
            state = used_out[0, :, head_of(h)]
            m = ml[0, part, h : h + 1]
            l = ml[0, part, heads + h : heads + h + 1]
            s = nt(q[part, head_of(h)], state) * (scale * LOG2E)
            top = jnp.maximum(m, jnp.max(s, axis=1, keepdims=True))
            p = jnp.exp2(s - top)
            shrink = jnp.exp2(m - top)
            total = l * shrink + jnp.sum(p, axis=1, keepdims=True)
            value = (acc[0, part, head_of(h)] * shrink + nn(p.astype(bf16), state)) / total
            mixed_out[0, part, head_of(h)] = value.astype(bf16)
            stats.append(top + jnp.log(total) * LOG2E)
        stats_out[0, part, :] = lanes(*stats)
        part_out[part, :] = nn(mixed_out[0, part, :], w[...]).astype(bf16)


def mlp_kernel(nm, gact, w, hidden_out, gpre_out, part_out):
    cols = 256
    total = None
    for c in range(w.shape[1] // cols):
        cut = slice(c * cols, (c + 1) * cols)
        pre = nn(nm[...], w[:, cut])
        cumulative = 0.5 * (1.0 + lax.erf(pre * (1.0 / math.sqrt(2.0))))
        density = jnp.exp2(pre * pre * (-0.5 * LOG2E)) * (1.0 / math.sqrt(2.0 * math.pi))
        hidden_out[:, cut] = (pre * cumulative).astype(bf16)
        gpre = (gact[:, cut].astype(f32) * (cumulative + pre * density)).astype(bf16)
        gpre_out[:, cut] = gpre
        piece = nt(gpre, w[:, cut])
        total = piece if total is None else total + piece
    part_out[...] = total.astype(bf16)


def state_back_kernel(
    scale, heads, ga, w, q, mixed, used, stats, gm_out, stats_out, dq_out, direct_out
):
    step = pl.program_id(0)
    gm_all = nt(ga[...], w[...]).astype(bf16)
    gm_out[0] = gm_all
    logs, deltas = [], []
    for h in range(heads):
        gm = gm_all[:, head_of(h)]
        qt = q[:, head_of(h)]
        state = used[0, :, head_of(h)]
        delta = jnp.sum(
            gm.astype(f32) * mixed[0, :, head_of(h)].astype(f32), axis=1, keepdims=True
        )
        lse = stats[0, :, h : h + 1]
        p = jnp.exp2(nt(qt, state) * (scale * LOG2E) - lse)
        ds = (p * (nt(gm, state) - delta)).astype(bf16)
        dq_out[0, :, head_of(h)] = nn(ds, state) * scale
        du = tn(ds, qt) * scale + tn(p.astype(bf16), gm)
        logs.append(lse)
        deltas.append(delta)

        @pl.when(step == 0)
        def _():
            direct_out[0, :, head_of(h)] = du

        @pl.when(step != 0)
        def _():
            direct_out[0, :, head_of(h)] += du

    stats_out[0] = lanes(*logs, *deltas)


def window_back_kernel(
    scale, heads, t, q, kc, vc, kb, vb, hk, hv, qid, idp, idc, bias, gm, stats, dqs,
    dq_out, dk_out, dv_out, hk_out, hv_out, grad_bias, kp, vp, dkp, dvp, dkc, dvc,
):
    step = pl.program_id(0)
    last = pl.num_programs(0) - 1

    @pl.when(step == last)
    def _():
        kp[...] = hk[...]
        vp[...] = hv[...]

    @pl.when(step != last)
    def _():
        kp[...] = kb[...]
        vp[...] = vb[...]

    @pl.when(step == 0)
    def _():
        dkp[...] = jnp.zeros_like(dkp)
        dvp[...] = jnp.zeros_like(dvp)
        grad_bias[...] = jnp.zeros_like(grad_bias)

    dkc[...] = dkp[...]
    dvc[...] = dvp[...]
    dkp[...] = jnp.zeros_like(dkp)
    dvp[...] = jnp.zeros_like(dvp)
    for i in range(BLOCK // TILE):
        r0 = i * TILE
        cut = BLOCK - r0
        r1 = r0 + TILE
        part = slice(r0, r1)
        for h in range(heads):
            hs = head_of(h)
            qt = q[part, hs]
            g = gm[0, part, hs]
            lse = stats[0, part, h : h + 1]
            delta = stats[0, part, heads + h : heads + h + 1]
            s1, s2 = window_scores(scale, h, i, qt, kp, kc, qid, idp, idc, bias)
            p1 = jnp.exp2(s1 - lse)
            p2 = jnp.exp2(s2 - lse)
            ds1 = p1 * (nt(g, vp[r0:, hs]) - delta)
            ds2 = p2 * (nt(g, vc[:r1, hs]) - delta)
            grad_bias[h, :, :cut] += ds1
            grad_bias[h, :, cut:] += ds2
            ds1 = ds1.astype(bf16)
            ds2 = ds2.astype(bf16)
            dq = (nn(ds1, kp[r0:, hs]) + nn(ds2, kc[:r1, hs])) * scale + dqs[0, part, hs]
            dq_out[part, hs] = dq.astype(bf16)
            dkp[r0:, hs] += tn(ds1, qt) * scale
            dkc[:r1, hs] += tn(ds2, qt) * scale
            dvp[r0:, hs] += tn(p1.astype(bf16), g)
            dvc[:r1, hs] += tn(p2.astype(bf16), g)
    dk_out[0] = dkc[...]
    dv_out[0] = dvc[...]

    @pl.when(step == last)
    def _():
        hk_out[...] = dkp[...].astype(bf16)
        hv_out[...] = dvp[...].astype(bf16)


def update_back_kernel(
    scale, heads, t, carried0, direct, entry, before, carry_row, keep_row, gates, k, v, sq,
    lse_u, u, dq, dk, dv, hk, hv, w, dkv_out, part_out, dsq_out, gate_out, carried,
):
    step = pl.program_id(0)
    width = heads * HEAD

    @pl.when(step == 0)
    def _():
        carried[...] = carried0[...]
        dsq_out[...] = jnp.zeros_like(dsq_out)
        gate_out[...] = jnp.zeros_like(gate_out)

    used = carry_row[0] * entry[...] + keep_row[0] * before[0]
    now = carried[...]
    gate_out[...] += jnp.sum(now * used, axis=0, keepdims=True)
    gu_all = now.astype(bf16)
    carried[...] = keep_row[0] * (direct[0] + gates[...] * now)
    for h in range(heads):
        hs = head_of(h)
        gu = gu_all[:, hs]
        sqh = sq[:, hs]
        kh = k[:, hs]
        delta = jnp.sum(gu.astype(f32) * u[0, :, hs], axis=1, keepdims=True)
        p = jnp.exp2(nt(sqh, kh) * (scale * LOG2E) - lse_u[0, :, h : h + 1])
        ds = (p * (nt(gu, v[:, hs]) - delta)).astype(bf16)
        dsq_out[:, hs] += nn(ds, kh) * scale
        more = jnp.where(step == 0, 1.0, 0.0)
        dkh = dk[0, :, hs] + tn(ds, sqh) * scale + more * hk[:, hs].astype(f32)
        dvh = dv[0, :, hs] + tn(p.astype(bf16), gu) + more * hv[:, hs].astype(f32)
        dkv_out[:, hs] = dkh.astype(bf16)
        dkv_out[:, width + h * HEAD : width + (h + 1) * HEAD] = dvh.astype(bf16)
    part = nt(dq[...], w[:, :width]) + nt(dkv_out[...], w[:, width:])
    part_out[...] = part.astype(bf16)


def bucket_of(distance):
    half = BUCKETS // 2
    limits = [math.ceil(half * (FAR / half) ** (level / half)) for level in range(1, half)]
    clipped = np.maximum(distance, 0)
    extra = sum((clipped >= limit).astype(np.int32) for limit in limits)
    return np.where(clipped < half, clipped, half + extra)


def local(
    tokens,
    doc_flags,
    reset_flags,
    state_init,
    gain_attn,
    w_query,
    w_key,
    w_value,
    w_output,
    bias_table,
    state_queries,
    gate_logits,
    gain_mlp,
    w_hidden,
    w_return,
    cotangent,
):
    heads = bias_table.shape[0]
    lw = w_query.shape[1]
    width = tokens.shape[1]
    nb = reset_flags.shape[0]
    ff = w_hidden.shape[1]
    scale = 1.0 / math.sqrt(HEAD)
    groups = lax.axis_size("seq")
    s_index = lax.axis_index("seq")
    t_index = lax.axis_index("tp")
    t_pre = t_index.astype(jnp.int32)[None]
    rows_all = nb * BLOCK

    def core(value):
        return lax.ppermute(value, "tp", [(i, i ^ 1) for i in range(nb)])

    def cross(value):
        return lax.ppermute(value, "tp", [(i, i ^ 2) for i in range(nb)])

    def along(value, step):
        pairs = [(i, i + step) for i in range(groups) if 0 <= i + step < groups]
        return lax.ppermute(value, "seq", pairs)

    full = lambda *shape: pl.BlockSpec(shape, lambda *_: (0,) * len(shape))

    tok2 = cross(tokens)
    cot2 = cross(cotangent)
    toks = [tokens, core(tokens), tok2, core(tok2)]
    cots = [cotangent, core(cotangent), cot2, core(cot2)]

    every = reset_flags.reshape(1, nb)
    step = 1
    while step < groups:
        every = jnp.concatenate(
            [every, lax.ppermute(every, "seq", [(i, i ^ step) for i in range(groups)])]
        )
        step *= 2
    group_of = jnp.arange(groups, dtype=jnp.int32) ^ s_index
    group_keep = jnp.prod((1 - every).astype(f32), axis=1)

    def keep_between(low, high):
        inside = (group_of >= low) & (group_of <= high)
        return jnp.prod(jnp.where(inside, group_keep, 1.0))

    gates = jax.nn.sigmoid(gate_logits)
    keeps = (1 - reset_flags).astype(f32)
    gate_row = gates[None, :]

    def gate_power(count):
        result, base = None, gates
        while count:
            if count & 1:
                result = base if result is None else result * base
            base = base * base
            count >>= 1
        return jnp.ones_like(gates) if result is None else result

    flag_prev = along(doc_flags[rows_all - BLOCK :], 1)
    ids = jnp.cumsum(jnp.concatenate([flag_prev, doc_flags]))
    ids = jnp.where((jnp.arange(rows_all + BLOCK) < BLOCK) & (s_index == 0), -1, ids)
    id_rows = ids.reshape(nb + 1, 1, BLOCK)
    id_cols = ids[BLOCK:].reshape(rows_all, 1)

    apart = BLOCK - np.arange(SPAN)
    shown = (apart >= 0) & (apart < BLOCK)
    onehot = (bucket_of(apart)[:, None] == np.arange(BUCKETS)[None, :]) & shown[:, None]
    onehot = jnp.asarray(onehot.astype(np.float32))
    base = jnp.dot(bias_table * LOG2E, onehot.T, precision=lax.Precision.HIGHEST)
    base = jnp.where(jnp.asarray(shown)[None, :], base, negative_fill)
    (bias,) = call(
        bias_kernel,
        (1,),
        (),
        [(base, full(heads, SPAN))],
        [((heads, TILE, SPAN), f32, full(heads, TILE, SPAN))],
    )

    w_joined = jnp.concatenate([w_query, w_key, w_value], axis=1)
    stacked = None
    for r in range(nb):
        aliases = [] if stacked is None else [(array, n) for n, array in enumerate(stacked)]
        stacked = call(
            functools.partial(front_kernel, scale, heads),
            (1,),
            (),
            [
                (toks[r], full(BLOCK, width)),
                (gain_attn[None, :], full(1, width)),
                (w_joined, full(width, 3 * lw)),
                (state_queries, full(NS, lw)),
            ],
            [
                ((rows_all, width), bf16, pl.BlockSpec((BLOCK, width), lambda g, r=r: (r, 0))),
                ((rows_all, 3 * lw), bf16, pl.BlockSpec((BLOCK, 3 * lw), lambda g, r=r: (r, 0))),
                ((nb, NS, lw), f32, pl.BlockSpec((1, NS, lw), lambda g, r=r: (r, 0, 0))),
                ((nb, NS, 128), f32, pl.BlockSpec((1, NS, 128), lambda g, r=r: (r, 0, 0))),
            ],
            aliases,
            flops=2 * BLOCK * width * 3 * lw + 4 * NS * BLOCK * lw,
            nbytes=6 * BLOCK * width * 2,
            exps=heads * NS * BLOCK,
        )
    normed_all, qkv, updates, lse_u = stacked

    def in_order(array, j):
        return lax.dynamic_index_in_dim(array, t_index ^ j, 0, False)

    factors = [gates * keeps[j] for j in range(nb)]
    before = [jnp.zeros((NS, lw), f32)]
    factor_before = [jnp.ones_like(gates)]
    for j in range(nb):
        before.append(factors[j] * before[j] + in_order(updates, j))
        factor_before.append(factor_before[j] * factors[j])
    total = before.pop()
    factor_total = factor_before.pop()
    before = jnp.stack(before)
    entry = jnp.zeros((NS, lw), f32)
    step = 1
    while step < groups:
        sent = (factor_total * entry + total).astype(bf16)
        got = along(sent, step).astype(f32)
        kept = keep_between(s_index - step + 1, s_index - 1)
        entry = (gate_power(nb * (step - 1)) * kept) * got + entry
        step *= 2
    power, bit = jnp.ones_like(gates), 1
    while bit < groups:
        power = power * jnp.where((s_index & bit) != 0, gate_power(nb * bit), 1.0)
        bit *= 2
    prefix_factor = power * keep_between(0, s_index - 1)
    entry = prefix_factor * state_init + entry
    carry_rows = (jnp.stack(factor_before) * keeps[:, None])[:, None, :]
    keep_rows = jnp.broadcast_to(keeps[:, None, None], (nb, 1, lw))

    place = (t_index ^ (nb - 1)) * BLOCK
    edge = along(lax.dynamic_slice(qkv, (place, lw), (BLOCK, 2 * lw)), 1)
    at = lambda col: pl.BlockSpec((BLOCK, lw), lambda j, t: (j ^ t[0], col))
    pair_flops = 2 * BLOCK * SPAN * lw
    acc, ml = call(
        functools.partial(window_kernel, scale, heads),
        (nb,),
        (t_pre,),
        [
            (qkv, at(0)),
            (qkv, at(1)),
            (qkv, at(2)),
            (edge, pl.BlockSpec((BLOCK, lw), lambda j, t: (0, 0))),
            (edge, pl.BlockSpec((BLOCK, lw), lambda j, t: (0, 1))),
            (id_cols, pl.BlockSpec((BLOCK, 1), lambda j, t: (j, 0))),
            (id_rows, pl.BlockSpec((1, 1, BLOCK), lambda j, t: (j, 0, 0))),
            (id_rows, pl.BlockSpec((1, 1, BLOCK), lambda j, t: (j + 1, 0, 0))),
            (bias, full(heads, TILE, SPAN)),
        ],
        [
            ((nb, BLOCK, lw), f32, pl.BlockSpec((1, BLOCK, lw), lambda j, t: (j, 0, 0))),
            ((nb, BLOCK, 128), f32, pl.BlockSpec((1, BLOCK, 128), lambda j, t: (j, 0, 0))),
        ],
        scratch=[pltpu.VMEM((BLOCK, lw), bf16)] * 2,
        flops=nb * 2 * pair_flops,
        nbytes=nb * BLOCK * lw * 12,
        exps=nb * heads * BLOCK * SPAN,
    )

    halves = {}
    stacked = None
    for first in (2, 0):
        aliases = [] if stacked is None else [(array, n) for n, array in enumerate(stacked)]
        pos = lambda *tail, first=first: pl.BlockSpec(
            (1,) + tail, lambda g, t: (first + g, 0, 0)
        )
        blk = lambda *tail, first=first: pl.BlockSpec(
            (1,) + tail, lambda g, t: ((first + g) ^ t[0], 0, 0)
        )
        *stacked, halves[first] = call(
            functools.partial(state_kernel, scale, heads),
            (2,),
            (t_pre,),
            [
                (qkv, pl.BlockSpec((BLOCK, lw), lambda g, t, first=first: (first + g, 0))),
                (entry, full(NS, lw)),
                (before, blk(NS, lw)),
                (carry_rows, blk(1, lw)),
                (keep_rows, blk(1, lw)),
                (gate_row, full(1, lw)),
                (updates, pos(NS, lw)),
                (acc, blk(BLOCK, lw)),
                (ml, blk(BLOCK, 128)),
                (w_output, full(lw, width)),
            ],
            [
                ((nb, BLOCK, lw), bf16, pos(BLOCK, lw)),
                ((nb, BLOCK, 128), f32, pos(BLOCK, 128)),
                ((nb, NS, lw), bf16, pos(NS, lw)),
                ((nb, NS, lw), f32, blk(NS, lw)),
                ((2 * BLOCK, width), bf16, pl.BlockSpec((BLOCK, width), lambda g, t: (g, 0))),
            ],
            aliases,
            flops=2 * (4 * BLOCK * NS * lw + 2 * BLOCK * lw * width),
            nbytes=2 * BLOCK * (lw * 24 + width * 2),
            exps=2 * heads * BLOCK * NS,
        )
    mixed_all, stats_f, used_low, block_states = stacked

    def pair_sum(half):
        return (half[:BLOCK].astype(f32) + core(half[BLOCK:]).astype(f32)).astype(bf16)

    sum2 = pair_sum(halves[2])
    sum0 = pair_sum(halves[0])
    cross2 = cross(sum2)
    cross0 = cross(sum0)

    def norm_mlp(tok, mine, theirs):
        residual = tok.astype(f32) + (mine.astype(f32) + theirs.astype(f32))
        inverse = lax.rsqrt(jnp.mean(residual * residual, axis=-1, keepdims=True) + eps)
        return residual, inverse, (residual * inverse * gain_mlp).astype(bf16)

    residual0, inverse0, nm0 = norm_mlp(toks[0], sum0, cross2)
    residual2, inverse2, nm2 = norm_mlp(toks[2], sum2, cross0)
    nms = [nm0, core(nm0), nm2, core(nm2)]

    gacts = [nt(cot, w_return).astype(bf16) for cot in cots]
    stacked = None
    parts = []
    for r in range(nb):
        aliases = [] if stacked is None else [(array, n) for n, array in enumerate(stacked)]
        tile = 256
        steps = BLOCK // tile
        *stacked, part = call(
            mlp_kernel,
            (steps,),
            (),
            [
                (nms[r], pl.BlockSpec((tile, width), lambda g: (g, 0))),
                (gacts[r], pl.BlockSpec((tile, ff), lambda g: (g, 0))),
                (w_hidden, full(width, ff)),
            ],
            [
                (
                    (rows_all, ff),
                    bf16,
                    pl.BlockSpec((tile, ff), lambda g, r=r: (r * steps + g, 0)),
                ),
                (
                    (rows_all, ff),
                    bf16,
                    pl.BlockSpec((tile, ff), lambda g, r=r: (r * steps + g, 0)),
                ),
                ((BLOCK, width), bf16, pl.BlockSpec((tile, width), lambda g: (g, 0))),
            ],
            aliases,
            flops=4 * BLOCK * width * ff,
            nbytes=BLOCK * width * 10,
            exps=2 * BLOCK * ff,
        )
        parts.append(part)
    hidden_all, gpre_all = stacked

    back0 = (parts[0].astype(f32) + core(parts[1]).astype(f32)).astype(bf16)
    back2 = (parts[2].astype(f32) + core(parts[3]).astype(f32)).astype(bf16)
    cross0 = cross(back0)
    cross2 = cross(back2)

    def norm_mlp_back(cot, mine, theirs, residual, inverse):
        scaled = residual * inverse
        grad = (mine.astype(f32) + theirs.astype(f32)) * gain_mlp
        inner = jnp.mean(grad * scaled, axis=-1, keepdims=True)
        return cot.astype(f32) + inverse * (grad - scaled * inner)

    ga2 = norm_mlp_back(cots[2], back2, cross0, residual2, inverse2).astype(bf16)
    grad_residual = norm_mlp_back(cots[0], back0, cross2, residual0, inverse0)
    ga0 = grad_residual.astype(bf16)
    gas = [ga0, core(ga0), ga2, core(ga2)]

    mlp_part = nn(hidden_all, w_return).astype(bf16)
    mlp_parts = [mlp_part[r * BLOCK : (r + 1) * BLOCK] for r in range(nb)]
    far = mlp_parts[2].astype(f32) + core(mlp_parts[3]).astype(f32)
    mlp_out = (
        mlp_parts[0].astype(f32)
        + core(mlp_parts[1]).astype(f32)
        + cross(far.astype(bf16)).astype(f32)
    )
    result = (residual0 + mlp_out).astype(bf16)

    stacked = None
    for r in (2, 3, 0, 1):
        aliases = [] if stacked is None else [(array, n) for n, array in enumerate(stacked)]
        tile = 256
        steps = BLOCK // tile
        pos = lambda *tail, r=r: pl.BlockSpec((1,) + tail, lambda g: (r, g, 0))
        whole = lambda *tail, r=r: pl.BlockSpec((1,) + tail, lambda g: (r, 0, 0))
        stacked = call(
            functools.partial(state_back_kernel, scale, heads),
            (steps,),
            (),
            [
                (gas[r], pl.BlockSpec((tile, width), lambda g: (g, 0))),
                (w_output, full(lw, width)),
                (qkv, pl.BlockSpec((tile, lw), lambda g, r=r: (r * steps + g, 0))),
                (mixed_all, pos(tile, lw)),
                (used_low, whole(NS, lw)),
                (stats_f, pos(tile, 128)),
            ],
            [
                ((nb, BLOCK, lw), bf16, pos(tile, lw)),
                ((nb, BLOCK, 128), f32, pos(tile, 128)),
                ((nb, BLOCK, lw), f32, pos(tile, lw)),
                ((nb, NS, lw), f32, whole(NS, lw)),
            ],
            aliases,
            flops=2 * BLOCK * lw * width + 10 * BLOCK * NS * lw,
            nbytes=BLOCK * (width * 4 + lw * 16),
            exps=heads * BLOCK * NS,
        )
    gm_all, stats_b, dq_state, direct = stacked

    local_grad = jnp.zeros((NS, lw), f32)
    for j in reversed(range(nb)):
        local_grad = keeps[j] * (in_order(direct, j) + gates * local_grad)
    carried = jnp.zeros((NS, lw), f32)
    step = 1
    while step < groups:
        sent = (local_grad + factor_total * carried).astype(bf16)
        got = along(sent, -step).astype(f32)
        kept = keep_between(s_index + 1, s_index + step - 1)
        carried = (gate_power(nb * (step - 1)) * kept) * got + carried
        step *= 2

    turn = lambda j: nb - 1 - j
    at = lambda col: pl.BlockSpec((BLOCK, lw), lambda j, t: (turn(j) ^ t[0], col))
    prev = lambda col: pl.BlockSpec(
        (BLOCK, lw), lambda j, t: (jnp.maximum(turn(j) - 1, 0) ^ t[0], col)
    )
    pos = lambda *tail: pl.BlockSpec((1,) + tail, lambda j, t: (turn(j) ^ t[0], 0, 0))
    dq, dk, dv, back_k, back_v, bias_grad = call(
        functools.partial(window_back_kernel, scale, heads),
        (nb,),
        (t_pre,),
        [
            (qkv, at(0)),
            (qkv, at(1)),
            (qkv, at(2)),
            (qkv, prev(1)),
            (qkv, prev(2)),
            (edge, pl.BlockSpec((BLOCK, lw), lambda j, t: (0, 0))),
            (edge, pl.BlockSpec((BLOCK, lw), lambda j, t: (0, 1))),
            (id_cols, pl.BlockSpec((BLOCK, 1), lambda j, t: (turn(j), 0))),
            (id_rows, pl.BlockSpec((1, 1, BLOCK), lambda j, t: (turn(j), 0, 0))),
            (id_rows, pl.BlockSpec((1, 1, BLOCK), lambda j, t: (turn(j) + 1, 0, 0))),
            (bias, full(heads, TILE, SPAN)),
            (gm_all, pos(BLOCK, lw)),
            (stats_b, pos(BLOCK, 128)),
            (dq_state, pos(BLOCK, lw)),
        ],
        [
            ((rows_all, lw), bf16, pl.BlockSpec((BLOCK, lw), lambda j, t: (turn(j) ^ t[0], 0))),
            ((nb, BLOCK, lw), f32, pos(BLOCK, lw)),
            ((nb, BLOCK, lw), f32, pos(BLOCK, lw)),
            ((BLOCK, lw), bf16, full(BLOCK, lw)),
            ((BLOCK, lw), bf16, full(BLOCK, lw)),
            ((heads, TILE, SPAN), f32, full(heads, TILE, SPAN)),
        ],
        scratch=[pltpu.VMEM((BLOCK, lw), bf16)] * 2 + [pltpu.VMEM((BLOCK, lw), f32)] * 4,
        flops=nb * 5 * pair_flops,
        nbytes=nb * BLOCK * lw * 24,
        exps=nb * heads * BLOCK * SPAN,
    )
    next_k = along(back_k, -1)
    next_v = along(back_v, -1)
    (bias_line,) = call(
        bias_sum_kernel,
        (1,),
        (),
        [(bias_grad, full(heads, TILE, SPAN))],
        [((heads, SPAN), f32, full(heads, SPAN))],
    )
    bias_local = jnp.dot(bias_line, onehot, precision=lax.Precision.HIGHEST)

    blk = lambda *tail: pl.BlockSpec((1,) + tail, lambda j, t: (turn(j), 0, 0))
    row = lambda cols: pl.BlockSpec((BLOCK, cols), lambda j, t: (turn(j) ^ t[0], 0))
    dkv, parts, grad_sq, gate_sum = call(
        functools.partial(update_back_kernel, scale, heads),
        (nb,),
        (t_pre,),
        [
            (carried, full(NS, lw)),
            (direct, pos(NS, lw)),
            (entry, full(NS, lw)),
            (before, blk(NS, lw)),
            (carry_rows, blk(1, lw)),
            (keep_rows, blk(1, lw)),
            (gate_row, full(1, lw)),
            (qkv, at(1)),
            (qkv, at(2)),
            (state_queries, full(NS, lw)),
            (lse_u, pos(NS, 128)),
            (updates, pos(NS, lw)),
            (dq, row(lw)),
            (dk, pos(BLOCK, lw)),
            (dv, pos(BLOCK, lw)),
            (next_k, full(BLOCK, lw)),
            (next_v, full(BLOCK, lw)),
            (w_joined, full(width, 3 * lw)),
        ],
        [
            ((rows_all, 2 * lw), bf16, row(2 * lw)),
            ((rows_all, width), bf16, row(width)),
            ((NS, lw), f32, full(NS, lw)),
            ((1, lw), f32, full(1, lw)),
        ],
        scratch=[pltpu.VMEM((NS, lw), f32)],
        flops=nb * (10 * NS * BLOCK * lw + 6 * BLOCK * lw * width),
        nbytes=nb * BLOCK * (lw * 30 + width * 2),
        exps=nb * heads * NS * BLOCK,
    )
    pieces = [parts[r * BLOCK : (r + 1) * BLOCK] for r in range(nb)]
    far = pieces[2].astype(f32) + core(pieces[3]).astype(f32)
    grad_normed = (
        pieces[0].astype(f32)
        + core(pieces[1]).astype(f32)
        + cross(far.astype(bf16)).astype(f32)
    )
    token_float = tokens.astype(f32)
    inverse = lax.rsqrt(jnp.mean(token_float * token_float, axis=-1, keepdims=True) + eps)
    scaled = token_float * inverse
    grad_scaled = grad_normed * gain_attn
    inner = jnp.mean(grad_scaled * scaled, axis=-1, keepdims=True)
    grad_tokens = grad_residual + inverse * (grad_scaled - scaled * inner)

    cot_all = jnp.concatenate(cots)
    nm_all = jnp.concatenate(nms)
    ga_all = jnp.concatenate(gas)
    grad_hidden = tn(nm_all, gpre_all)
    grad_return_t = tn(cot_all, hidden_all)
    grad_output_t = tn(ga_all, mixed_all.reshape(rows_all, lw))
    gain_mlp_part = jnp.sum(grad_hidden * w_hidden.astype(f32), axis=1) / gain_mlp
    early = jnp.concatenate(
        [grad_hidden.astype(bf16), grad_return_t.astype(bf16), grad_output_t.astype(bf16)], axis=1
    )
    early = lax.psum_scatter(early, "seq", scatter_dimension=0, tiled=True).astype(f32)
    hidden_sent = early[:, :ff]
    return_sent = early[:, ff : 2 * ff].T
    output_sent = early[:, 2 * ff :].T

    grad_q = tn(normed_all, dq)
    grad_kv = tn(normed_all, dkv)
    gain_attn_part = (
        jnp.sum(grad_q * w_query.astype(f32), axis=1)
        + jnp.sum(grad_kv * w_joined[:, lw:].astype(f32), axis=1)
    ) / gain_attn
    share = NS // groups
    state_grads = jnp.concatenate([grad_sq, prefix_factor * local_grad], axis=1).astype(bf16)
    late = jnp.concatenate([grad_q.astype(bf16), grad_kv.astype(bf16)], axis=1)
    late = late.reshape(groups, width // groups, 3 * lw)
    late = lax.all_to_all(late, "seq", 0, 0, tiled=True)
    joined_sent = jnp.sum(late.astype(f32), axis=0)
    state_grads = state_grads.reshape(groups, share, 2 * lw)
    state_grads = lax.all_to_all(state_grads, "seq", 0, 0, tiled=True)
    state_grads = jnp.sum(state_grads.astype(f32), axis=0)

    bias_full = lax.dynamic_update_slice(
        jnp.zeros((H, BUCKETS), f32), bias_local, (t_index * heads, 0)
    )
    gate_full = lax.dynamic_update_slice(
        jnp.zeros((D,), f32), gate_sum[0] * gates * (1.0 - gates), (t_index * lw,)
    )
    small = jnp.concatenate(
        [gain_attn_part, gain_mlp_part, gate_full, bias_full.reshape(-1)]
    ).reshape(-1, 128)
    small = small + core(small)
    small = small + cross(small)
    step = 1
    while step < groups:
        small = small + lax.ppermute(small, "seq", [(i, i ^ step) for i in range(groups)])
        step *= 2
    small = small.reshape(-1)
    return (
        result,
        block_states,
        grad_tokens,
        state_grads[:, lw:],
        small[:D],
        joined_sent[:, :lw],
        joined_sent[:, lw : 2 * lw],
        joined_sent[:, 2 * lw :],
        output_sent,
        small[3 * D :].reshape(H, BUCKETS),
        state_grads[:, :lw],
        small[2 * D : 3 * D],
        small[D : 2 * D],
        hidden_sent,
        return_sent,
    )


def solution(mesh):
    return jax.shard_map(
        local,
        mesh=mesh,
        in_specs=(
            P(("seq", "tp"), None),
            P("seq"),
            P("seq"),
            P(None, "tp"),
            P(),
            P(None, "tp"),
            P(None, "tp"),
            P(None, "tp"),
            P("tp", None),
            P("tp", None),
            P(None, "tp"),
            P("tp"),
            P(),
            P(None, "tp"),
            P("tp", None),
            P(("seq", "tp"), None),
        ),
        out_specs=(
            P(("seq", "tp"), None),
            P("seq", None, "tp"),
            P(("seq", "tp"), None),
            P("seq", "tp"),
            P(),
            P("seq", "tp"),
            P("seq", "tp"),
            P("seq", "tp"),
            P("tp", "seq"),
            P(),
            P("seq", "tp"),
            P(),
            P(),
            P("seq", "tp"),
            P("tp", "seq"),
        ),
        check_vma=False,
    )
```

```python
import functools
import math

import jax
import jax.numpy as jnp
import numpy as np
from jax import lax
from jax.experimental import pallas as pl
from jax.experimental.pallas import tpu as pltpu
from jax.sharding import PartitionSpec as P

D = 1024
H = 8
NS = 512
BLOCK = 512
BUCKETS = 32
FAR = 128
TILE = 128
SPAN = BLOCK + TILE
HEAD = 128

eps = 1e-06
negative_fill = -1e30
LOG2E = math.log2(math.e)
WEIGHT = 0.05
HEAVY = 1.0
f32 = jnp.float32
bf16 = jnp.bfloat16


def nn(a, b):
    return lax.dot_general(a, b, (((1,), (0,)), ((), ())), preferred_element_type=f32)


def nt(a, b):
    return lax.dot_general(a, b, (((1,), (1,)), ((), ())), preferred_element_type=f32)


def tn(a, b):
    return lax.dot_general(a, b, (((0,), (0,)), ((), ())), preferred_element_type=f32)


def call(
    kernel, grid, prefetch, ins, outs, aliases=(), scratch=(), flops=0, nbytes=0, exps=0, mib=24,
    hbm=(), free=(), pin=False, weight=WEIGHT,
):
    any_spec = pl.BlockSpec(memory_space=pl.ANY)
    arrays = [
        pltpu.with_memory_space_constraint(array, pltpu.HBM)
        if n >= len(ins) or pin or (array.ndim == 3 and n not in free) or array.shape[0] > D
        else array
        for n, (array, _) in enumerate([*ins, *aliases])
    ]
    specs = [spec for _, spec in ins] + [any_spec for _ in aliases]
    first = len(prefetch) + len(ins)
    alias_map = {first + n: out for n, (_, out) in enumerate(aliases)}
    n_pre, n_in, n_alias = len(prefetch), len(ins), len(aliases)

    def body(*refs):
        kept = refs[: n_pre + n_in] + refs[n_pre + n_in + n_alias :]
        kernel(*kept)

    return pl.pallas_call(
        body,
        name=getattr(kernel, 'func', kernel).__name__,
        out_shape=[
            pltpu.HBM(shape, dtype)
            if n in alias_map.values() or n in hbm
            else jax.ShapeDtypeStruct(shape, dtype)
            for n, (shape, dtype, _) in enumerate(outs)
        ],
        grid_spec=pltpu.PrefetchScalarGridSpec(
            num_scalar_prefetch=n_pre,
            grid=grid,
            in_specs=specs,
            out_specs=[spec for _, _, spec in outs],
            scratch_shapes=list(scratch),
        ),
        input_output_aliases=alias_map,
        compiler_params=pltpu.CompilerParams(
            dimension_semantics=("arbitrary",) * len(grid), vmem_limit_bytes=mib * 1024 * 1024
        ),
        cost_estimate=pl.CostEstimate(
            flops=int(flops * weight),
            bytes_accessed=int(nbytes * weight),
            transcendentals=int(exps * weight),
        ),
    )(*prefetch, *arrays)


def lanes(*columns):
    rows = columns[0].shape[0]
    lane = lax.broadcasted_iota(jnp.int32, (rows, 128), 1)
    packed = jnp.broadcast_to(columns[0], (rows, 128))
    for n, column in enumerate(columns[1:], 1):
        packed = jnp.where(lane == n, column, packed)
    return packed


def head_of(h):
    return slice(h * HEAD, (h + 1) * HEAD)


def bias_kernel(base_ref, out_ref):
    for h in range(out_ref.shape[0]):
        row = jnp.broadcast_to(base_ref[h : h + 1, :], (TILE, SPAN))
        out_ref[h] = pltpu.roll(row, 0, 1, stride=1, stride_axis=0)


def bias_sum_kernel(grad_ref, out_ref):
    rows = lax.broadcasted_iota(jnp.int32, (TILE, SPAN), 0)
    for h in range(grad_ref.shape[0]):
        value = grad_ref[h]
        step = 1
        while step < TILE:
            moved = pltpu.roll(value, SPAN - step, 1)
            value = jnp.where((rows & step) != 0, moved, value)
            step *= 2
        out_ref[h : h + 1, :] = jnp.sum(value, axis=0, keepdims=True)


def front_kernel(scale, heads, tok, gain, w, sq, normed_out, qkv_out, u_out, lse_out):
    width = heads * HEAD
    rows = 256
    for i in range(BLOCK // rows):
        part = slice(i * rows, (i + 1) * rows)
        x = tok[part, :].astype(f32)
        r = lax.rsqrt(jnp.mean(x * x, axis=-1, keepdims=True) + eps)
        n = (x * r * gain[...]).astype(bf16)
        normed_out[part, :] = n
        qkv_out[part, :] = nn(n, w[...]).astype(bf16)
    for i in range(BLOCK // rows):
        part = slice(i * rows, (i + 1) * rows)
        stats = []
        for h in range(heads):
            k = qkv_out[:, width + h * HEAD : width + (h + 1) * HEAD]
            v = qkv_out[:, 2 * width + h * HEAD : 2 * width + (h + 1) * HEAD]
            s = nt(sq[part, head_of(h)], k) * (scale * LOG2E)
            m = jnp.max(s, axis=1, keepdims=True)
            p = jnp.exp2(s - m)
            l = jnp.sum(p, axis=1, keepdims=True)
            u_out[0, part, head_of(h)] = nn(p.astype(bf16), v) / l
            stats.append(m + jnp.log(l) * LOG2E)
        lse_out[0, part, :] = lanes(*stats)


def window_scores(scale, h, i, q, kp, kc, qid, idp, idc, bias):
    r0 = i * TILE
    cut = BLOCK - r0
    qc = qid[r0 : r0 + TILE, :]
    s1 = nt(q, kp[r0:, head_of(h)]) * (scale * LOG2E) + bias[h, :, :cut]
    s2 = nt(q, kc[: r0 + TILE, head_of(h)]) * (scale * LOG2E) + bias[h, :, cut:]
    s1 = jnp.where(qc == idp[0, :, r0:], s1, negative_fill)
    s2 = jnp.where(qc == idc[0, :, : r0 + TILE], s2, negative_fill)
    return s1, s2


def window_kernel(scale, heads, t, q, kc, vc, kp, vp, qid, idp, idc, bias, acc, ml):
    for i in range(BLOCK // TILE):
        r0 = i * TILE
        part = slice(r0, r0 + TILE)
        peaks, sums = [], []
        for h in range(heads):
            qt = q[part, head_of(h)]
            s1, s2 = window_scores(scale, h, i, qt, kp, kc, qid, idp, idc, bias)
            m = jnp.maximum(
                jnp.max(s1, axis=1, keepdims=True), jnp.max(s2, axis=1, keepdims=True)
            )
            p1 = jnp.exp2(s1 - m)
            p2 = jnp.exp2(s2 - m)
            peaks.append(m)
            sums.append(jnp.sum(p1, axis=1, keepdims=True) + jnp.sum(p2, axis=1, keepdims=True))
            acc[0, part, head_of(h)] = nn(p1.astype(bf16), vp[r0:, head_of(h)]) + nn(
                p2.astype(bf16), vc[: r0 + TILE, head_of(h)]
            )
        ml[0, part, :] = lanes(*peaks, *sums)


def chain_kernel(t, updates, factors, before_out, total_out):
    state = jnp.zeros(total_out.shape, f32)
    for j in range(updates.shape[0]):
        before_out[j] = state
        state = factors[j] * state + updates[t[0] ^ j]
    total_out[...] = state.astype(bf16)


def scan_kernel(s, totals, factors, init, out):
    state = init[...]
    for g in range(totals.shape[0]):
        out[g] = state.astype(bf16)
        state = factors[g] * state + totals[g].astype(f32)


def chain_back_kernel(t, direct, gates, keep_rows, out):
    state = jnp.zeros(out.shape, f32)
    for j in reversed(range(direct.shape[0])):
        state = keep_rows[j] * (direct[t[0] ^ j] + gates[...] * state)
    out[...] = state.astype(bf16)


def scan_back_kernel(totals, factors, out, first_out):
    state = jnp.zeros(first_out.shape, f32)
    for g in reversed(range(totals.shape[0])):
        out[g] = state.astype(bf16)
        state = factors[g] * state + totals[g].astype(f32)
    first_out[...] = state


def carry_kernel(
    t, carried0, direct, entry, before, carry_rows, keep_rows, gates, gu_out, gate_out
):
    now = carried0[...].astype(f32)
    start = entry[...].astype(f32)
    total = jnp.zeros(gate_out.shape, f32)
    for j in reversed(range(direct.shape[0])):
        used = carry_rows[j] * start + keep_rows[j] * before[j]
        total = total + jnp.sum(now * used, axis=0, keepdims=True)
        gu_out[t[0] ^ j] = now.astype(bf16)
        now = keep_rows[j] * (direct[t[0] ^ j] + gates[...] * now)
    gate_out[...] = total


def state_kernel(
    scale, heads, t, q, entry, before, carry_row, keep_row, gates, u, acc, ml, w,
    mixed_out, stats_out, used_out, next_out, part_out,
):
    @pl.when(pl.program_id(0) == 0)
    def _():
        used = carry_row[0] * entry[...].astype(f32) + keep_row[0] * before[0]
        next_out[0] = gates[...] * used + u[0]
        used_out[0] = used.astype(bf16)

    stats = []
    for h in range(heads):
        state = used_out[0, :, head_of(h)]
        m = ml[0, :, h : h + 1]
        l = ml[0, :, heads + h : heads + h + 1]
        s = nt(q[:, head_of(h)], state) * (scale * LOG2E)
        top = jnp.maximum(m, jnp.max(s, axis=1, keepdims=True))
        p = jnp.exp2(s - top)
        shrink = jnp.exp2(m - top)
        total = l * shrink + jnp.sum(p, axis=1, keepdims=True)
        value = (acc[0, :, head_of(h)] * shrink + nn(p.astype(bf16), state)) / total
        mixed_out[0, :, head_of(h)] = value.astype(bf16)
        stats.append(top + jnp.log(total) * LOG2E)
    stats_out[0] = lanes(*stats)
    part_out[...] = nn(mixed_out[0], w[...]).astype(bf16)


def return_kernel(hidden, w, away_out, stay_out):
    even = pl.program_id(0) % 2 == 0

    @pl.when(even)
    def _():
        away_out[...] = nn(hidden[...], w[...]).astype(bf16)

    @pl.when(jnp.logical_not(even))
    def _():
        stay_out[...] = nn(hidden[...], w[...]).astype(bf16)


def norm_kernel(tok, mine, theirs, gain, residual_out, nm_out):
    residual = tok[...].astype(f32) + (mine[...].astype(f32) + theirs[...].astype(f32))
    residual_out[...] = residual
    inverse = lax.rsqrt(jnp.mean(residual * residual, axis=-1, keepdims=True) + eps)
    nm_out[...] = (residual * inverse * gain[...]).astype(bf16)


def norm_back_kernel(cot, mine, theirs, residual, gain, grad_out, low_out):
    r = residual[...]
    inverse = lax.rsqrt(jnp.mean(r * r, axis=-1, keepdims=True) + eps)
    scaled = r * inverse
    grad = (mine[...].astype(f32) + theirs[...].astype(f32)) * gain[...]
    inner = jnp.mean(grad * scaled, axis=-1, keepdims=True)
    result = cot[...].astype(f32) + inverse * (grad - scaled * inner)
    grad_out[...] = result
    low_out[...] = result.astype(bf16)


def final_kernel(tok, mine, near, far, residual_grad, gain, out):
    x = tok[...].astype(f32)
    inverse = lax.rsqrt(jnp.mean(x * x, axis=-1, keepdims=True) + eps)
    scaled = x * inverse
    grad = mine[...].astype(f32) + near[...].astype(f32) + far[...].astype(f32)
    grad = grad * gain[...]
    inner = jnp.mean(grad * scaled, axis=-1, keepdims=True)
    out[...] = residual_grad[...] + inverse * (grad - scaled * inner)


def row_sums(value):
    ones = jnp.ones((8, value.shape[1]), f32)
    return lax.dot_general(
        ones,
        value,
        (((1,), (1,)), ((), ())),
        precision=lax.Precision.HIGHEST,
        preferred_element_type=f32,
    )


def feed_grads_kernel(n, *refs):
    nms, cots = refs[:n], refs[n : 2 * n]
    gpre, hidden, w, out, gain_out = refs[2 * n :]
    rows = nms[0].shape[0]
    ff = w.shape[1]
    for which, left, right in ((0, nms, gpre), (1, cots, hidden)):
        total = None
        for r in range(n):
            piece = tn(left[r][...], right[r * rows : (r + 1) * rows, :])
            total = piece if total is None else total + piece
        out[:, which * ff : (which + 1) * ff] = total.astype(bf16)
        if which == 0:
            gain_out[...] = row_sums(total * w[...].astype(f32))


def query_grads_kernel(n, *refs):
    gas = refs[:n]
    mixed, normed, dq, w, out, row_out = refs[n:]
    rows, lw = gas[0].shape[0], dq.shape[1]
    total = None
    for r in range(n):
        piece = tn(gas[r][...], mixed[r])
        total = piece if total is None else total + piece
    out[:, lw:] = total.astype(bf16)
    grad = tn(normed[...], dq[...])
    out[:, :lw] = grad.astype(bf16)
    row_out[...] = row_sums(grad * w[...].astype(f32))


def key_grads_kernel(normed, dkv, wk, wv, dsq, row, out, row_out):
    grad = tn(normed[...], dkv[...])
    rows, lw = grad.shape[0], wk.shape[1]
    slab = rows // out.shape[0]
    part = dsq.shape[0] // out.shape[0] // 2
    low = grad.astype(bf16)
    for g in range(out.shape[0]):
        out[g, :slab] = low[g * slab : (g + 1) * slab]
        out[g, slab:, :lw] = dsq[2 * g * part : (2 * g + 1) * part].astype(bf16)
        out[g, slab:, lw:] = dsq[(2 * g + 1) * part : (2 * g + 2) * part].astype(bf16)
    both = jnp.concatenate([wk[...].astype(f32), wv[...].astype(f32)], axis=1)
    row_out[...] = row[...] + row_sums(grad * both)


def mlp_kernel(nm, gact, w, hidden_out, gpre_out, part_out):
    cols = 256
    total = None
    for c in range(w.shape[1] // cols):
        cut = slice(c * cols, (c + 1) * cols)
        pre = nn(nm[...], w[:, cut])
        cumulative = 0.5 * (1.0 + lax.erf(pre * (1.0 / math.sqrt(2.0))))
        density = jnp.exp2(pre * pre * (-0.5 * LOG2E)) * (1.0 / math.sqrt(2.0 * math.pi))
        hidden_out[:, cut] = (pre * cumulative).astype(bf16)
        gpre = (gact[:, cut].astype(f32) * (cumulative + pre * density)).astype(bf16)
        gpre_out[:, cut] = gpre
        piece = nt(gpre, w[:, cut])
        total = piece if total is None else total + piece
    part_out[...] = total.astype(bf16)


def state_back_kernel(
    scale, heads, ga, w, q, mixed, used, stats, gm_out, stats_out, dq_out, direct_out
):
    step = pl.program_id(0)
    gm_all = nt(ga[...], w[...]).astype(bf16)
    gm_out[0] = gm_all
    logs, deltas = [], []
    for h in range(heads):
        gm = gm_all[:, head_of(h)]
        qt = q[:, head_of(h)]
        state = used[0, :, head_of(h)]
        delta = jnp.sum(
            gm.astype(f32) * mixed[0, :, head_of(h)].astype(f32), axis=1, keepdims=True
        )
        lse = stats[0, :, h : h + 1]
        p = jnp.exp2(nt(qt, state) * (scale * LOG2E) - lse)
        ds = (p * (nt(gm, state) - delta)).astype(bf16)
        dq_out[0, :, head_of(h)] = nn(ds, state) * scale
        du = tn(ds, qt) * scale + tn(p.astype(bf16), gm)
        logs.append(lse)
        deltas.append(delta)

        @pl.when(step == 0)
        def _():
            direct_out[0, :, head_of(h)] = du

        @pl.when(step != 0)
        def _():
            direct_out[0, :, head_of(h)] += du

    stats_out[0] = lanes(*logs, *deltas)


def window_back_kernel(
    scale, heads, t, q, kc, vc, kb, vb, hk, hv, qid, idp, idc, bias, gm, stats, dqs,
    dq_out, dk_out, dv_out, edge_out, grad_bias, kp, vp, dkp, dvp, dkc, dvc,
):
    step = pl.program_id(0)
    last = pl.num_programs(0) - 1

    @pl.when(step == last)
    def _():
        kp[...] = hk[...]
        vp[...] = hv[...]

    @pl.when(step != last)
    def _():
        kp[...] = kb[...]
        vp[...] = vb[...]

    @pl.when(step == 0)
    def _():
        dkp[...] = jnp.zeros_like(dkp)
        dvp[...] = jnp.zeros_like(dvp)
        grad_bias[...] = jnp.zeros_like(grad_bias)

    dkc[...] = dkp[...]
    dvc[...] = dvp[...]
    dkp[...] = jnp.zeros_like(dkp)
    dvp[...] = jnp.zeros_like(dvp)
    for i in range(BLOCK // TILE):
        r0 = i * TILE
        cut = BLOCK - r0
        r1 = r0 + TILE
        part = slice(r0, r1)
        for h in range(heads):
            hs = head_of(h)
            qt = q[part, hs]
            g = gm[0, part, hs]
            lse = stats[0, part, h : h + 1]
            delta = stats[0, part, heads + h : heads + h + 1]
            s1, s2 = window_scores(scale, h, i, qt, kp, kc, qid, idp, idc, bias)
            p1 = jnp.exp2(s1 - lse)
            p2 = jnp.exp2(s2 - lse)
            ds1 = p1 * (nt(g, vp[r0:, hs]) - delta)
            ds2 = p2 * (nt(g, vc[:r1, hs]) - delta)
            grad_bias[h, :, :cut] += ds1
            grad_bias[h, :, cut:] += ds2
            ds1 = ds1.astype(bf16)
            ds2 = ds2.astype(bf16)
            dq = (nn(ds1, kp[r0:, hs]) + nn(ds2, kc[:r1, hs])) * scale + dqs[0, part, hs]
            dq_out[part, hs] = dq.astype(bf16)
            dkp[r0:, hs] += tn(ds1, qt) * scale
            dkc[:r1, hs] += tn(ds2, qt) * scale
            dvp[r0:, hs] += tn(p1.astype(bf16), g)
            dvc[:r1, hs] += tn(p2.astype(bf16), g)
    dk_out[0] = dkc[...]
    dv_out[0] = dvc[...]

    @pl.when(step == last)
    def _():
        width = heads * HEAD
        edge_out[:, :width] = dkp[...].astype(bf16)
        edge_out[:, width:] = dvp[...].astype(bf16)


def update_back_kernel(
    scale, heads, r, last, t, gu_all, k, v, sq, lse_u, u, dq, dk, dv, hk, hv, w, dsq_in,
    dkv_out, part_out, dsq_out,
):
    width = heads * HEAD
    edge = jnp.where((t[0] ^ r) == last, 1.0, 0.0)
    for h in range(heads):
        hs = head_of(h)
        gu = gu_all[0, :, hs]
        sqh = sq[:, hs]
        kh = k[:, hs]
        delta = jnp.sum(gu.astype(f32) * u[0, :, hs], axis=1, keepdims=True)
        p = jnp.exp2(nt(sqh, kh) * (scale * LOG2E) - lse_u[0, :, h : h + 1])
        ds = (p * (nt(gu, v[:, hs]) - delta)).astype(bf16)
        dsq_out[:, hs] = dsq_in[:, hs] + nn(ds, kh) * scale
        dkh = dk[0, :, hs] + tn(ds, sqh) * scale + edge * hk[:, hs].astype(f32)
        dvh = dv[0, :, hs] + tn(p.astype(bf16), gu) + edge * hv[:, hs].astype(f32)
        dkv_out[:, hs] = dkh.astype(bf16)
        dkv_out[:, width + h * HEAD : width + (h + 1) * HEAD] = dvh.astype(bf16)
    part = nt(dq[...], w[:, :width]) + nt(dkv_out[...], w[:, width:])
    part_out[...] = part.astype(bf16)


def bucket_of(distance):
    half = BUCKETS // 2
    limits = [math.ceil(half * (FAR / half) ** (level / half)) for level in range(1, half)]
    clipped = np.maximum(distance, 0)
    extra = sum((clipped >= limit).astype(np.int32) for limit in limits)
    return np.where(clipped < half, clipped, half + extra)


def local(
    tokens,
    doc_flags,
    reset_flags,
    state_init,
    gain_attn,
    w_query,
    w_key,
    w_value,
    w_output,
    bias_table,
    state_queries,
    gate_logits,
    gain_mlp,
    w_hidden,
    w_return,
    cotangent,
):
    heads = bias_table.shape[0]
    lw = w_query.shape[1]
    width = tokens.shape[1]
    nb = reset_flags.shape[0]
    ff = w_hidden.shape[1]
    scale = 1.0 / math.sqrt(HEAD)
    groups = lax.axis_size("seq")
    s_index = lax.axis_index("seq")
    t_index = lax.axis_index("tp")
    t_pre = t_index.astype(jnp.int32)[None]
    s_pre = s_index.astype(jnp.int32)[None]
    rows_all = nb * BLOCK

    def core(value):
        return lax.ppermute(value, "tp", [(i, i ^ 1) for i in range(nb)])

    def cross(value):
        return lax.ppermute(value, "tp", [(i, i ^ 2) for i in range(nb)])

    def along(value, step):
        pairs = [(i, i + step) for i in range(groups) if 0 <= i + step < groups]
        return lax.ppermute(value, "seq", pairs)

    def swap(value):
        return lax.all_to_all(value, "seq", 0, 0, tiled=True)

    def hold(value, *others):
        return lax.optimization_barrier((value, *others))[0]

    full = lambda *shape: pl.BlockSpec(shape, lambda *_: (0,) * len(shape))
    half = BLOCK // 2
    tall = lambda *tail: pl.BlockSpec((half,) + tail, lambda g, *_: (g, 0))
    share = NS // groups

    tok2 = cross(tokens)
    tok1 = core(tokens)

    every = swap(jnp.broadcast_to(reset_flags.reshape(1, nb), (groups, nb)))
    group_keep = jnp.prod((1 - every).astype(f32), axis=1)

    gates = jax.nn.sigmoid(gate_logits)
    keeps = (1 - reset_flags).astype(f32)
    gate_row = gates[None, :]
    gate_group = gates
    for _ in range(nb - 1):
        gate_group = gate_group * gates
    group_rows = (group_keep[:, None] * gate_group[None, :])[:, None, :]

    flag_prev = along(doc_flags[rows_all - BLOCK :], 1)
    ids = jnp.cumsum(jnp.concatenate([flag_prev, doc_flags]))
    ids = jnp.where((jnp.arange(rows_all + BLOCK) < BLOCK) & (s_index == 0), -1, ids)
    id_rows = ids.reshape(nb + 1, 1, BLOCK)
    id_cols = ids[BLOCK:].reshape(rows_all, 1)

    apart = BLOCK - np.arange(SPAN)
    shown = (apart >= 0) & (apart < BLOCK)
    onehot = (bucket_of(apart)[:, None] == np.arange(BUCKETS)[None, :]) & shown[:, None]
    onehot = jnp.asarray(onehot.astype(np.float32))
    base = jnp.dot(bias_table * LOG2E, onehot.T, precision=lax.Precision.HIGHEST)
    base = jnp.where(jnp.asarray(shown)[None, :], base, negative_fill)
    (bias,) = call(
        bias_kernel,
        (1,),
        (),
        [(base, full(heads, SPAN))],
        [((heads, TILE, SPAN), f32, full(heads, TILE, SPAN))],
    )

    w_joined = jnp.concatenate([w_query, w_key, w_value], axis=1)
    stacked = None
    toks = [tokens, tok1]
    for r in range(nb):
        aliases = [] if stacked is None else [(array, n) for n, array in enumerate(stacked)]
        if r == 2:
            tok2, *aliased = lax.optimization_barrier((tok2, *stacked))
            aliases = [(array, n) for n, array in enumerate(aliased)]
            toks += [tok2, core(tok2)]
            cot1 = core(cotangent)
            cot2 = cross(hold(cotangent, tok2))
        stacked = call(
            functools.partial(front_kernel, scale, heads),
            (1,),
            (),
            [
                (toks[r], full(BLOCK, width)),
                (gain_attn[None, :], full(1, width)),
                (w_joined, full(width, 3 * lw)),
                (state_queries, full(NS, lw)),
            ],
            [
                ((rows_all, width), bf16, pl.BlockSpec((BLOCK, width), lambda g, r=r: (r, 0))),
                ((rows_all, 3 * lw), bf16, pl.BlockSpec((BLOCK, 3 * lw), lambda g, r=r: (r, 0))),
                ((nb, NS, lw), f32, pl.BlockSpec((1, NS, lw), lambda g, r=r: (r, 0, 0))),
                ((nb, NS, 128), f32, pl.BlockSpec((1, NS, 128), lambda g, r=r: (r, 0, 0))),
            ],
            aliases,
            flops=2 * BLOCK * width * 3 * lw + 4 * NS * BLOCK * lw,
            nbytes=6 * BLOCK * width * 2,
            exps=heads * NS * BLOCK,
            hbm=range(4),
        )
    normed_all, qkv, updates, lse_u = stacked

    place = (t_index ^ (nb - 1)) * BLOCK
    edge = along(lax.dynamic_slice(qkv, (place, lw), (BLOCK, 2 * lw)), 1)

    block_rows = (keeps[:, None] * gates[None, :])[:, None, :]
    before, total = call(
        chain_kernel,
        (1,),
        (t_pre,),
        [(updates, full(nb, NS, lw)), (block_rows, full(nb, 1, lw))],
        [((nb, NS, lw), f32, full(nb, NS, lw)), ((NS, lw), bf16, full(NS, lw))],
        flops=nb * NS * lw * 2,
        nbytes=nb * NS * lw * 8,
        hbm=(0,),
    )
    pair_flops = 2 * BLOCK * SPAN * lw

    def window(first, count, edge, stacked, weight):
        at = lambda col, back=0: pl.BlockSpec(
            (BLOCK, lw), lambda j, t: ((j + first - back) ^ t[0], col)
        )
        ids_at = lambda back: pl.BlockSpec((1, 1, BLOCK), lambda j, t: (j + first + 1 - back, 0, 0))
        blk = lambda *tail: pl.BlockSpec((1,) + tail, lambda j, t: (j + first, 0, 0))
        if edge is None:
            before_block = [(qkv, at(1, 1)), (qkv, at(2, 1))]
        else:
            before_block = [
                (edge, pl.BlockSpec((BLOCK, lw), lambda j, t: (0, 0))),
                (edge, pl.BlockSpec((BLOCK, lw), lambda j, t: (0, 1))),
            ]
        return call(
            functools.partial(window_kernel, scale, heads),
            (count,),
            (t_pre,),
            [(qkv, at(0)), (qkv, at(1)), (qkv, at(2))]
            + before_block
            + [
                (id_cols, pl.BlockSpec((BLOCK, 1), lambda j, t: (j + first, 0))),
                (id_rows, ids_at(1)),
                (id_rows, ids_at(0)),
                (bias, full(heads, TILE, SPAN)),
            ],
            [
                ((nb, BLOCK, lw), f32, blk(BLOCK, lw)),
                ((nb, BLOCK, 128), f32, blk(BLOCK, 128)),
            ],
            [] if stacked is None else [(array, n) for n, array in enumerate(stacked)],
            flops=count * 2 * pair_flops,
            nbytes=count * BLOCK * lw * 12,
            exps=count * heads * BLOCK * SPAN,
            hbm=(0, 1),
            weight=weight,
        )

    windows = window(1, nb - 1, None, None, WEIGHT)
    late_edge, total, *windows = lax.optimization_barrier((edge, total, *windows))
    totals = swap(total.reshape(groups, share, lw))
    acc, ml = window(0, 1, late_edge, windows, HEAVY)
    cot2 = hold(cot2, acc)
    cots = [hold(cotangent, acc), hold(cot1, acc), cot2, core(cot2)]
    gacts = [nt(cot, w_return).astype(bf16) for cot in cots]
    totals, gacts[0], gacts[1] = lax.optimization_barrier((totals, gacts[0], gacts[1]))
    (entries,) = call(
        scan_kernel,
        (1,),
        (s_pre,),
        [
            (totals, full(groups, share, lw)),
            (group_rows, full(groups, 1, lw)),
            (state_init, pl.BlockSpec((share, lw), lambda g, s: (s[0], 0))),
        ],
        [((groups, share, lw), bf16, full(groups, share, lw))],
        flops=NS * lw * 2,
        nbytes=NS * lw * 4,
    )
    entry = swap(entries).reshape(NS, lw)
    starts = [jnp.ones_like(gates)]
    for j in range(nb - 1):
        starts.append(starts[j] * (gates * keeps[j]))
    carry_rows = (jnp.stack(starts) * keeps[:, None])[:, None, :]
    keep_rows = jnp.broadcast_to(keeps[:, None, None], (nb, 1, lw))

    entry, *gacts = lax.optimization_barrier((entry, *gacts))

    parts = {}
    stacked = None
    for r in (3, 2, 1, 0):
        aliases = [] if stacked is None else [(array, n) for n, array in enumerate(stacked)]
        blk = lambda *tail, r=r: pl.BlockSpec((1,) + tail, lambda g, t: (t[0] ^ r, 0, 0))
        blk_tile = lambda *tail, r=r: pl.BlockSpec((1,) + tail, lambda g, t: (t[0] ^ r, g, 0))
        pos = lambda *tail, r=r: pl.BlockSpec((1,) + tail, lambda g, t: (r, 0, 0))
        pos_tile = lambda *tail, r=r: pl.BlockSpec((1,) + tail, lambda g, t: (r, g, 0))
        *stacked, parts[r] = call(
            functools.partial(state_kernel, scale, heads),
            (2,),
            (t_pre,),
            [
                (qkv, pl.BlockSpec((half, lw), lambda g, t, r=r: (2 * r + g, 0))),
                (entry, full(NS, lw)),
                (before, blk(NS, lw)),
                (carry_rows, blk(1, lw)),
                (keep_rows, blk(1, lw)),
                (gate_row, full(1, lw)),
                (updates, pos(NS, lw)),
                (acc, blk_tile(half, lw)),
                (ml, blk_tile(half, 128)),
                (w_output, full(lw, width)),
            ],
            [
                ((nb, BLOCK, lw), bf16, pos_tile(half, lw)),
                ((nb, BLOCK, 128), f32, pos_tile(half, 128)),
                ((nb, NS, lw), bf16, pos(NS, lw)),
                ((nb, NS, lw), f32, blk(NS, lw)),
                ((BLOCK, width), bf16, tall(width)),
            ],
            aliases,
            flops=4 * BLOCK * NS * lw + 2 * BLOCK * lw * width,
            nbytes=BLOCK * (lw * 24 + width * 2),
            exps=heads * BLOCK * NS,
            hbm=range(4),
        )
    mixed_all, stats_f, used_low, block_states = stacked

    def pair_sum(mine, theirs):
        return (mine.astype(f32) + theirs.astype(f32)).astype(bf16)

    sum2 = pair_sum(parts[2], core(parts[3]))
    sum0 = pair_sum(parts[0], core(parts[1]))
    far2 = cross(sum2)
    far0 = cross(hold(sum0, far2))

    def norm_mlp(tok, mine, theirs):
        return call(
            norm_kernel,
            (2,),
            (),
            [(x, tall(width)) for x in (tok, mine, theirs)] + [(gain_mlp[None, :], full(1, width))],
            [((BLOCK, width), f32, tall(width)), ((BLOCK, width), bf16, tall(width))],
            flops=BLOCK * width * 8,
            nbytes=BLOCK * width * 12,
            hbm=(0,),
        )

    def feed(r, nm, stacked):
        aliases = [] if stacked is None else [(array, n) for n, array in enumerate(stacked)]
        return call(
            mlp_kernel,
            (2,),
            (),
            [(nm, tall(width)), (gacts[r], tall(ff)), (w_hidden, full(width, ff))],
            [
                ((rows_all, ff), bf16, pl.BlockSpec((half, ff), lambda g: (2 * r + g, 0))),
                ((rows_all, ff), bf16, pl.BlockSpec((half, ff), lambda g: (2 * r + g, 0))),
                ((BLOCK, width), bf16, tall(width)),
            ],
            aliases,
            flops=4 * BLOCK * width * ff,
            nbytes=BLOCK * width * 10,
            exps=2 * BLOCK * ff,
            hbm=(0, 1),
        )

    residual0, nm0 = norm_mlp(toks[0], sum0, far2)
    nm1 = core(nm0)
    *stacked, back0 = feed(0, nm0, None)
    *stacked, back1 = feed(1, nm1, stacked)
    far0, back1 = lax.optimization_barrier((far0, back1))
    back0 = pair_sum(back0, core(back1))
    home0 = cross(back0)
    residual2, nm2 = norm_mlp(toks[2], sum2, far0)
    nm3 = core(nm2)
    *stacked, back2 = feed(2, nm2, stacked)
    *stacked, back3 = feed(3, nm3, stacked)
    hidden_all, gpre_all = stacked
    slab = width // groups
    cut = 256
    per = cut // slab

    nms = [nm0, nm1, nm2, nm3]
    feed_grads, gain_mlp_part = call(
        functools.partial(feed_grads_kernel, nb),
        (width // cut,),
        (),
        [(x, pl.BlockSpec((BLOCK, cut), lambda g: (0, g))) for x in nms + cots]
        + [
            (gpre_all, full(rows_all, ff)),
            (hidden_all, full(rows_all, ff)),
            (w_hidden, pl.BlockSpec((cut, ff), lambda g: (g, 0))),
        ],
        [
            ((width, 2 * ff), bf16, pl.BlockSpec((cut, 2 * ff), lambda g: (g, 0))),
            ((8, width), f32, pl.BlockSpec((8, cut), lambda g: (0, g))),
        ],
        flops=4 * rows_all * width * ff,
        nbytes=rows_all * width * 8,
        mib=48,
        pin=True,
    )
    home0, back3, feed_grads = lax.optimization_barrier((home0, back3, feed_grads))
    back2 = pair_sum(back2, core(back3))
    home2 = cross(back2)

    def norm_mlp_back(cot, mine, theirs, residual):
        return call(
            norm_back_kernel,
            (2,),
            (),
            [(x, tall(width)) for x in (cot, mine, theirs, residual)]
            + [(gain_mlp[None, :], full(1, width))],
            [((BLOCK, width), f32, tall(width)), ((BLOCK, width), bf16, tall(width))],
            flops=BLOCK * width * 12,
            nbytes=BLOCK * width * 16,
            hbm=(0,),
        )

    early = lax.psum_scatter(feed_grads, "seq", scatter_dimension=0, tiled=True).astype(f32)

    _, ga2 = norm_mlp_back(cots[2], back2, home0, residual2)
    ga3 = core(ga2)
    away, stay = call(
        return_kernel,
        (nb,),
        (),
        [
            (hidden_all, pl.BlockSpec((BLOCK, ff), lambda g: (nb - 1 - g, 0))),
            (w_return, full(ff, width)),
        ],
        [
            ((2 * BLOCK, width), bf16, pl.BlockSpec((BLOCK, width), lambda g: (g // 2, 0))),
            ((2 * BLOCK, width), bf16, pl.BlockSpec((BLOCK, width), lambda g: (jnp.maximum(g - 1, 0) // 2, 0))),
        ],
        flops=2 * rows_all * ff * width,
        nbytes=rows_all * (ff + width) * 2,
    )
    stacked = None
    gas = {2: ga2, 3: ga3}
    for r in (2, 3, 0, 1):
        if r == 0:
            home2, away, stay, *stacked = lax.optimization_barrier((home2, away, stay, *stacked))
            grad_residual, gas[0] = norm_mlp_back(cots[0], back0, home2, residual0)
            gas[1] = core(gas[0])
            near_out = core(hold(away, home2))
            far_out = cross(pair_sum(stay[:BLOCK], near_out[:BLOCK]))
        aliases = [] if stacked is None else [(array, n) for n, array in enumerate(stacked)]
        pos = lambda *tail, r=r: pl.BlockSpec((1,) + tail, lambda g: (r, g, 0))
        whole = lambda *tail, r=r: pl.BlockSpec((1,) + tail, lambda g: (r, 0, 0))
        stacked = call(
            functools.partial(state_back_kernel, scale, heads),
            (2,),
            (),
            [
                (gas[r], tall(width)),
                (w_output, full(lw, width)),
                (qkv, pl.BlockSpec((half, lw), lambda g, r=r: (r * 2 + g, 0))),
                (mixed_all, pos(half, lw)),
                (used_low, whole(NS, lw)),
                (stats_f, pos(half, 128)),
            ],
            [
                ((nb, BLOCK, lw), bf16, pos(half, lw)),
                ((nb, BLOCK, 128), f32, pos(half, 128)),
                ((nb, BLOCK, lw), f32, pos(half, lw)),
                ((nb, NS, lw), f32, whole(NS, lw)),
            ],
            aliases,
            flops=2 * BLOCK * lw * width + 10 * BLOCK * NS * lw,
            nbytes=BLOCK * (width * 4 + lw * 16),
            exps=heads * BLOCK * NS,
            hbm=range(4),
        )
    gm_all, stats_b, dq_state, direct = stacked

    (local_grad,) = call(
        chain_back_kernel,
        (1,),
        (t_pre,),
        [
            (direct, full(nb, NS, lw)),
            (gate_row, full(1, lw)),
            (keep_rows, full(nb, 1, lw)),
        ],
        [((NS, lw), bf16, full(NS, lw))],
        flops=nb * NS * lw * 2,
        nbytes=nb * NS * lw * 4,
    )
    local_grads = swap(local_grad.reshape(groups, share, lw))
    turn = lambda j: nb - 1 - j
    at = lambda col: pl.BlockSpec((BLOCK, lw), lambda j, t: (turn(j) ^ t[0], col))
    prev = lambda col: pl.BlockSpec(
        (BLOCK, lw), lambda j, t: (jnp.maximum(turn(j) - 1, 0) ^ t[0], col)
    )
    pos = lambda *tail: pl.BlockSpec((1,) + tail, lambda j, t: (turn(j) ^ t[0], 0, 0))
    dq, dk, dv, back_kv, bias_grad = call(
        functools.partial(window_back_kernel, scale, heads),
        (nb,),
        (t_pre,),
        [
            (qkv, at(0)),
            (qkv, at(1)),
            (qkv, at(2)),
            (qkv, prev(1)),
            (qkv, prev(2)),
            (edge, pl.BlockSpec((BLOCK, lw), lambda j, t: (0, 0))),
            (edge, pl.BlockSpec((BLOCK, lw), lambda j, t: (0, 1))),
            (id_cols, pl.BlockSpec((BLOCK, 1), lambda j, t: (turn(j), 0))),
            (id_rows, pl.BlockSpec((1, 1, BLOCK), lambda j, t: (turn(j), 0, 0))),
            (id_rows, pl.BlockSpec((1, 1, BLOCK), lambda j, t: (turn(j) + 1, 0, 0))),
            (bias, full(heads, TILE, SPAN)),
            (gm_all, pos(BLOCK, lw)),
            (stats_b, pos(BLOCK, 128)),
            (dq_state, pos(BLOCK, lw)),
        ],
        [
            ((rows_all, lw), bf16, pl.BlockSpec((BLOCK, lw), lambda j, t: (turn(j) ^ t[0], 0))),
            ((nb, BLOCK, lw), f32, pos(BLOCK, lw)),
            ((nb, BLOCK, lw), f32, pos(BLOCK, lw)),
            ((BLOCK, 2 * lw), bf16, full(BLOCK, 2 * lw)),
            ((heads, TILE, SPAN), f32, full(heads, TILE, SPAN)),
        ],
        scratch=[pltpu.VMEM((BLOCK, lw), bf16)] * 2 + [pltpu.VMEM((BLOCK, lw), f32)] * 4,
        flops=nb * 5 * pair_flops,
        nbytes=nb * BLOCK * lw * 24,
        exps=nb * heads * BLOCK * SPAN,
        hbm=range(3),
    )
    local_grads = hold(local_grads, dq)
    carries, grad_state = call(
        scan_back_kernel,
        (1,),
        (),
        [(local_grads, full(groups, share, lw)), (group_rows, full(groups, 1, lw))],
        [
            ((groups, share, lw), bf16, full(groups, share, lw)),
            ((share, lw), f32, full(share, lw)),
        ],
        flops=NS * lw * 2,
        nbytes=NS * lw * 4,
    )
    carried = swap(carries).reshape(NS, lw)

    next_kv = along(back_kv, -1)
    (bias_line,) = call(
        bias_sum_kernel,
        (1,),
        (),
        [(bias_grad, full(heads, TILE, SPAN))],
        [((heads, SPAN), f32, full(heads, SPAN))],
    )
    bias_local = jnp.dot(bias_line, onehot, precision=lax.Precision.HIGHEST)

    mid, row_part = call(
        functools.partial(query_grads_kernel, nb),
        (width // cut,),
        (),
        [(gas[r], pl.BlockSpec((BLOCK, cut), lambda g: (0, g))) for r in range(nb)]
        + [
            (mixed_all, full(nb, BLOCK, lw)),
            (normed_all, pl.BlockSpec((rows_all, cut), lambda g: (0, g))),
            (dq, full(rows_all, lw)),
            (w_query, pl.BlockSpec((cut, lw), lambda g: (g, 0))),
        ],
        [
            ((width, 2 * lw), bf16, pl.BlockSpec((cut, 2 * lw), lambda g: (g, 0))),
            ((8, width), f32, pl.BlockSpec((8, cut), lambda g: (0, g))),
        ],
        flops=4 * rows_all * width * lw,
        nbytes=rows_all * width * 4,
        mib=32,
        pin=True,
    )
    carried, mid, *_ = lax.optimization_barrier((carried, mid, far_out, bias_local))
    mid = swap(mid.reshape(groups, width // groups, 2 * lw))
    result = (
        residual0 + stay[BLOCK:].astype(f32) + near_out[BLOCK:].astype(f32) + far_out.astype(f32)
    ).astype(bf16)

    gu_all, gate_sum = call(
        carry_kernel,
        (1,),
        (t_pre,),
        [
            (carried, full(NS, lw)),
            (direct, full(nb, NS, lw)),
            (entry, full(NS, lw)),
            (before, full(nb, NS, lw)),
            (carry_rows, full(nb, 1, lw)),
            (keep_rows, full(nb, 1, lw)),
            (gate_row, full(1, lw)),
        ],
        [((nb, NS, lw), bf16, full(nb, NS, lw)), ((1, lw), f32, full(1, lw))],
        flops=nb * NS * lw * 8,
        nbytes=nb * NS * lw * 10,
    )
    parts = {}
    dkv = None
    grad_sq = jnp.zeros((NS, lw), f32)
    for r in (3, 2, 1, 0):
        if r == 1:
            far = pair_sum(parts[2], core(parts[3]))
            gu_all = hold(gu_all, far)
            far = cross(far)
        pos = lambda *tail, r=r: pl.BlockSpec((1,) + tail, lambda g, t: (r, 0, 0))
        row = lambda cols, col=0, r=r: pl.BlockSpec((BLOCK, cols), lambda g, t: (r, col))
        dkv, parts[r], grad_sq = call(
            functools.partial(update_back_kernel, scale, heads, r, nb - 1),
            (1,),
            (t_pre,),
            [
                (gu_all, pos(NS, lw)),
                (qkv, row(lw, 1)),
                (qkv, row(lw, 2)),
                (state_queries, full(NS, lw)),
                (lse_u, pos(NS, 128)),
                (updates, pos(NS, lw)),
                (dq, row(lw)),
                (dk, pos(BLOCK, lw)),
                (dv, pos(BLOCK, lw)),
                (next_kv, pl.BlockSpec((BLOCK, lw), lambda g, t: (0, 0))),
                (next_kv, pl.BlockSpec((BLOCK, lw), lambda g, t: (0, 1))),
                (w_joined, full(width, 3 * lw)),
                (grad_sq, full(NS, lw)),
            ],
            [
                ((rows_all, 2 * lw), bf16, row(2 * lw)),
                ((BLOCK, width), bf16, full(BLOCK, width)),
                ((NS, lw), f32, full(NS, lw)),
            ],
            [] if dkv is None else [(dkv, 0)],
            flops=10 * NS * BLOCK * lw + 6 * BLOCK * lw * width,
            nbytes=BLOCK * (lw * 30 + width * 2),
            exps=heads * NS * BLOCK,
            hbm=(0,),
        )
    near = core(parts[1])

    late, gain_attn_part = call(
        key_grads_kernel,
        (width // cut,),
        (),
        [
            (normed_all, pl.BlockSpec((rows_all, cut), lambda g: (0, g))),
            (dkv, full(rows_all, 2 * lw)),
            (w_key, pl.BlockSpec((cut, lw), lambda g: (g, 0))),
            (w_value, pl.BlockSpec((cut, lw), lambda g: (g, 0))),
            (grad_sq, pl.BlockSpec((per * share, lw), lambda g: (g, 0))),
            (row_part, pl.BlockSpec((8, cut), lambda g: (0, g))),
        ],
        [
            (
                (groups, slab + share // 2, 2 * lw),
                bf16,
                pl.BlockSpec((per, slab + share // 2, 2 * lw), lambda g: (g, 0, 0)),
            ),
            ((8, width), f32, pl.BlockSpec((8, cut), lambda g: (0, g))),
        ],
        flops=4 * rows_all * width * lw,
        nbytes=rows_all * width * 4,
        mib=32,
    )
    late = swap(hold(late, far))

    bias_full = lax.dynamic_update_slice(
        jnp.zeros((H, BUCKETS), f32), bias_local, (t_index * heads, 0)
    )
    gate_full = lax.dynamic_update_slice(
        jnp.zeros((D,), f32), gate_sum[0] * gates * (1.0 - gates), (t_index * lw,)
    )
    small = jnp.concatenate(
        [
            gain_attn_part[0] / gain_attn,
            gain_mlp_part[0] / gain_mlp,
            gate_full,
            bias_full.reshape(-1),
        ]
    ).reshape(-1, 128)
    small = hold(small, mid)
    small = small + core(small)
    small = small + cross(small)
    step = 1
    while step < groups:
        small = small + lax.ppermute(small, "seq", [(i, i ^ step) for i in range(groups)])
        step *= 2
    small = small.reshape(-1)

    (grad_tokens,) = call(
        final_kernel,
        (2,),
        (),
        [(x, tall(width)) for x in (tokens, parts[0], near, far, grad_residual)]
        + [(gain_attn[None, :], full(1, width))],
        [((BLOCK, width), f32, tall(width))],
        flops=BLOCK * width * 12,
        nbytes=BLOCK * width * 16,
    )

    mid = jnp.sum(mid.astype(f32), axis=0)
    late = jnp.sum(late.astype(f32), axis=0)
    queries_sent = jnp.concatenate([late[slab:, :lw], late[slab:, lw:]])
    return (
        result,
        block_states,
        grad_tokens,
        grad_state,
        small[:D],
        mid[:, :lw],
        late[:slab, :lw],
        late[:slab, lw:],
        mid[:, lw:].T,
        small[3 * D :].reshape(H, BUCKETS),
        queries_sent,
        small[2 * D : 3 * D],
        small[D : 2 * D],
        early[:, :ff],
        early[:, ff:].T,
    )


def solution(mesh):
    return jax.shard_map(
        local,
        mesh=mesh,
        in_specs=(
            P(("seq", "tp"), None),
            P("seq"),
            P("seq"),
            P(None, "tp"),
            P(),
            P(None, "tp"),
            P(None, "tp"),
            P(None, "tp"),
            P("tp", None),
            P("tp", None),
            P(None, "tp"),
            P("tp"),
            P(),
            P(None, "tp"),
            P("tp", None),
            P(("seq", "tp"), None),
        ),
        out_specs=(
            P(("seq", "tp"), None),
            P("seq", None, "tp"),
            P(("seq", "tp"), None),
            P("seq", "tp"),
            P(),
            P("seq", "tp"),
            P("seq", "tp"),
            P("seq", "tp"),
            P("tp", "seq"),
            P(),
            P("seq", "tp"),
            P(),
            P(),
            P("seq", "tp"),
            P("tp", "seq"),
        ),
        check_vma=False,
    )
```

```python
import functools
import math

import jax
import jax.numpy as jnp
import numpy as np
from jax import lax
from jax.experimental import pallas as pl
from jax.experimental.pallas import tpu as pltpu
from jax.sharding import PartitionSpec as P

D = 1024
H = 8
NS = 512
BLOCK = 512
BUCKETS = 32
FAR = 128
TILE = 128
SPAN = BLOCK + TILE
HEAD = 128

eps = 1e-06
negative_fill = -1e30
LOG2E = math.log2(math.e)
WEIGHT = 0.05
HEAVY = 1.0
f32 = jnp.float32
bf16 = jnp.bfloat16


def nn(a, b):
    return lax.dot_general(a, b, (((1,), (0,)), ((), ())), preferred_element_type=f32)


def nt(a, b):
    return lax.dot_general(a, b, (((1,), (1,)), ((), ())), preferred_element_type=f32)


def tn(a, b):
    return lax.dot_general(a, b, (((0,), (0,)), ((), ())), preferred_element_type=f32)


def pinned(array):
    return pltpu.with_memory_space_constraint(array, pltpu.HBM)


def call(
    kernel, grid, prefetch, ins, outs, aliases=(), scratch=(), flops=0, nbytes=0, exps=0, mib=24,
    hbm=(), pin=(), weight=WEIGHT,
):
    any_spec = pl.BlockSpec(memory_space=pl.ANY)
    arrays = [
        pinned(array) if n in pin or array.ndim == 3 or array.shape[0] > D else array
        for n, (array, _) in enumerate(ins)
    ]
    arrays += [pinned(array) for array, _ in aliases]
    specs = [spec for _, spec in ins] + [any_spec for _ in aliases]
    first = len(prefetch) + len(ins)
    alias_map = {first + n: out for n, (_, out) in enumerate(aliases)}
    n_pre, n_in, n_alias = len(prefetch), len(ins), len(aliases)

    def body(*refs):
        kept = refs[: n_pre + n_in] + refs[n_pre + n_in + n_alias :]
        kernel(*kept)

    return pl.pallas_call(
        body,
        name=getattr(kernel, 'func', kernel).__name__,
        out_shape=[
            pltpu.HBM(shape, dtype)
            if len(shape) == 3 or shape[0] > D or n in hbm
            else jax.ShapeDtypeStruct(shape, dtype)
            for n, (shape, dtype, _) in enumerate(outs)
        ],
        grid_spec=pltpu.PrefetchScalarGridSpec(
            num_scalar_prefetch=n_pre,
            grid=grid,
            in_specs=specs,
            out_specs=[spec for _, _, spec in outs],
            scratch_shapes=list(scratch),
        ),
        input_output_aliases=alias_map,
        compiler_params=pltpu.CompilerParams(
            dimension_semantics=("arbitrary",) * len(grid), vmem_limit_bytes=mib * 1024 * 1024
        ),
        cost_estimate=pl.CostEstimate(
            flops=int(flops * weight),
            bytes_accessed=int(nbytes * weight),
            transcendentals=int(exps * weight),
        ),
    )(*prefetch, *arrays)


def lanes(*columns):
    rows = columns[0].shape[0]
    lane = lax.broadcasted_iota(jnp.int32, (rows, 128), 1)
    packed = jnp.broadcast_to(columns[0], (rows, 128))
    for n, column in enumerate(columns[1:], 1):
        packed = jnp.where(lane == n, column, packed)
    return packed


def pick(*columns):
    lane = lax.broadcasted_iota(jnp.int32, columns[0].shape, 1)
    packed = columns[0]
    for n, column in enumerate(columns[1:], 1):
        packed = jnp.where(lane == n, column, packed)
    return packed


def with_ones(values):
    return jnp.concatenate([values, jnp.ones((values.shape[0], HEAD), bf16)], axis=1)


def head_of(h):
    return slice(h * HEAD, (h + 1) * HEAD)


def bias_kernel(base_ref, out_ref):
    for h in range(out_ref.shape[0]):
        row = jnp.broadcast_to(base_ref[h : h + 1, :], (TILE, SPAN))
        out_ref[h] = pltpu.roll(row, 0, 1, stride=1, stride_axis=0)


def bias_sum_kernel(grad_ref, out_ref):
    rows = lax.broadcasted_iota(jnp.int32, (TILE, SPAN), 0)
    for h in range(grad_ref.shape[0]):
        value = grad_ref[h]
        step = 1
        while step < TILE:
            moved = pltpu.roll(value, SPAN - step, 1)
            value = jnp.where((rows & step) != 0, moved, value)
            step *= 2
        out_ref[h : h + 1, :] = jnp.sum(value, axis=0, keepdims=True)


def front_kernel(scale, heads, tok_a, tok_b, gain, w, sq, normed_out, qkv_out, u_out, lse_out):
    width = heads * HEAD
    first = pl.program_id(0) == 0
    rows = 256
    for i in range(BLOCK // rows):
        part = slice(i * rows, (i + 1) * rows)
        x = jnp.where(first, tok_a[part, :].astype(f32), tok_b[part, :].astype(f32))
        r = lax.rsqrt(jnp.mean(x * x, axis=-1, keepdims=True) + eps)
        n = (x * r * gain[...]).astype(bf16)
        normed_out[part, :] = n
        qkv_out[part, :] = nn(n, w[...]).astype(bf16)
    values = [
        with_ones(qkv_out[:, 2 * width + h * HEAD : 2 * width + (h + 1) * HEAD])
        for h in range(heads)
    ]
    for i in range(BLOCK // rows):
        part = slice(i * rows, (i + 1) * rows)
        stats = []
        for h in range(heads):
            k = qkv_out[:, width + h * HEAD : width + (h + 1) * HEAD]
            s = nt(sq[part, head_of(h)], k) * (scale * LOG2E)
            m = jnp.max(s, axis=1, keepdims=True)
            p = jnp.exp2(s - m)
            both = nn(p.astype(bf16), values[h])
            total = both[:, HEAD:]
            u_out[0, part, head_of(h)] = both[:, :HEAD] / total
            stats.append(m + jnp.log(total) * LOG2E)
        lse_out[0, part, :] = pick(*stats)


def window_scores(scale, h, i, q, kp, kc, qid, idp, idc, bias):
    r0 = i * TILE
    cut = BLOCK - r0
    qc = qid[r0 : r0 + TILE, :]
    s1 = nt(q, kp[r0:, head_of(h)]) * (scale * LOG2E) + bias[h, :, :cut]
    s2 = nt(q, kc[: r0 + TILE, head_of(h)]) * (scale * LOG2E) + bias[h, :, cut:]
    s1 = jnp.where(qc == idp[0, :, r0:], s1, negative_fill)
    s2 = jnp.where(qc == idc[0, :, : r0 + TILE], s2, negative_fill)
    return s1, s2


def window_kernel(scale, heads, t, q, kc, vc, kp, vp, qid, idp, idc, bias, acc, ml):
    before_values = [with_ones(vp[:, head_of(h)]) for h in range(heads)]
    own_values = [with_ones(vc[:, head_of(h)]) for h in range(heads)]
    for i in range(BLOCK // TILE):
        r0 = i * TILE
        part = slice(r0, r0 + TILE)
        peaks, sums = [], []
        for h in range(heads):
            qt = q[part, head_of(h)]
            s1, s2 = window_scores(scale, h, i, qt, kp, kc, qid, idp, idc, bias)
            m = jnp.maximum(
                jnp.max(s1, axis=1, keepdims=True), jnp.max(s2, axis=1, keepdims=True)
            )
            p1 = jnp.exp2(s1 - m)
            p2 = jnp.exp2(s2 - m)
            both = nn(p1.astype(bf16), before_values[h][r0:, :]) + nn(
                p2.astype(bf16), own_values[h][: r0 + TILE, :]
            )
            acc[0, part, head_of(h)] = both[:, :HEAD]
            peaks.append(jnp.broadcast_to(m, (TILE, HEAD)))
            sums.append(both[:, HEAD:])
        ml[0, part, :] = pick(*peaks, *sums)


def chain_kernel(t, updates, factors, before_out, total_out):
    state = jnp.zeros(total_out.shape, f32)
    for j in range(updates.shape[0]):
        before_out[j] = state
        state = factors[j] * state + updates[t[0] ^ j]
    total_out[...] = state.astype(bf16)


def scan_kernel(s, totals, factors, init, out):
    state = init[...]
    for g in range(totals.shape[0]):
        out[g] = state.astype(bf16)
        state = factors[g] * state + totals[g].astype(f32)


def chain_back_kernel(t, direct, gates, keep_rows, out):
    state = jnp.zeros(out.shape, f32)
    for j in reversed(range(direct.shape[0])):
        state = keep_rows[j] * (direct[t[0] ^ j] + gates[...] * state)
    out[...] = state.astype(bf16)


def scan_back_kernel(totals, factors, out, first_out):
    state = jnp.zeros(first_out.shape, f32)
    for g in reversed(range(totals.shape[0])):
        out[g] = state.astype(bf16)
        state = factors[g] * state + totals[g].astype(f32)
    first_out[...] = state


def carry_kernel(
    t, carried0, direct, entry, before, carry_rows, keep_rows, gates, gu_out, gate_out
):
    now = carried0[...].astype(f32)
    start = entry[...].astype(f32)
    total = jnp.zeros(gate_out.shape, f32)
    for j in reversed(range(direct.shape[0])):
        used = carry_rows[j] * start + keep_rows[j] * before[j]
        total = total + jnp.sum(now * used, axis=0, keepdims=True)
        gu_out[t[0] ^ j] = now.astype(bf16)
        now = keep_rows[j] * (direct[t[0] ^ j] + gates[...] * now)
    gate_out[...] = total


def state_kernel(
    scale, heads, t, q, entry, before, carry_row, keep_row, acc, ml, w,
    mixed_out, stats_out, used_out, first_out, second_out,
):
    used_out[0] = (carry_row[0] * entry[...].astype(f32) + keep_row[0] * before[0]).astype(bf16)
    values = [with_ones(used_out[0, :, head_of(h)]) for h in range(heads)]
    rows = 256
    for i in range(BLOCK // rows):
        part = slice(i * rows, (i + 1) * rows)
        stats = []
        for h in range(heads):
            m = ml[0, part, h : h + 1]
            l = ml[0, part, heads + h : heads + h + 1]
            s = nt(q[part, head_of(h)], used_out[0, :, head_of(h)]) * (scale * LOG2E)
            top = jnp.maximum(m, jnp.max(s, axis=1, keepdims=True))
            p = jnp.exp2(s - top)
            shrink = jnp.exp2(m - top)
            both = nn(p.astype(bf16), values[h])
            total = l * shrink + both[:, HEAD:]
            value = (acc[0, part, head_of(h)] * shrink + both[:, :HEAD]) / total
            mixed_out[0, part, head_of(h)] = value.astype(bf16)
            stats.append(top + jnp.log(total) * LOG2E)
        stats_out[0, part, :] = pick(*stats)
    result = nn(mixed_out[0], w[...]).astype(bf16)
    first = pl.program_id(0) == 0

    @pl.when(first)
    def _():
        first_out[...] = result

    @pl.when(jnp.logical_not(first))
    def _():
        second_out[...] = result


def states_kernel(t, entry, before, carry_row, keep_row, gates, u, next_out):
    used = carry_row[0] * entry[...].astype(f32) + keep_row[0] * before[0]
    next_out[0] = gates[...] * used + u[0]


def return_kernel(hidden, w, away_out, stay_out):
    even = pl.program_id(0) % 2 == 0

    @pl.when(even)
    def _():
        away_out[...] = nn(hidden[...], w[...]).astype(bf16)

    @pl.when(jnp.logical_not(even))
    def _():
        stay_out[...] = nn(hidden[...], w[...]).astype(bf16)


def norm_kernel(tok, mine, theirs, gain, residual_out, nm_out):
    residual = tok[...].astype(f32) + (mine[...].astype(f32) + theirs[...].astype(f32))
    residual_out[...] = residual
    inverse = lax.rsqrt(jnp.mean(residual * residual, axis=-1, keepdims=True) + eps)
    nm_out[...] = (residual * inverse * gain[...]).astype(bf16)


def norm_back_kernel(cot, mine, theirs, residual, gain, grad_out, low_out):
    r = residual[...]
    inverse = lax.rsqrt(jnp.mean(r * r, axis=-1, keepdims=True) + eps)
    scaled = r * inverse
    grad = (mine[...].astype(f32) + theirs[...].astype(f32)) * gain[...]
    inner = jnp.mean(grad * scaled, axis=-1, keepdims=True)
    result = cot[...].astype(f32) + inverse * (grad - scaled * inner)
    grad_out[...] = result
    low_out[...] = result.astype(bf16)


def final_kernel(tok, mine, near, far, residual_grad, gain, out):
    x = tok[...].astype(f32)
    inverse = lax.rsqrt(jnp.mean(x * x, axis=-1, keepdims=True) + eps)
    scaled = x * inverse
    grad = mine[...].astype(f32) + near[...].astype(f32) + far[...].astype(f32)
    grad = grad * gain[...]
    inner = jnp.mean(grad * scaled, axis=-1, keepdims=True)
    out[...] = residual_grad[...] + inverse * (grad - scaled * inner)


def row_sums(value):
    sums = jnp.broadcast_to(jnp.sum(value, axis=1, keepdims=True), (value.shape[0], HEAD))
    return sums.T[:8]


def feed_grads_kernel(n, s, *refs):
    nms, cots = refs[:n], refs[n : 2 * n]
    gpre, hidden, w, kept_out, sent_out, return_out, gain_out = refs[2 * n :]
    odd = s[0] % 2 == 1
    rows = nms[0].shape[0]
    ff = w.shape[1]
    for which, left, right in ((0, nms, gpre), (1, cots, hidden)):
        total = None
        for r in range(n):
            piece = tn(left[r][...], right[r * rows : (r + 1) * rows, :])
            total = piece if total is None else total + piece
        low = total.astype(bf16)
        if which == 0:
            slab = kept_out.shape[1]
            for g in range(kept_out.shape[0]):
                even_rows = low[2 * g * slab : (2 * g + 1) * slab]
                odd_rows = low[(2 * g + 1) * slab : (2 * g + 2) * slab]
                kept_out[g] = jnp.where(odd, odd_rows, even_rows)
                sent_out[g] = jnp.where(odd, even_rows, odd_rows)
        else:
            return_out[...] = low
        if which == 0:
            gain_out[...] = row_sums(total * w[...].astype(f32))


def query_grads_kernel(n, *refs):
    gas = refs[:n]
    mixed, normed, dq, w, out, row_out = refs[n:]
    rows, lw = gas[0].shape[0], dq.shape[1]
    total = None
    for r in range(n):
        piece = tn(gas[r][...], mixed[r])
        total = piece if total is None else total + piece
    out[:, lw:] = total.astype(bf16)
    grad = tn(normed[...], dq[...])
    out[:, :lw] = grad.astype(bf16)
    row_out[...] = row_sums(grad * w[...].astype(f32))


def key_grads_kernel(normed, dkv, wk, wv, dsq, row, out, row_out):
    grad = tn(normed[...], dkv[...])
    rows, lw = grad.shape[0], wk.shape[1]
    slab = rows // out.shape[0]
    part = dsq.shape[0] // out.shape[0] // 2
    low = grad.astype(bf16)
    for g in range(out.shape[0]):
        out[g, :slab] = low[g * slab : (g + 1) * slab]
        out[g, slab:, :lw] = dsq[2 * g * part : (2 * g + 1) * part].astype(bf16)
        out[g, slab:, lw:] = dsq[(2 * g + 1) * part : (2 * g + 2) * part].astype(bf16)
    both = jnp.concatenate([wk[...].astype(f32), wv[...].astype(f32)], axis=1)
    row_out[...] = row[...] + row_sums(grad * both)


def mlp_kernel(steps, nm_a, nm_b, gact_a, gact_b, w, hidden_out, gpre_out, first_out, second_out):
    first = pl.program_id(0) < steps
    cols = 256
    x = jnp.where(first, nm_a[...], nm_b[...])
    for c in range(w.shape[1] // cols):
        cut = slice(c * cols, (c + 1) * cols)
        pre = nn(x, w[:, cut])
        cumulative = 0.5 * (1.0 + lax.erf(pre * (1.0 / math.sqrt(2.0))))
        density = jnp.exp2(pre * pre * (-0.5 * LOG2E)) * (1.0 / math.sqrt(2.0 * math.pi))
        hidden_out[:, cut] = (pre * cumulative).astype(bf16)
        gact = jnp.where(first, gact_a[:, cut].astype(f32), gact_b[:, cut].astype(f32))
        gpre_out[:, cut] = (gact * (cumulative + pre * density)).astype(bf16)
    result = nt(gpre_out[...], w[...]).astype(bf16)

    @pl.when(first)
    def _():
        first_out[...] = result

    @pl.when(jnp.logical_not(first))
    def _():
        second_out[...] = result


def state_back_kernel(
    scale, heads, ga_a, ga_b, w, q, mixed, used, stats, gm_out, stats_out, dq_out, direct_out
):
    first = pl.program_id(0) == 0
    gm_out[0] = nt(jnp.where(first, ga_a[...], ga_b[...]), w[...]).astype(bf16)
    logs, deltas = [], []
    for h in range(heads):
        hs = head_of(h)
        gm = gm_out[0, :, hs]
        qt = q[:, hs]
        state = used[0, :, hs]
        delta = jnp.sum(gm.astype(f32) * mixed[0, :, hs].astype(f32), axis=1, keepdims=True)
        lse = stats[0, :, h : h + 1]
        p = jnp.exp2(nt(qt, state) * (scale * LOG2E) - lse)
        ds = (p * (nt(gm, state) - delta)).astype(bf16)
        dq_out[0, :, hs] = nn(ds, state) * scale
        direct_out[0, :, hs] = tn(ds, qt) * scale + tn(p.astype(bf16), gm)
        logs.append(lse)
        deltas.append(delta)
    stats_out[0] = lanes(*logs, *deltas)


def window_back_kernel(
    scale, heads, t, q, kc, vc, kb, vb, hk, hv, qid, idp, idc, bias, gm, stats, dqs,
    dq_out, dk_out, dv_out, edge_out, grad_bias, kp, vp, dkp, dvp, dkc, dvc,
):
    step = pl.program_id(0)
    last = pl.num_programs(0) - 1

    @pl.when(step == last)
    def _():
        kp[...] = hk[...]
        vp[...] = hv[...]

    @pl.when(step != last)
    def _():
        kp[...] = kb[...]
        vp[...] = vb[...]

    @pl.when(step == 0)
    def _():
        dkp[...] = jnp.zeros_like(dkp)
        dvp[...] = jnp.zeros_like(dvp)
        grad_bias[...] = jnp.zeros_like(grad_bias)

    dkc[...] = dkp[...]
    dvc[...] = dvp[...]
    dkp[...] = jnp.zeros_like(dkp)
    dvp[...] = jnp.zeros_like(dvp)
    for i in range(BLOCK // TILE):
        r0 = i * TILE
        cut = BLOCK - r0
        r1 = r0 + TILE
        part = slice(r0, r1)
        for h in range(heads):
            hs = head_of(h)
            qt = q[part, hs]
            g = gm[0, part, hs]
            lse = stats[0, part, h : h + 1]
            delta = stats[0, part, heads + h : heads + h + 1]
            s1, s2 = window_scores(scale, h, i, qt, kp, kc, qid, idp, idc, bias)
            p1 = jnp.exp2(s1 - lse)
            p2 = jnp.exp2(s2 - lse)
            ds1 = p1 * (nt(g, vp[r0:, hs]) - delta)
            ds2 = p2 * (nt(g, vc[:r1, hs]) - delta)
            grad_bias[h, :, :cut] += ds1
            grad_bias[h, :, cut:] += ds2
            ds1 = ds1.astype(bf16)
            ds2 = ds2.astype(bf16)
            dq = (nn(ds1, kp[r0:, hs]) + nn(ds2, kc[:r1, hs])) * scale + dqs[0, part, hs]
            dq_out[part, hs] = dq.astype(bf16)
            dkp[r0:, hs] += tn(ds1, qt) * scale
            dkc[:r1, hs] += tn(ds2, qt) * scale
            dvp[r0:, hs] += tn(p1.astype(bf16), g)
            dvc[:r1, hs] += tn(p2.astype(bf16), g)
    dk_out[0] = dkc[...]
    dv_out[0] = dvc[...]

    @pl.when(step == last)
    def _():
        width = heads * HEAD
        edge_out[:, :width] = dkp[...].astype(bf16)
        edge_out[:, width:] = dvp[...].astype(bf16)


def update_back_kernel(
    scale, heads, high, last, t, gu_all, k, v, sq, lse_u, u, dq, dk, dv, hk, hv, w, dsq_in,
    dkv_out, first_out, second_out, dsq_out,
):
    width = heads * HEAD
    step = pl.program_id(0)
    edge = jnp.where((t[0] ^ (high - step)) == last, 1.0, 0.0)

    @pl.when(step == 0)
    def _():
        dsq_out[...] = dsq_in[...]

    for h in range(heads):
        hs = head_of(h)
        gu = gu_all[0, :, hs]
        sqh = sq[:, hs]
        kh = k[:, hs]
        delta = jnp.sum(gu.astype(f32) * u[0, :, hs], axis=1, keepdims=True)
        p = jnp.exp2(nt(sqh, kh) * (scale * LOG2E) - lse_u[0, :, h : h + 1])
        ds = (p * (nt(gu, v[:, hs]) - delta)).astype(bf16)
        dsq_out[:, hs] += nn(ds, kh) * scale
        dkh = dk[0, :, hs] + tn(ds, sqh) * scale + edge * hk[:, hs].astype(f32)
        dvh = dv[0, :, hs] + tn(p.astype(bf16), gu) + edge * hv[:, hs].astype(f32)
        dkv_out[:, hs] = dkh.astype(bf16)
        dkv_out[:, width + h * HEAD : width + (h + 1) * HEAD] = dvh.astype(bf16)
    part = nt(dq[...], w[:, :width]) + nt(dkv_out[...], w[:, width:])
    result = part.astype(bf16)

    @pl.when(step == 0)
    def _():
        first_out[...] = result

    @pl.when(step != 0)
    def _():
        second_out[...] = result


def bucket_of(distance):
    half = BUCKETS // 2
    limits = [math.ceil(half * (FAR / half) ** (level / half)) for level in range(1, half)]
    clipped = np.maximum(distance, 0)
    extra = sum((clipped >= limit).astype(np.int32) for limit in limits)
    return np.where(clipped < half, clipped, half + extra)


def local(
    tokens,
    doc_flags,
    reset_flags,
    state_init,
    gain_attn,
    w_query,
    w_key,
    w_value,
    w_output,
    bias_table,
    state_queries,
    gate_logits,
    gain_mlp,
    w_hidden,
    w_return,
    cotangent,
):
    heads = bias_table.shape[0]
    lw = w_query.shape[1]
    width = tokens.shape[1]
    nb = reset_flags.shape[0]
    ff = w_hidden.shape[1]
    scale = 1.0 / math.sqrt(HEAD)
    groups = lax.axis_size("seq")
    s_index = lax.axis_index("seq")
    t_index = lax.axis_index("tp")
    t_pre = t_index.astype(jnp.int32)[None]
    s_pre = s_index.astype(jnp.int32)[None]
    rows_all = nb * BLOCK

    def core(value):
        return lax.ppermute(value, "tp", [(i, i ^ 1) for i in range(nb)])

    def cross(value):
        return lax.ppermute(value, "tp", [(i, i ^ 2) for i in range(nb)])

    def along(value, step):
        pairs = [(i, i + step) for i in range(groups) if 0 <= i + step < groups]
        return lax.ppermute(value, "seq", pairs)

    def swap(value):
        return lax.all_to_all(value, "seq", 0, 0, tiled=True)

    def hold(value, *others):
        return lax.optimization_barrier((value, *others))[0]

    full = lambda *shape: pl.BlockSpec(shape, lambda *_: (0,) * len(shape))
    half = BLOCK // 2
    tall = lambda *tail: pl.BlockSpec((half,) + tail, lambda g, *_: (g, 0))
    share = NS // groups

    tok2 = cross(tokens)
    tok1 = core(tokens)

    every = swap(jnp.broadcast_to(reset_flags.reshape(1, nb), (groups, nb)))
    group_keep = jnp.prod((1 - every).astype(f32), axis=1)

    gates = jax.nn.sigmoid(gate_logits)
    keeps = (1 - reset_flags).astype(f32)
    gate_row = gates[None, :]
    gate_group = gates
    for _ in range(nb - 1):
        gate_group = gate_group * gates
    group_rows = (group_keep[:, None] * gate_group[None, :])[:, None, :]

    flag_prev = along(doc_flags[rows_all - BLOCK :], 1)
    ids = jnp.cumsum(jnp.concatenate([flag_prev, doc_flags]))
    ids = jnp.where((jnp.arange(rows_all + BLOCK) < BLOCK) & (s_index == 0), -1, ids)
    id_rows = ids.reshape(nb + 1, 1, BLOCK)
    id_cols = ids[BLOCK:].reshape(rows_all, 1)

    apart = BLOCK - np.arange(SPAN)
    shown = (apart >= 0) & (apart < BLOCK)
    onehot = (bucket_of(apart)[:, None] == np.arange(BUCKETS)[None, :]) & shown[:, None]
    onehot = jnp.asarray(onehot.astype(np.float32))
    base = jnp.dot(bias_table * LOG2E, onehot.T, precision=lax.Precision.HIGHEST)
    base = jnp.where(jnp.asarray(shown)[None, :], base, negative_fill)
    (bias,) = call(
        bias_kernel,
        (1,),
        (),
        [(base, full(heads, SPAN))],
        [((heads, TILE, SPAN), f32, full(heads, TILE, SPAN))],
    )

    w_joined = jnp.concatenate([w_query, w_key, w_value], axis=1)
    def front(first, tok_a, tok_b, stacked):
        row = lambda cols: pl.BlockSpec((BLOCK, cols), lambda g: (first + g, 0))
        pos = lambda *tail: pl.BlockSpec((1,) + tail, lambda g: (first + g, 0, 0))
        return call(
            functools.partial(front_kernel, scale, heads),
            (2,),
            (),
            [
                (tok_a, full(BLOCK, width)),
                (tok_b, full(BLOCK, width)),
                (gain_attn[None, :], full(1, width)),
                (w_joined, full(width, 3 * lw)),
                (state_queries, full(NS, lw)),
            ],
            [
                ((rows_all, width), bf16, row(width)),
                ((rows_all, 3 * lw), bf16, row(3 * lw)),
                ((nb, NS, lw), f32, pos(NS, lw)),
                ((nb, NS, 128), f32, pos(NS, 128)),
            ],
            [] if stacked is None else [(array, n) for n, array in enumerate(stacked)],
            flops=4 * BLOCK * width * 3 * lw + 8 * NS * BLOCK * lw,
            nbytes=12 * BLOCK * width * 2,
            exps=2 * heads * NS * BLOCK,
        )

    stacked = front(0, tokens, tok1, None)
    tok2, *stacked = lax.optimization_barrier((tok2, *stacked))
    toks = [tokens, tok1, tok2, core(tok2)]
    cot1 = core(cotangent)
    cot2 = cross(hold(cotangent, tok2))
    stacked = front(2, toks[2], toks[3], stacked)
    normed_all, qkv, updates, lse_u = stacked

    place = (t_index ^ (nb - 1)) * BLOCK
    edge = along(lax.dynamic_slice(qkv, (place, lw), (BLOCK, 2 * lw)), 1)

    block_rows = (keeps[:, None] * gates[None, :])[:, None, :]
    before, total = call(
        chain_kernel,
        (1,),
        (t_pre,),
        [(updates, full(nb, NS, lw)), (block_rows, full(nb, 1, lw))],
        [((nb, NS, lw), f32, full(nb, NS, lw)), ((NS, lw), bf16, full(NS, lw))],
        flops=nb * NS * lw * 2,
        nbytes=nb * NS * lw * 8,
        hbm=(0,),
    )
    pair_flops = 2 * BLOCK * SPAN * lw

    def window(first, count, edge, stacked, weight):
        at = lambda col, back=0: pl.BlockSpec(
            (BLOCK, lw), lambda j, t: ((j + first - back) ^ t[0], col)
        )
        ids_at = lambda back: pl.BlockSpec((1, 1, BLOCK), lambda j, t: (j + first + 1 - back, 0, 0))
        blk = lambda *tail: pl.BlockSpec((1,) + tail, lambda j, t: (j + first, 0, 0))
        if edge is None:
            before_block = [(qkv, at(1, 1)), (qkv, at(2, 1))]
        else:
            before_block = [
                (edge, pl.BlockSpec((BLOCK, lw), lambda j, t: (0, 0))),
                (edge, pl.BlockSpec((BLOCK, lw), lambda j, t: (0, 1))),
            ]
        return call(
            functools.partial(window_kernel, scale, heads),
            (count,),
            (t_pre,),
            [(qkv, at(0)), (qkv, at(1)), (qkv, at(2))]
            + before_block
            + [
                (id_cols, pl.BlockSpec((BLOCK, 1), lambda j, t: (j + first, 0))),
                (id_rows, ids_at(1)),
                (id_rows, ids_at(0)),
                (bias, full(heads, TILE, SPAN)),
            ],
            [
                ((nb, BLOCK, lw), f32, blk(BLOCK, lw)),
                ((nb, BLOCK, 128), f32, blk(BLOCK, 128)),
            ],
            [] if stacked is None else [(array, n) for n, array in enumerate(stacked)],
            flops=count * 2 * pair_flops,
            nbytes=count * BLOCK * lw * 12,
            exps=count * heads * BLOCK * SPAN,
            weight=weight,
        )

    windows = window(1, nb - 1, None, None, WEIGHT)
    late_edge, total, *windows = lax.optimization_barrier((edge, total, *windows))
    totals = swap(total.reshape(groups, share, lw))
    acc, ml = window(0, 1, late_edge, windows, HEAVY)
    cot2 = hold(cot2, acc)
    cots = [hold(cotangent, acc), hold(cot1, acc), cot2, core(cot2)]
    gacts = [nt(cot, w_return).astype(bf16) for cot in cots]
    totals, gacts[0], gacts[1] = lax.optimization_barrier((totals, gacts[0], gacts[1]))
    (entries,) = call(
        scan_kernel,
        (1,),
        (s_pre,),
        [
            (totals, full(groups, share, lw)),
            (group_rows, full(groups, 1, lw)),
            (state_init, pl.BlockSpec((share, lw), lambda g, s: (s[0], 0))),
        ],
        [((groups, share, lw), bf16, full(groups, share, lw))],
        flops=NS * lw * 2,
        nbytes=NS * lw * 4,
    )
    entry = swap(entries).reshape(NS, lw)
    starts = [jnp.ones_like(gates)]
    for j in range(nb - 1):
        starts.append(starts[j] * (gates * keeps[j]))
    carry_rows = (jnp.stack(starts) * keeps[:, None])[:, None, :]
    keep_rows = jnp.broadcast_to(keeps[:, None, None], (nb, 1, lw))

    entry, *gacts = lax.optimization_barrier((entry, *gacts))

    def attend(high, stacked):
        blk = lambda *tail: pl.BlockSpec((1,) + tail, lambda g, t: (t[0] ^ (high - g), 0, 0))
        pos = lambda *tail: pl.BlockSpec((1,) + tail, lambda g, t: (high - g, 0, 0))
        return call(
            functools.partial(state_kernel, scale, heads),
            (2,),
            (t_pre,),
            [
                (qkv, pl.BlockSpec((BLOCK, lw), lambda g, t: (high - g, 0))),
                (entry, full(NS, lw)),
                (before, blk(NS, lw)),
                (carry_rows, blk(1, lw)),
                (keep_rows, blk(1, lw)),
                (acc, blk(BLOCK, lw)),
                (ml, blk(BLOCK, 128)),
                (w_output, full(lw, width)),
            ],
            [
                ((nb, BLOCK, lw), bf16, pos(BLOCK, lw)),
                ((nb, BLOCK, 128), f32, pos(BLOCK, 128)),
                ((nb, NS, lw), bf16, pos(NS, lw)),
                ((BLOCK, width), bf16, full(BLOCK, width)),
                ((BLOCK, width), bf16, full(BLOCK, width)),
            ],
            [] if stacked is None else [(array, n) for n, array in enumerate(stacked)],
            flops=8 * BLOCK * NS * lw + 4 * BLOCK * lw * width,
            nbytes=2 * BLOCK * (lw * 24 + width * 2),
            exps=2 * heads * BLOCK * NS,
        )

    *stacked, part3, part2 = attend(3, None)
    *stacked, part1, part0 = attend(1, stacked)
    mixed_all, stats_f, used_low = stacked

    def pair_sum(mine, theirs):
        return (mine.astype(f32) + theirs.astype(f32)).astype(bf16)

    sum2 = pair_sum(part2, core(part3))
    sum0 = pair_sum(part0, core(part1))
    far2 = cross(sum2)
    blk = lambda *tail: pl.BlockSpec((1,) + tail, lambda g, t: (t[0] ^ g, 0, 0))
    pos = lambda *tail: pl.BlockSpec((1,) + tail, lambda g, t: (g, 0, 0))
    (block_states,) = call(
        states_kernel,
        (nb,),
        (t_pre,),
        [
            (hold(entry, sum0), full(NS, lw)),
            (before, blk(NS, lw)),
            (carry_rows, blk(1, lw)),
            (keep_rows, blk(1, lw)),
            (gate_row, full(1, lw)),
            (updates, pos(NS, lw)),
        ],
        [((nb, NS, lw), f32, blk(NS, lw))],
        flops=nb * NS * lw * 4,
        nbytes=nb * NS * lw * 12,
        hbm=(0,),
    )
    far2 = hold(far2, block_states)
    far0 = cross(hold(sum0, far2))

    def norm_mlp(tok, mine, theirs):
        return call(
            norm_kernel,
            (2,),
            (),
            [(x, tall(width)) for x in (tok, mine, theirs)] + [(gain_mlp[None, :], full(1, width))],
            [((BLOCK, width), f32, tall(width)), ((BLOCK, width), bf16, tall(width))],
            flops=BLOCK * width * 8,
            nbytes=BLOCK * width * 12,
            hbm=(0,),
        )

    def feed(first, nm_a, nm_b, stacked):
        early_tile = lambda cols: pl.BlockSpec((half, cols), lambda g: (jnp.minimum(g, 1), 0))
        late_tile = lambda cols: pl.BlockSpec((half, cols), lambda g: (jnp.maximum(g - 2, 0), 0))
        return call(
            functools.partial(mlp_kernel, 2),
            (4,),
            (),
            [
                (nm_a, early_tile(width)),
                (nm_b, late_tile(width)),
                (gacts[first], early_tile(ff)),
                (gacts[first + 1], late_tile(ff)),
                (w_hidden, full(width, ff)),
            ],
            [
                ((rows_all, ff), bf16, pl.BlockSpec((half, ff), lambda g: (2 * first + g, 0))),
                ((rows_all, ff), bf16, pl.BlockSpec((half, ff), lambda g: (2 * first + g, 0))),
                ((BLOCK, width), bf16, early_tile(width)),
                ((BLOCK, width), bf16, late_tile(width)),
            ],
            [] if stacked is None else [(array, n) for n, array in enumerate(stacked)],
            flops=8 * BLOCK * width * ff,
            nbytes=2 * BLOCK * width * 10,
            exps=4 * BLOCK * ff,
        )

    residual0, nm0 = norm_mlp(toks[0], sum0, far2)
    nm1 = core(nm0)
    *stacked, back0, back1 = feed(0, nm0, nm1, None)
    far0, back1 = lax.optimization_barrier((far0, back1))
    back0 = pair_sum(back0, core(back1))
    home0 = cross(back0)
    residual2, nm2 = norm_mlp(toks[2], sum2, far0)
    nm3 = core(nm2)
    *stacked, back2, back3 = feed(2, nm2, nm3, stacked)
    hidden_all, gpre_all = stacked
    slab = width // groups
    cut = 256
    per = cut // slab

    nms = [nm0, nm1, nm2, nm3]
    *feed_grads, gain_mlp_part = call(
        functools.partial(feed_grads_kernel, nb),
        (width // cut,),
        (s_pre,),
        [(x, pl.BlockSpec((BLOCK, cut), lambda g, s: (0, g))) for x in nms + cots]
        + [
            (gpre_all, full(rows_all, ff)),
            (hidden_all, full(rows_all, ff)),
            (w_hidden, pl.BlockSpec((cut, ff), lambda g, s: (g, 0))),
        ],
        [
            ((groups // 2, slab, ff), bf16, pl.BlockSpec((per // 2, slab, ff), lambda g, s: (g, 0, 0))),
            ((groups // 2, slab, ff), bf16, pl.BlockSpec((per // 2, slab, ff), lambda g, s: (g, 0, 0))),
            ((width, ff), bf16, pl.BlockSpec((cut, ff), lambda g, s: (g, 0))),
            ((8, width), f32, pl.BlockSpec((8, cut), lambda g, s: (0, g))),
        ],
        flops=4 * rows_all * width * ff,
        nbytes=rows_all * width * 8,
        mib=48,
        pin=range(16),
        hbm=range(4),
    )

    flip = [(i, i ^ 1) for i in range(groups)]
    columns = [list(range(side, groups, 2)) for side in range(2)]

    def over_columns(value):
        return lax.psum_scatter(
            value, "seq", scatter_dimension=0, tiled=True, axis_index_groups=columns
        )

    home0, back3, *feed_grads = lax.optimization_barrier((home0, back3, *feed_grads))
    back2 = pair_sum(back2, core(back3))
    home2 = cross(back2)

    def norm_mlp_back(cot, mine, theirs, residual):
        return call(
            norm_back_kernel,
            (2,),
            (),
            [(x, tall(width)) for x in (cot, mine, theirs, residual)]
            + [(gain_mlp[None, :], full(1, width))],
            [((BLOCK, width), f32, tall(width)), ((BLOCK, width), bf16, tall(width))],
            flops=BLOCK * width * 12,
            nbytes=BLOCK * width * 16,
            hbm=(0,),
            pin=(0, 3),
        )

    hidden_got = lax.ppermute(feed_grads[1], "seq", flip)
    return_sum = over_columns(feed_grads[2])

    _, ga2 = norm_mlp_back(cots[2], back2, home0, residual2)
    ga3 = core(ga2)
    away, stay = call(
        return_kernel,
        (nb,),
        (),
        [
            (hidden_all, pl.BlockSpec((BLOCK, ff), lambda g: (nb - 1 - g, 0))),
            (w_return, full(ff, width)),
        ],
        [
            ((2 * BLOCK, width), bf16, pl.BlockSpec((BLOCK, width), lambda g: (g // 2, 0))),
            ((2 * BLOCK, width), bf16, pl.BlockSpec((BLOCK, width), lambda g: (jnp.maximum(g - 1, 0) // 2, 0))),
        ],
        flops=2 * rows_all * ff * width,
        nbytes=rows_all * (ff + width) * 2,
    )
    def attend_back(first, ga_a, ga_b, stacked):
        pos = lambda *tail: pl.BlockSpec((1,) + tail, lambda g: (first + g, 0, 0))
        return call(
            functools.partial(state_back_kernel, scale, heads),
            (2,),
            (),
            [
                (ga_a, full(BLOCK, width)),
                (ga_b, full(BLOCK, width)),
                (w_output, full(lw, width)),
                (qkv, pl.BlockSpec((BLOCK, lw), lambda g: (first + g, 0))),
                (mixed_all, pos(BLOCK, lw)),
                (used_low, pos(NS, lw)),
                (stats_f, pos(BLOCK, 128)),
            ],
            [
                ((nb, BLOCK, lw), bf16, pos(BLOCK, lw)),
                ((nb, BLOCK, 128), f32, pos(BLOCK, 128)),
                ((nb, BLOCK, lw), f32, pos(BLOCK, lw)),
                ((nb, NS, lw), f32, pos(NS, lw)),
            ],
            [] if stacked is None else [(array, n) for n, array in enumerate(stacked)],
            flops=4 * BLOCK * lw * width + 20 * BLOCK * NS * lw,
            nbytes=2 * BLOCK * (width * 4 + lw * 16),
            exps=2 * heads * BLOCK * NS,
        )

    stacked = attend_back(2, ga2, ga3, None)
    home2, away, stay, hidden_got, *stacked = lax.optimization_barrier(
        (home2, away, stay, hidden_got, *stacked)
    )
    hidden_sum = (feed_grads[0].astype(f32) + hidden_got.astype(f32)).astype(bf16)
    grad_residual, ga0 = norm_mlp_back(cots[0], back0, home2, residual0)
    ga1 = core(ga0)
    gas = [ga0, ga1, ga2, ga3]
    near_out = core(hold(away, home2))
    far_out = cross(pair_sum(stay[:BLOCK], near_out[:BLOCK]))
    hidden_sum, *stacked = lax.optimization_barrier((hidden_sum, *stacked))
    hidden_sum = over_columns(hidden_sum.reshape(width // 2, ff))
    stacked = attend_back(0, ga0, ga1, stacked)
    gm_all, stats_b, dq_state, direct = stacked

    (local_grad,) = call(
        chain_back_kernel,
        (1,),
        (t_pre,),
        [
            (direct, full(nb, NS, lw)),
            (gate_row, full(1, lw)),
            (keep_rows, full(nb, 1, lw)),
        ],
        [((NS, lw), bf16, full(NS, lw))],
        flops=nb * NS * lw * 2,
        nbytes=nb * NS * lw * 4,
    )
    local_grads = swap(local_grad.reshape(groups, share, lw))
    turn = lambda j: nb - 1 - j
    at = lambda col: pl.BlockSpec((BLOCK, lw), lambda j, t: (turn(j) ^ t[0], col))
    prev = lambda col: pl.BlockSpec(
        (BLOCK, lw), lambda j, t: (jnp.maximum(turn(j) - 1, 0) ^ t[0], col)
    )
    pos = lambda *tail: pl.BlockSpec((1,) + tail, lambda j, t: (turn(j) ^ t[0], 0, 0))
    dq, dk, dv, back_kv, bias_grad = call(
        functools.partial(window_back_kernel, scale, heads),
        (nb,),
        (t_pre,),
        [
            (qkv, at(0)),
            (qkv, at(1)),
            (qkv, at(2)),
            (qkv, prev(1)),
            (qkv, prev(2)),
            (edge, pl.BlockSpec((BLOCK, lw), lambda j, t: (0, 0))),
            (edge, pl.BlockSpec((BLOCK, lw), lambda j, t: (0, 1))),
            (id_cols, pl.BlockSpec((BLOCK, 1), lambda j, t: (turn(j), 0))),
            (id_rows, pl.BlockSpec((1, 1, BLOCK), lambda j, t: (turn(j), 0, 0))),
            (id_rows, pl.BlockSpec((1, 1, BLOCK), lambda j, t: (turn(j) + 1, 0, 0))),
            (bias, full(heads, TILE, SPAN)),
            (gm_all, pos(BLOCK, lw)),
            (stats_b, pos(BLOCK, 128)),
            (dq_state, pos(BLOCK, lw)),
        ],
        [
            ((rows_all, lw), bf16, pl.BlockSpec((BLOCK, lw), lambda j, t: (turn(j) ^ t[0], 0))),
            ((nb, BLOCK, lw), f32, pos(BLOCK, lw)),
            ((nb, BLOCK, lw), f32, pos(BLOCK, lw)),
            ((BLOCK, 2 * lw), bf16, full(BLOCK, 2 * lw)),
            ((heads, TILE, SPAN), f32, full(heads, TILE, SPAN)),
        ],
        scratch=[pltpu.VMEM((BLOCK, lw), bf16)] * 2 + [pltpu.VMEM((BLOCK, lw), f32)] * 4,
        flops=nb * 5 * pair_flops,
        nbytes=nb * BLOCK * lw * 24,
        exps=nb * heads * BLOCK * SPAN,
    )
    local_grads, dq, return_sum = lax.optimization_barrier((local_grads, dq, return_sum))
    odd = s_index & 1
    return_own = lax.dynamic_slice_in_dim(return_sum, odd * slab, slab, 0)
    return_other = lax.dynamic_slice_in_dim(return_sum, (1 - odd) * slab, slab, 0)
    return_got = lax.ppermute(return_other, "seq", flip)
    carries, grad_state = call(
        scan_back_kernel,
        (1,),
        (),
        [(local_grads, full(groups, share, lw)), (group_rows, full(groups, 1, lw))],
        [
            ((groups, share, lw), bf16, full(groups, share, lw)),
            ((share, lw), f32, full(share, lw)),
        ],
        flops=NS * lw * 2,
        nbytes=NS * lw * 4,
    )
    carried = swap(carries).reshape(NS, lw)

    next_kv = along(back_kv, -1)
    (bias_line,) = call(
        bias_sum_kernel,
        (1,),
        (),
        [(bias_grad, full(heads, TILE, SPAN))],
        [((heads, SPAN), f32, full(heads, SPAN))],
    )
    bias_local = jnp.dot(bias_line, onehot, precision=lax.Precision.HIGHEST)

    mid, row_part = call(
        functools.partial(query_grads_kernel, nb),
        (width // cut,),
        (),
        [(gas[r], pl.BlockSpec((BLOCK, cut), lambda g: (0, g))) for r in range(nb)]
        + [
            (mixed_all, full(nb, BLOCK, lw)),
            (normed_all, pl.BlockSpec((rows_all, cut), lambda g: (0, g))),
            (dq, full(rows_all, lw)),
            (w_query, pl.BlockSpec((cut, lw), lambda g: (g, 0))),
        ],
        [
            ((width, 2 * lw), bf16, pl.BlockSpec((cut, 2 * lw), lambda g: (g, 0))),
            ((8, width), f32, pl.BlockSpec((8, cut), lambda g: (0, g))),
        ],
        flops=4 * rows_all * width * lw,
        nbytes=rows_all * width * 4,
        mib=32,
        pin=range(16),
    )
    carried, mid, hidden_sum, return_got, *_ = lax.optimization_barrier(
        (carried, mid, hidden_sum, return_got, far_out, bias_local)
    )
    mid = swap(mid.reshape(groups, width // groups, 2 * lw))
    result = (
        residual0 + stay[BLOCK:].astype(f32) + near_out[BLOCK:].astype(f32) + far_out.astype(f32)
    ).astype(bf16)

    gu_all, gate_sum = call(
        carry_kernel,
        (1,),
        (t_pre,),
        [
            (carried, full(NS, lw)),
            (direct, full(nb, NS, lw)),
            (entry, full(NS, lw)),
            (before, full(nb, NS, lw)),
            (carry_rows, full(nb, 1, lw)),
            (keep_rows, full(nb, 1, lw)),
            (gate_row, full(1, lw)),
        ],
        [((nb, NS, lw), bf16, full(nb, NS, lw)), ((1, lw), f32, full(1, lw))],
        flops=nb * NS * lw * 8,
        nbytes=nb * NS * lw * 10,
    )
    def learn_back(high, gu_all, grad_sq, dkv):
        pos = lambda *tail: pl.BlockSpec((1,) + tail, lambda g, t: (high - g, 0, 0))
        row = lambda cols, col=0: pl.BlockSpec((BLOCK, cols), lambda g, t: (high - g, col))
        return call(
            functools.partial(update_back_kernel, scale, heads, high, nb - 1),
            (2,),
            (t_pre,),
            [
                (gu_all, pos(NS, lw)),
                (qkv, row(lw, 1)),
                (qkv, row(lw, 2)),
                (state_queries, full(NS, lw)),
                (lse_u, pos(NS, 128)),
                (updates, pos(NS, lw)),
                (dq, row(lw)),
                (dk, pos(BLOCK, lw)),
                (dv, pos(BLOCK, lw)),
                (next_kv, pl.BlockSpec((BLOCK, lw), lambda g, t: (0, 0))),
                (next_kv, pl.BlockSpec((BLOCK, lw), lambda g, t: (0, 1))),
                (w_joined, full(width, 3 * lw)),
                (grad_sq, full(NS, lw)),
            ],
            [
                ((rows_all, 2 * lw), bf16, row(2 * lw)),
                ((BLOCK, width), bf16, full(BLOCK, width)),
                ((BLOCK, width), bf16, full(BLOCK, width)),
                ((NS, lw), f32, full(NS, lw)),
            ],
            [] if dkv is None else [(dkv, 0)],
            flops=20 * NS * BLOCK * lw + 12 * BLOCK * lw * width,
            nbytes=2 * BLOCK * (lw * 30 + width * 2),
            exps=2 * heads * NS * BLOCK,
        )

    dkv, part3, part2, grad_sq = learn_back(3, gu_all, jnp.zeros((NS, lw), f32), None)
    far = pair_sum(part2, core(part3))
    gu_all = hold(gu_all, far)
    far = cross(far)
    dkv, part1, part0, grad_sq = learn_back(1, gu_all, grad_sq, dkv)
    near = core(part1)

    late, gain_attn_part = call(
        key_grads_kernel,
        (width // cut,),
        (),
        [
            (normed_all, pl.BlockSpec((rows_all, cut), lambda g: (0, g))),
            (dkv, full(rows_all, 2 * lw)),
            (w_key, pl.BlockSpec((cut, lw), lambda g: (g, 0))),
            (w_value, pl.BlockSpec((cut, lw), lambda g: (g, 0))),
            (grad_sq, pl.BlockSpec((per * share, lw), lambda g: (g, 0))),
            (row_part, pl.BlockSpec((8, cut), lambda g: (0, g))),
        ],
        [
            (
                (groups, slab + share // 2, 2 * lw),
                bf16,
                pl.BlockSpec((per, slab + share // 2, 2 * lw), lambda g: (g, 0, 0)),
            ),
            ((8, width), f32, pl.BlockSpec((8, cut), lambda g: (0, g))),
        ],
        flops=4 * rows_all * width * lw,
        nbytes=rows_all * width * 4,
        mib=32,
    )
    late = swap(hold(late, far))

    bias_full = lax.dynamic_update_slice(
        jnp.zeros((H, BUCKETS), f32), bias_local, (t_index * heads, 0)
    )
    gate_full = lax.dynamic_update_slice(
        jnp.zeros((D,), f32), gate_sum[0] * gates * (1.0 - gates), (t_index * lw,)
    )
    small = jnp.concatenate(
        [
            gain_attn_part[0] / gain_attn,
            gain_mlp_part[0] / gain_mlp,
            gate_full,
            bias_full.reshape(-1),
        ]
    ).reshape(-1, 128)
    small = hold(small, mid)
    small = small + core(small)
    small = small + cross(small)
    step = 1
    while step < groups:
        small = small + lax.ppermute(small, "seq", [(i, i ^ step) for i in range(groups)])
        step *= 2
    small = small.reshape(-1)

    (grad_tokens,) = call(
        final_kernel,
        (2,),
        (),
        [(x, tall(width)) for x in (tokens, part0, near, far, grad_residual)]
        + [(gain_attn[None, :], full(1, width))],
        [((BLOCK, width), f32, tall(width))],
        flops=BLOCK * width * 12,
        nbytes=BLOCK * width * 16,
        pin=(0, 4),
    )

    mid = jnp.sum(mid.astype(f32), axis=0)
    late = jnp.sum(late.astype(f32), axis=0)
    queries_sent = jnp.concatenate([late[slab:, :lw], late[slab:, lw:]])
    return (
        result,
        block_states,
        grad_tokens,
        grad_state,
        small[:D],
        mid[:, :lw],
        late[:slab, :lw],
        late[:slab, lw:],
        mid[:, lw:].T,
        small[3 * D :].reshape(H, BUCKETS),
        queries_sent,
        small[2 * D : 3 * D],
        small[D : 2 * D],
        hidden_sum.astype(f32),
        (return_own.astype(f32) + return_got.astype(f32)).T,
    )


def solution(mesh):
    return jax.shard_map(
        local,
        mesh=mesh,
        in_specs=(
            P(("seq", "tp"), None),
            P("seq"),
            P("seq"),
            P(None, "tp"),
            P(),
            P(None, "tp"),
            P(None, "tp"),
            P(None, "tp"),
            P("tp", None),
            P("tp", None),
            P(None, "tp"),
            P("tp"),
            P(),
            P(None, "tp"),
            P("tp", None),
            P(("seq", "tp"), None),
        ),
        out_specs=(
            P(("seq", "tp"), None),
            P("seq", None, "tp"),
            P(("seq", "tp"), None),
            P("seq", "tp"),
            P(),
            P("seq", "tp"),
            P("seq", "tp"),
            P("seq", "tp"),
            P("tp", "seq"),
            P(),
            P("seq", "tp"),
            P(),
            P(),
            P("seq", "tp"),
            P("tp", "seq"),
        ),
        check_vma=False,
    )
```

```python
import functools
import math

import jax
import jax.numpy as jnp
import numpy as np
from jax import lax
from jax.experimental import pallas as pl
from jax.experimental.pallas import tpu as pltpu
from jax.sharding import PartitionSpec as P

D = 1024
H = 8
NS = 512
BLOCK = 512
BUCKETS = 32
FAR = 128
TILE = 128
SPAN = BLOCK + TILE
HEAD = 128

eps = 1e-06
negative_fill = -1e30
LOG2E = math.log2(math.e)
WEIGHT = 0.05
HEAVY = 1.0
f32 = jnp.float32
bf16 = jnp.bfloat16


def nn(a, b):
    return lax.dot_general(a, b, (((1,), (0,)), ((), ())), preferred_element_type=f32)


def nt(a, b):
    return lax.dot_general(a, b, (((1,), (1,)), ((), ())), preferred_element_type=f32)


def tn(a, b):
    return lax.dot_general(a, b, (((0,), (0,)), ((), ())), preferred_element_type=f32)


def pinned(array):
    return pltpu.with_memory_space_constraint(array, pltpu.HBM)


def call(
    kernel, grid, prefetch, ins, outs, aliases=(), scratch=(), flops=0, nbytes=0, exps=0, mib=24,
    hbm=(), pin=(), weight=WEIGHT,
):
    any_spec = pl.BlockSpec(memory_space=pl.ANY)
    arrays = [
        pinned(array) if n in pin or array.ndim == 3 or array.shape[0] > D else array
        for n, (array, _) in enumerate(ins)
    ]
    arrays += [pinned(array) for array, _ in aliases]
    specs = [spec for _, spec in ins] + [any_spec for _ in aliases]
    first = len(prefetch) + len(ins)
    alias_map = {first + n: out for n, (_, out) in enumerate(aliases)}
    n_pre, n_in, n_alias = len(prefetch), len(ins), len(aliases)

    def body(*refs):
        kept = refs[: n_pre + n_in] + refs[n_pre + n_in + n_alias :]
        kernel(*kept)

    return pl.pallas_call(
        body,
        name=getattr(kernel, 'func', kernel).__name__,
        out_shape=[
            pltpu.HBM(shape, dtype)
            if len(shape) == 3 or shape[0] > D or n in hbm
            else jax.ShapeDtypeStruct(shape, dtype)
            for n, (shape, dtype, _) in enumerate(outs)
        ],
        grid_spec=pltpu.PrefetchScalarGridSpec(
            num_scalar_prefetch=n_pre,
            grid=grid,
            in_specs=specs,
            out_specs=[spec for _, _, spec in outs],
            scratch_shapes=list(scratch),
        ),
        input_output_aliases=alias_map,
        compiler_params=pltpu.CompilerParams(
            dimension_semantics=("arbitrary",) * len(grid), vmem_limit_bytes=mib * 1024 * 1024
        ),
        cost_estimate=pl.CostEstimate(
            flops=int(flops * weight),
            bytes_accessed=int(nbytes * weight),
            transcendentals=int(exps * weight),
        ),
    )(*prefetch, *arrays)


def lanes(*columns):
    rows = columns[0].shape[0]
    lane = lax.broadcasted_iota(jnp.int32, (rows, 128), 1)
    packed = jnp.broadcast_to(columns[0], (rows, 128))
    for n, column in enumerate(columns[1:], 1):
        packed = jnp.where(lane == n, column, packed)
    return packed


def pick(*columns):
    lane = lax.broadcasted_iota(jnp.int32, columns[0].shape, 1)
    packed = columns[0]
    for n, column in enumerate(columns[1:], 1):
        packed = jnp.where(lane == n, column, packed)
    return packed


def with_ones(values):
    return jnp.concatenate([values, jnp.ones((values.shape[0], HEAD), bf16)], axis=1)


def head_of(h):
    return slice(h * HEAD, (h + 1) * HEAD)


def bias_kernel(base_ref, out_ref):
    for h in range(out_ref.shape[0]):
        row = jnp.broadcast_to(base_ref[h : h + 1, :], (TILE, SPAN))
        out_ref[h] = pltpu.roll(row, 0, 1, stride=1, stride_axis=0)


def bias_sum_kernel(grad_ref, out_ref):
    rows = lax.broadcasted_iota(jnp.int32, (TILE, SPAN), 0)
    for h in range(grad_ref.shape[0]):
        value = grad_ref[h]
        step = 1
        while step < TILE:
            moved = pltpu.roll(value, SPAN - step, 1)
            value = jnp.where((rows & step) != 0, moved, value)
            step *= 2
        out_ref[h : h + 1, :] = jnp.sum(value, axis=0, keepdims=True)


def front_kernel(scale, heads, tok_a, tok_b, gain, w, sq, normed_out, qkv_out, u_out, lse_out):
    width = heads * HEAD
    first = pl.program_id(0) == 0
    rows = 256
    for i in range(BLOCK // rows):
        part = slice(i * rows, (i + 1) * rows)
        x = jnp.where(first, tok_a[part, :].astype(f32), tok_b[part, :].astype(f32))
        r = lax.rsqrt(jnp.mean(x * x, axis=-1, keepdims=True) + eps)
        n = (x * r * gain[...]).astype(bf16)
        normed_out[part, :] = n
        qkv_out[part, :] = nn(n, w[...]).astype(bf16)
    values = [
        with_ones(qkv_out[:, 2 * width + h * HEAD : 2 * width + (h + 1) * HEAD])
        for h in range(heads)
    ]
    for i in range(BLOCK // rows):
        part = slice(i * rows, (i + 1) * rows)
        stats = []
        for h in range(heads):
            k = qkv_out[:, width + h * HEAD : width + (h + 1) * HEAD]
            s = nt(sq[part, head_of(h)], k) * (scale * LOG2E)
            m = jnp.max(s, axis=1, keepdims=True)
            p = jnp.exp2(s - m)
            both = nn(p.astype(bf16), values[h])
            total = both[:, HEAD:]
            u_out[0, part, head_of(h)] = both[:, :HEAD] / total
            stats.append(m + jnp.log(total) * LOG2E)
        lse_out[0, part, :] = pick(*stats)


def masked(scale, h, raw, qid, kid, bias):
    return jnp.where(qid == kid, raw * (scale * LOG2E) + bias[h], negative_fill)


def window_kernel(scale, heads, t, q, kc, vc, kp, vp, qid, kid, bias, acc, ml, keys, values):
    keys[:BLOCK] = kp[...]
    keys[BLOCK:] = kc[...]
    values[:BLOCK] = vp[...]
    values[BLOCK:] = vc[...]

    def scores_of(i, h):
        part = slice(i * TILE, (i + 1) * TILE)
        return nt(q[part, head_of(h)], keys[i * TILE : i * TILE + SPAN, head_of(h)])

    work = [(i, h) for i in range(BLOCK // TILE) for h in range(heads)]
    ready = scores_of(*work[0])
    peaks, sums = [], []
    for n, (i, h) in enumerate(work):
        raw = ready
        if n + 1 < len(work):
            ready = scores_of(*work[n + 1])
        part = slice(i * TILE, (i + 1) * TILE)
        span = slice(i * TILE, i * TILE + SPAN)
        s = masked(scale, h, raw, qid[part, :], kid[0, :, span], bias)
        m = jnp.max(s, axis=1, keepdims=True)
        p = jnp.exp2(s - m)
        both = nn(p.astype(bf16), with_ones(values[span, head_of(h)]))
        acc[0, part, head_of(h)] = both[:, :HEAD]
        peaks.append(jnp.broadcast_to(m, (TILE, HEAD)))
        sums.append(both[:, HEAD:])
        if h == heads - 1:
            ml[0, part, :] = pick(*peaks, *sums)
            peaks, sums = [], []


def chain_kernel(t, updates, factors, before_out, total_out):
    state = jnp.zeros(total_out.shape, f32)
    for j in range(updates.shape[0]):
        before_out[j] = state
        state = factors[j] * state + updates[t[0] ^ j]
    total_out[...] = state.astype(bf16)


def scan_kernel(s, totals, factors, init, out):
    state = init[...]
    for g in range(totals.shape[0]):
        out[g] = state.astype(bf16)
        state = factors[g] * state + totals[g].astype(f32)


def chain_back_kernel(t, direct, gates, keep_rows, out):
    state = jnp.zeros(out.shape, f32)
    for j in reversed(range(direct.shape[0])):
        state = keep_rows[j] * (direct[t[0] ^ j] + gates[...] * state)
    out[...] = state.astype(bf16)


def scan_back_kernel(totals, factors, out, first_out):
    state = jnp.zeros(first_out.shape, f32)
    for g in reversed(range(totals.shape[0])):
        out[g] = state.astype(bf16)
        state = factors[g] * state + totals[g].astype(f32)
    first_out[...] = state


def carry_kernel(
    t, carried0, direct, entry, before, carry_rows, keep_rows, gates, gu_out, gate_out
):
    now = carried0[...].astype(f32)
    start = entry[...].astype(f32)
    total = jnp.zeros(gate_out.shape, f32)
    for j in reversed(range(direct.shape[0])):
        used = carry_rows[j] * start + keep_rows[j] * before[j]
        total = total + jnp.sum(now * used, axis=0, keepdims=True)
        gu_out[t[0] ^ j] = now.astype(bf16)
        now = keep_rows[j] * (direct[t[0] ^ j] + gates[...] * now)
    gate_out[...] = total


def state_kernel(
    scale, heads, t, q, entry, before, carry_row, keep_row, acc, ml, w,
    mixed_out, stats_out, used_out, first_out, second_out,
):
    used_out[0] = (carry_row[0] * entry[...].astype(f32) + keep_row[0] * before[0]).astype(bf16)
    values = [with_ones(used_out[0, :, head_of(h)]) for h in range(heads)]
    rows = 256
    for i in range(BLOCK // rows):
        part = slice(i * rows, (i + 1) * rows)
        stats = []
        for h in range(heads):
            m = ml[0, part, h : h + 1]
            l = ml[0, part, heads + h : heads + h + 1]
            s = nt(q[part, head_of(h)], used_out[0, :, head_of(h)]) * (scale * LOG2E)
            top = jnp.maximum(m, jnp.max(s, axis=1, keepdims=True))
            p = jnp.exp2(s - top)
            shrink = jnp.exp2(m - top)
            both = nn(p.astype(bf16), values[h])
            total = l * shrink + both[:, HEAD:]
            value = (acc[0, part, head_of(h)] * shrink + both[:, :HEAD]) / total
            mixed_out[0, part, head_of(h)] = value.astype(bf16)
            stats.append(top + jnp.log(total) * LOG2E)
        stats_out[0, part, :] = pick(*stats)
    result = nn(mixed_out[0], w[...]).astype(bf16)
    first = pl.program_id(0) == 0

    @pl.when(first)
    def _():
        first_out[...] = result

    @pl.when(jnp.logical_not(first))
    def _():
        second_out[...] = result


def states_kernel(t, entry, before, carry_row, keep_row, gates, u, next_out):
    used = carry_row[0] * entry[...].astype(f32) + keep_row[0] * before[0]
    next_out[0] = gates[...] * used + u[0]


def return_kernel(hidden, w, away_out, stay_out):
    even = pl.program_id(0) % 2 == 0

    @pl.when(even)
    def _():
        away_out[...] = nn(hidden[...], w[...]).astype(bf16)

    @pl.when(jnp.logical_not(even))
    def _():
        stay_out[...] = nn(hidden[...], w[...]).astype(bf16)


def norm_kernel(tok, mine, theirs, gain, residual_out, nm_out):
    residual = tok[...].astype(f32) + (mine[...].astype(f32) + theirs[...].astype(f32))
    residual_out[...] = residual
    inverse = lax.rsqrt(jnp.mean(residual * residual, axis=-1, keepdims=True) + eps)
    nm_out[...] = (residual * inverse * gain[...]).astype(bf16)


def norm_back_kernel(cot, mine, theirs, residual, gain, grad_out, low_out):
    r = residual[...]
    inverse = lax.rsqrt(jnp.mean(r * r, axis=-1, keepdims=True) + eps)
    scaled = r * inverse
    grad = (mine[...].astype(f32) + theirs[...].astype(f32)) * gain[...]
    inner = jnp.mean(grad * scaled, axis=-1, keepdims=True)
    result = cot[...].astype(f32) + inverse * (grad - scaled * inner)
    grad_out[...] = result
    low_out[...] = result.astype(bf16)


def final_kernel(tok, mine, near, far, residual_grad, gain, out):
    x = tok[...].astype(f32)
    inverse = lax.rsqrt(jnp.mean(x * x, axis=-1, keepdims=True) + eps)
    scaled = x * inverse
    grad = mine[...].astype(f32) + near[...].astype(f32) + far[...].astype(f32)
    grad = grad * gain[...]
    inner = jnp.mean(grad * scaled, axis=-1, keepdims=True)
    out[...] = residual_grad[...] + inverse * (grad - scaled * inner)


def row_sums(value):
    sums = jnp.broadcast_to(jnp.sum(value, axis=1, keepdims=True), (value.shape[0], HEAD))
    return sums.T[:8]


def feed_grads_kernel(n, s, *refs):
    nms, cots = refs[:n], refs[n : 2 * n]
    gpre, hidden, w, kept_out, sent_out, return_out, gain_out = refs[2 * n :]
    odd = s[0] % 2 == 1
    rows = nms[0].shape[0]
    ff = w.shape[1]
    for which, left, right in ((0, nms, gpre), (1, cots, hidden)):
        total = None
        for r in range(n):
            piece = tn(left[r][...], right[r * rows : (r + 1) * rows, :])
            total = piece if total is None else total + piece
        low = total.astype(bf16)
        if which == 0:
            slab = kept_out.shape[1]
            for g in range(kept_out.shape[0]):
                even_rows = low[2 * g * slab : (2 * g + 1) * slab]
                odd_rows = low[(2 * g + 1) * slab : (2 * g + 2) * slab]
                kept_out[g] = jnp.where(odd, odd_rows, even_rows)
                sent_out[g] = jnp.where(odd, even_rows, odd_rows)
        else:
            return_out[...] = low
        if which == 0:
            gain_out[...] = row_sums(total * w[...].astype(f32))


def query_grads_kernel(n, *refs):
    gas = refs[:n]
    mixed, normed, dq, w, out, row_out = refs[n:]
    rows, lw = gas[0].shape[0], dq.shape[1]
    total = None
    for r in range(n):
        piece = tn(gas[r][...], mixed[r])
        total = piece if total is None else total + piece
    out[:, lw:] = total.astype(bf16)
    grad = tn(normed[...], dq[...])
    out[:, :lw] = grad.astype(bf16)
    row_out[...] = row_sums(grad * w[...].astype(f32))


def key_grads_kernel(normed, dkv, wk, wv, dsq, row, out, row_out):
    grad = tn(normed[...], dkv[...])
    rows, lw = grad.shape[0], wk.shape[1]
    slab = rows // out.shape[0]
    part = dsq.shape[0] // out.shape[0] // 2
    low = grad.astype(bf16)
    for g in range(out.shape[0]):
        out[g, :slab] = low[g * slab : (g + 1) * slab]
        out[g, slab:, :lw] = dsq[2 * g * part : (2 * g + 1) * part].astype(bf16)
        out[g, slab:, lw:] = dsq[(2 * g + 1) * part : (2 * g + 2) * part].astype(bf16)
    both = jnp.concatenate([wk[...].astype(f32), wv[...].astype(f32)], axis=1)
    row_out[...] = row[...] + row_sums(grad * both)


def mlp_kernel(steps, nm_a, nm_b, gact_a, gact_b, w, hidden_out, gpre_out, first_out, second_out):
    first = pl.program_id(0) < steps
    cols = 256
    x = jnp.where(first, nm_a[...], nm_b[...])
    for c in range(w.shape[1] // cols):
        cut = slice(c * cols, (c + 1) * cols)
        pre = nn(x, w[:, cut])
        cumulative = 0.5 * (1.0 + lax.erf(pre * (1.0 / math.sqrt(2.0))))
        density = jnp.exp2(pre * pre * (-0.5 * LOG2E)) * (1.0 / math.sqrt(2.0 * math.pi))
        hidden_out[:, cut] = (pre * cumulative).astype(bf16)
        gact = jnp.where(first, gact_a[:, cut].astype(f32), gact_b[:, cut].astype(f32))
        gpre_out[:, cut] = (gact * (cumulative + pre * density)).astype(bf16)
    result = nt(gpre_out[...], w[...]).astype(bf16)

    @pl.when(first)
    def _():
        first_out[...] = result

    @pl.when(jnp.logical_not(first))
    def _():
        second_out[...] = result


def state_back_kernel(
    scale, heads, ga_a, ga_b, w, q, mixed, used, stats, gm_out, stats_out, dq_out, direct_out
):
    first = pl.program_id(0) == 0
    gm_out[0] = nt(jnp.where(first, ga_a[...], ga_b[...]), w[...]).astype(bf16)
    logs, deltas = [], []
    for h in range(heads):
        hs = head_of(h)
        gm = gm_out[0, :, hs]
        qt = q[:, hs]
        state = used[0, :, hs]
        delta = jnp.sum(gm.astype(f32) * mixed[0, :, hs].astype(f32), axis=1, keepdims=True)
        lse = stats[0, :, h : h + 1]
        p = jnp.exp2(nt(qt, state) * (scale * LOG2E) - lse)
        ds = (p * (nt(gm, state) - delta)).astype(bf16)
        dq_out[0, :, hs] = nn(ds, state) * scale
        direct_out[0, :, hs] = tn(ds, qt) * scale + tn(p.astype(bf16), gm)
        logs.append(lse)
        deltas.append(delta)
    stats_out[0] = lanes(*logs, *deltas)


def window_back_kernel(
    scale, heads, t, q, kc, vc, kb, vb, hk, hv, qid, kid, bias, gm, stats, dqs,
    dq_out, dk_out, dv_out, edge_out, grad_bias, keys, values, dkeys, dvalues,
):
    step = pl.program_id(0)
    last = pl.num_programs(0) - 1

    @pl.when(step == last)
    def _():
        keys[:BLOCK] = hk[...]
        values[:BLOCK] = hv[...]

    @pl.when(step != last)
    def _():
        keys[:BLOCK] = kb[...]
        values[:BLOCK] = vb[...]

    keys[BLOCK:] = kc[...]
    values[BLOCK:] = vc[...]

    @pl.when(step == 0)
    def _():
        dkeys[...] = jnp.zeros_like(dkeys)
        dvalues[...] = jnp.zeros_like(dvalues)
        grad_bias[...] = jnp.zeros_like(grad_bias)

    @pl.when(step != 0)
    def _():
        for total in (dkeys, dvalues):
            total[BLOCK:] = total[:BLOCK]
            total[:BLOCK] = jnp.zeros((BLOCK, total.shape[1]), f32)

    def scores_of(i, h):
        part = slice(i * TILE, (i + 1) * TILE)
        span = slice(i * TILE, i * TILE + SPAN)
        hs = head_of(h)
        return nt(q[part, hs], keys[span, hs]), nt(gm[0, part, hs], values[span, hs])

    work = [(i, h) for i in range(BLOCK // TILE) for h in range(heads)]
    ready = scores_of(*work[0])
    for n, (i, h) in enumerate(work):
        raw, grad_p = ready
        if n + 1 < len(work):
            ready = scores_of(*work[n + 1])
        part = slice(i * TILE, (i + 1) * TILE)
        span = slice(i * TILE, i * TILE + SPAN)
        hs = head_of(h)
        qt = q[part, hs]
        g = gm[0, part, hs]
        lse = stats[0, part, h : h + 1]
        delta = stats[0, part, heads + h : heads + h + 1]
        p = jnp.exp2(masked(scale, h, raw, qid[part, :], kid[0, :, span], bias) - lse)
        ds = p * (grad_p - delta)
        low = ds.astype(bf16)
        zero = jnp.zeros_like(qt)
        sides = jnp.concatenate(
            [jnp.concatenate([qt, zero], axis=1), jnp.concatenate([zero, g], axis=1)]
        )
        both = tn(jnp.concatenate([low, p.astype(bf16)]), sides)
        dq = nn(low, keys[span, hs]) * scale + dqs[0, part, hs]
        grad_bias[h] += ds
        dq_out[part, hs] = dq.astype(bf16)
        dkeys[span, hs] += both[:, :HEAD] * scale
        dvalues[span, hs] += both[:, HEAD:]
    dk_out[0] = dkeys[BLOCK:]
    dv_out[0] = dvalues[BLOCK:]

    @pl.when(step == last)
    def _():
        width = heads * HEAD
        edge_out[:, :width] = dkeys[:BLOCK].astype(bf16)
        edge_out[:, width:] = dvalues[:BLOCK].astype(bf16)


def update_back_kernel(
    scale, heads, high, last, t, gu_all, k, v, sq, lse_u, u, dq, dk, dv, hk, hv, w, dsq_in,
    dkv_out, first_out, second_out, dsq_out,
):
    width = heads * HEAD
    step = pl.program_id(0)
    edge = jnp.where((t[0] ^ (high - step)) == last, 1.0, 0.0)

    @pl.when(step == 0)
    def _():
        dsq_out[...] = dsq_in[...]

    for h in range(heads):
        hs = head_of(h)
        gu = gu_all[0, :, hs]
        sqh = sq[:, hs]
        kh = k[:, hs]
        delta = jnp.sum(gu.astype(f32) * u[0, :, hs], axis=1, keepdims=True)
        p = jnp.exp2(nt(sqh, kh) * (scale * LOG2E) - lse_u[0, :, h : h + 1])
        ds = (p * (nt(gu, v[:, hs]) - delta)).astype(bf16)
        dsq_out[:, hs] += nn(ds, kh) * scale
        dkh = dk[0, :, hs] + tn(ds, sqh) * scale + edge * hk[:, hs].astype(f32)
        dvh = dv[0, :, hs] + tn(p.astype(bf16), gu) + edge * hv[:, hs].astype(f32)
        dkv_out[:, hs] = dkh.astype(bf16)
        dkv_out[:, width + h * HEAD : width + (h + 1) * HEAD] = dvh.astype(bf16)
    part = nt(dq[...], w[:, :width]) + nt(dkv_out[...], w[:, width:])
    result = part.astype(bf16)

    @pl.when(step == 0)
    def _():
        first_out[...] = result

    @pl.when(step != 0)
    def _():
        second_out[...] = result


def bucket_of(distance):
    half = BUCKETS // 2
    limits = [math.ceil(half * (FAR / half) ** (level / half)) for level in range(1, half)]
    clipped = np.maximum(distance, 0)
    extra = sum((clipped >= limit).astype(np.int32) for limit in limits)
    return np.where(clipped < half, clipped, half + extra)


def local(
    tokens,
    doc_flags,
    reset_flags,
    state_init,
    gain_attn,
    w_query,
    w_key,
    w_value,
    w_output,
    bias_table,
    state_queries,
    gate_logits,
    gain_mlp,
    w_hidden,
    w_return,
    cotangent,
):
    heads = bias_table.shape[0]
    lw = w_query.shape[1]
    width = tokens.shape[1]
    nb = reset_flags.shape[0]
    ff = w_hidden.shape[1]
    scale = 1.0 / math.sqrt(HEAD)
    groups = lax.axis_size("seq")
    s_index = lax.axis_index("seq")
    t_index = lax.axis_index("tp")
    t_pre = t_index.astype(jnp.int32)[None]
    s_pre = s_index.astype(jnp.int32)[None]
    rows_all = nb * BLOCK

    def core(value):
        return lax.ppermute(value, "tp", [(i, i ^ 1) for i in range(nb)])

    def cross(value):
        return lax.ppermute(value, "tp", [(i, i ^ 2) for i in range(nb)])

    def along(value, step):
        pairs = [(i, i + step) for i in range(groups) if 0 <= i + step < groups]
        return lax.ppermute(value, "seq", pairs)

    def swap(value):
        return lax.all_to_all(value, "seq", 0, 0, tiled=True)

    def hold(value, *others):
        return lax.optimization_barrier((value, *others))[0]

    full = lambda *shape: pl.BlockSpec(shape, lambda *_: (0,) * len(shape))
    half = BLOCK // 2
    tall = lambda *tail: pl.BlockSpec((half,) + tail, lambda g, *_: (g, 0))
    share = NS // groups

    tok2 = cross(tokens)
    tok1 = core(tokens)

    gates = jax.nn.sigmoid(gate_logits)
    keeps = (1 - reset_flags).astype(f32)
    gate_row = gates[None, :]
    gate_group = gates
    for _ in range(nb - 1):
        gate_group = gate_group * gates
    apart = BLOCK - np.arange(SPAN)
    shown = (apart >= 0) & (apart < BLOCK)
    onehot = (bucket_of(apart)[:, None] == np.arange(BUCKETS)[None, :]) & shown[:, None]
    onehot = jnp.asarray(onehot.astype(np.float32))
    base = jnp.dot(bias_table * LOG2E, onehot.T, precision=lax.Precision.HIGHEST)
    base = jnp.where(jnp.asarray(shown)[None, :], base, negative_fill)
    (bias,) = call(
        bias_kernel,
        (1,),
        (),
        [(base, full(heads, SPAN))],
        [((heads, TILE, SPAN), f32, full(heads, TILE, SPAN))],
    )

    w_joined = jnp.concatenate([w_query, w_key, w_value], axis=1)
    def front(first, tok_a, tok_b, stacked):
        row = lambda cols: pl.BlockSpec((BLOCK, cols), lambda g: (first + g, 0))
        pos = lambda *tail: pl.BlockSpec((1,) + tail, lambda g: (first + g, 0, 0))
        return call(
            functools.partial(front_kernel, scale, heads),
            (2,),
            (),
            [
                (tok_a, full(BLOCK, width)),
                (tok_b, full(BLOCK, width)),
                (gain_attn[None, :], full(1, width)),
                (w_joined, full(width, 3 * lw)),
                (state_queries, full(NS, lw)),
            ],
            [
                ((rows_all, width), bf16, row(width)),
                ((rows_all, 3 * lw), bf16, row(3 * lw)),
                ((nb, NS, lw), f32, pos(NS, lw)),
                ((nb, NS, 128), f32, pos(NS, 128)),
            ],
            [] if stacked is None else [(array, n) for n, array in enumerate(stacked)],
            flops=4 * BLOCK * width * 3 * lw + 8 * NS * BLOCK * lw,
            nbytes=12 * BLOCK * width * 2,
            exps=2 * heads * NS * BLOCK,
        )

    starts = [jnp.ones_like(gates)]
    for j in range(nb - 1):
        starts.append(starts[j] * (gates * keeps[j]))
    carry_rows = (jnp.stack(starts) * keeps[:, None])[:, None, :]
    keep_rows = jnp.broadcast_to(keeps[:, None, None], (nb, 1, lw))
    block_rows = (keeps[:, None] * gates[None, :])[:, None, :]
    stacked = front(0, tokens, tok1, None)
    reset_sent, flags_sent, *stacked = lax.optimization_barrier((reset_flags, doc_flags, *stacked))
    every = swap(jnp.broadcast_to(reset_sent.reshape(1, nb), (groups, nb)))
    flag_prev = along(flags_sent[rows_all - BLOCK :], 1)
    tok2, bias, every, flag_prev, *stacked = lax.optimization_barrier(
        (tok2, bias, every, flag_prev, *stacked)
    )
    toks = [tokens, tok1, tok2, core(tok2)]
    cot1 = core(cotangent)
    stacked = list(front(2, toks[2], toks[3], stacked))
    every, flag_prev, *stacked = lax.optimization_barrier((every, flag_prev, *stacked))
    group_keep = jnp.prod((1 - every).astype(f32), axis=1)

    group_rows = (group_keep[:, None] * gate_group[None, :])[:, None, :]

    ids = jnp.cumsum(jnp.concatenate([flag_prev, doc_flags]))
    ids = jnp.where((jnp.arange(rows_all + BLOCK) < BLOCK) & (s_index == 0), -1, ids)
    id_rows = ids.reshape(nb + 1, 1, BLOCK)
    id_rows = jnp.concatenate([id_rows[:-1], id_rows[1:]], axis=2)
    id_cols = ids[BLOCK:].reshape(rows_all, 1)
    cot2, stacked[0] = lax.optimization_barrier((cotangent, stacked[0]))
    cot2 = cross(cot2)
    normed_all, qkv, updates, lse_u = stacked

    place = (t_index ^ (nb - 1)) * BLOCK
    edge = along(lax.dynamic_slice(qkv, (place, lw), (BLOCK, 2 * lw)), 1)

    before, total = call(
        chain_kernel,
        (1,),
        (t_pre,),
        [(updates, full(nb, NS, lw)), (block_rows, full(nb, 1, lw))],
        [((nb, NS, lw), f32, full(nb, NS, lw)), ((NS, lw), bf16, full(NS, lw))],
        flops=nb * NS * lw * 2,
        nbytes=nb * NS * lw * 8,
        hbm=(0,),
    )
    pair_flops = 2 * BLOCK * SPAN * lw

    def window(first, count, edge, stacked, weight):
        at = lambda col, back=0: pl.BlockSpec(
            (BLOCK, lw), lambda j, t: ((j + first - back) ^ t[0], col)
        )
        blk = lambda *tail: pl.BlockSpec((1,) + tail, lambda j, t: (j + first, 0, 0))
        if edge is None:
            before_block = [(qkv, at(1, 1)), (qkv, at(2, 1))]
        else:
            before_block = [
                (edge, pl.BlockSpec((BLOCK, lw), lambda j, t: (0, 0))),
                (edge, pl.BlockSpec((BLOCK, lw), lambda j, t: (0, 1))),
            ]
        return call(
            functools.partial(window_kernel, scale, heads),
            (count,),
            (t_pre,),
            [(qkv, at(0)), (qkv, at(1)), (qkv, at(2))]
            + before_block
            + [
                (id_cols, pl.BlockSpec((BLOCK, 1), lambda j, t: (j + first, 0))),
                (id_rows, pl.BlockSpec((1, 1, 2 * BLOCK), lambda j, t: (j + first, 0, 0))),
                (bias, full(heads, TILE, SPAN)),
            ],
            [
                ((nb, BLOCK, lw), f32, blk(BLOCK, lw)),
                ((nb, BLOCK, 128), f32, blk(BLOCK, 128)),
            ],
            [] if stacked is None else [(array, n) for n, array in enumerate(stacked)],
            flops=count * 2 * pair_flops,
            nbytes=count * BLOCK * lw * 12,
            exps=count * heads * BLOCK * SPAN,
            scratch=[pltpu.VMEM((2 * BLOCK, lw), bf16)] * 2,
            weight=weight,
        )

    windows = window(1, nb - 1, None, None, WEIGHT)
    late_edge, total, *windows = lax.optimization_barrier((edge, total, *windows))
    totals = swap(total.reshape(groups, share, lw))
    acc, ml = window(0, 1, late_edge, windows, HEAVY)
    cot2 = hold(cot2, acc)
    cots = [hold(cotangent, acc), hold(cot1, acc), cot2, core(cot2)]
    gacts = [nt(cot, w_return).astype(bf16) for cot in cots]
    totals, gacts[0], gacts[1] = lax.optimization_barrier((totals, gacts[0], gacts[1]))
    (entries,) = call(
        scan_kernel,
        (1,),
        (s_pre,),
        [
            (totals, full(groups, share, lw)),
            (group_rows, full(groups, 1, lw)),
            (state_init, pl.BlockSpec((share, lw), lambda g, s: (s[0], 0))),
        ],
        [((groups, share, lw), bf16, full(groups, share, lw))],
        flops=NS * lw * 2,
        nbytes=NS * lw * 4,
    )
    entry = swap(entries).reshape(NS, lw)

    entry, *gacts = lax.optimization_barrier((entry, *gacts))

    def attend(high, stacked):
        blk = lambda *tail: pl.BlockSpec((1,) + tail, lambda g, t: (t[0] ^ (high - g), 0, 0))
        pos = lambda *tail: pl.BlockSpec((1,) + tail, lambda g, t: (high - g, 0, 0))
        return call(
            functools.partial(state_kernel, scale, heads),
            (2,),
            (t_pre,),
            [
                (qkv, pl.BlockSpec((BLOCK, lw), lambda g, t: (high - g, 0))),
                (entry, full(NS, lw)),
                (before, blk(NS, lw)),
                (carry_rows, blk(1, lw)),
                (keep_rows, blk(1, lw)),
                (acc, blk(BLOCK, lw)),
                (ml, blk(BLOCK, 128)),
                (w_output, full(lw, width)),
            ],
            [
                ((nb, BLOCK, lw), bf16, pos(BLOCK, lw)),
                ((nb, BLOCK, 128), f32, pos(BLOCK, 128)),
                ((nb, NS, lw), bf16, pos(NS, lw)),
                ((BLOCK, width), bf16, full(BLOCK, width)),
                ((BLOCK, width), bf16, full(BLOCK, width)),
            ],
            [] if stacked is None else [(array, n) for n, array in enumerate(stacked)],
            flops=8 * BLOCK * NS * lw + 4 * BLOCK * lw * width,
            nbytes=2 * BLOCK * (lw * 24 + width * 2),
            exps=2 * heads * BLOCK * NS,
        )

    *stacked, part3, part2 = attend(3, None)
    *stacked, part1, part0 = attend(1, stacked)
    mixed_all, stats_f, used_low = stacked

    def pair_sum(mine, theirs):
        return (mine.astype(f32) + theirs.astype(f32)).astype(bf16)

    sum2 = pair_sum(part2, core(part3))
    sum0 = pair_sum(part0, core(part1))
    far2 = cross(sum2)
    blk = lambda *tail: pl.BlockSpec((1,) + tail, lambda g, t: (t[0] ^ g, 0, 0))
    pos = lambda *tail: pl.BlockSpec((1,) + tail, lambda g, t: (g, 0, 0))
    (block_states,) = call(
        states_kernel,
        (nb,),
        (t_pre,),
        [
            (hold(entry, sum0), full(NS, lw)),
            (before, blk(NS, lw)),
            (carry_rows, blk(1, lw)),
            (keep_rows, blk(1, lw)),
            (gate_row, full(1, lw)),
            (updates, pos(NS, lw)),
        ],
        [((nb, NS, lw), f32, blk(NS, lw))],
        flops=nb * NS * lw * 4,
        nbytes=nb * NS * lw * 12,
        hbm=(0,),
    )
    far2 = hold(far2, block_states)
    far0 = cross(hold(sum0, far2))

    def norm_mlp(tok, mine, theirs):
        return call(
            norm_kernel,
            (2,),
            (),
            [(x, tall(width)) for x in (tok, mine, theirs)] + [(gain_mlp[None, :], full(1, width))],
            [((BLOCK, width), f32, tall(width)), ((BLOCK, width), bf16, tall(width))],
            flops=BLOCK * width * 8,
            nbytes=BLOCK * width * 12,
            hbm=(0,),
        )

    def feed(first, nm_a, nm_b, stacked):
        early_tile = lambda cols: pl.BlockSpec((half, cols), lambda g: (jnp.minimum(g, 1), 0))
        late_tile = lambda cols: pl.BlockSpec((half, cols), lambda g: (jnp.maximum(g - 2, 0), 0))
        return call(
            functools.partial(mlp_kernel, 2),
            (4,),
            (),
            [
                (nm_a, early_tile(width)),
                (nm_b, late_tile(width)),
                (gacts[first], early_tile(ff)),
                (gacts[first + 1], late_tile(ff)),
                (w_hidden, full(width, ff)),
            ],
            [
                ((rows_all, ff), bf16, pl.BlockSpec((half, ff), lambda g: (2 * first + g, 0))),
                ((rows_all, ff), bf16, pl.BlockSpec((half, ff), lambda g: (2 * first + g, 0))),
                ((BLOCK, width), bf16, early_tile(width)),
                ((BLOCK, width), bf16, late_tile(width)),
            ],
            [] if stacked is None else [(array, n) for n, array in enumerate(stacked)],
            flops=8 * BLOCK * width * ff,
            nbytes=2 * BLOCK * width * 10,
            exps=4 * BLOCK * ff,
        )

    residual0, nm0 = norm_mlp(toks[0], sum0, far2)
    nm1 = core(nm0)
    *stacked, back0, back1 = feed(0, nm0, nm1, None)
    far0, back1 = lax.optimization_barrier((far0, back1))
    back0 = pair_sum(back0, core(back1))
    home0 = cross(back0)
    residual2, nm2 = norm_mlp(toks[2], sum2, far0)
    nm3 = core(nm2)
    *stacked, back2, back3 = feed(2, nm2, nm3, stacked)
    hidden_all, gpre_all = stacked
    slab = width // groups
    cut = 256
    per = cut // slab

    nms = [nm0, nm1, nm2, nm3]
    *feed_grads, gain_mlp_part = call(
        functools.partial(feed_grads_kernel, nb),
        (width // cut,),
        (s_pre,),
        [(x, pl.BlockSpec((BLOCK, cut), lambda g, s: (0, g))) for x in nms + cots]
        + [
            (gpre_all, full(rows_all, ff)),
            (hidden_all, full(rows_all, ff)),
            (w_hidden, pl.BlockSpec((cut, ff), lambda g, s: (g, 0))),
        ],
        [
            ((groups // 2, slab, ff), bf16, pl.BlockSpec((per // 2, slab, ff), lambda g, s: (g, 0, 0))),
            ((groups // 2, slab, ff), bf16, pl.BlockSpec((per // 2, slab, ff), lambda g, s: (g, 0, 0))),
            ((width, ff), bf16, pl.BlockSpec((cut, ff), lambda g, s: (g, 0))),
            ((8, width), f32, pl.BlockSpec((8, cut), lambda g, s: (0, g))),
        ],
        flops=4 * rows_all * width * ff,
        nbytes=rows_all * width * 8,
        mib=48,
        pin=range(16),
        hbm=range(4),
    )

    flip = [(i, i ^ 1) for i in range(groups)]
    columns = [list(range(side, groups, 2)) for side in range(2)]

    def over_columns(value):
        return lax.psum_scatter(
            value, "seq", scatter_dimension=0, tiled=True, axis_index_groups=columns
        )

    home0, back3, *feed_grads = lax.optimization_barrier((home0, back3, *feed_grads))
    back2 = pair_sum(back2, core(back3))
    home2 = cross(back2)

    def norm_mlp_back(cot, mine, theirs, residual):
        return call(
            norm_back_kernel,
            (2,),
            (),
            [(x, tall(width)) for x in (cot, mine, theirs, residual)]
            + [(gain_mlp[None, :], full(1, width))],
            [((BLOCK, width), f32, tall(width)), ((BLOCK, width), bf16, tall(width))],
            flops=BLOCK * width * 12,
            nbytes=BLOCK * width * 16,
            hbm=(0,),
            pin=(0, 3),
        )

    hidden_got = lax.ppermute(feed_grads[1], "seq", flip)
    return_sum = over_columns(feed_grads[2])

    _, ga2 = norm_mlp_back(cots[2], back2, home0, residual2)
    ga3 = core(ga2)
    away, stay = call(
        return_kernel,
        (nb,),
        (),
        [
            (hidden_all, pl.BlockSpec((BLOCK, ff), lambda g: (nb - 1 - g, 0))),
            (w_return, full(ff, width)),
        ],
        [
            ((2 * BLOCK, width), bf16, pl.BlockSpec((BLOCK, width), lambda g: (g // 2, 0))),
            ((2 * BLOCK, width), bf16, pl.BlockSpec((BLOCK, width), lambda g: (jnp.maximum(g - 1, 0) // 2, 0))),
        ],
        flops=2 * rows_all * ff * width,
        nbytes=rows_all * (ff + width) * 2,
    )
    def attend_back(first, ga_a, ga_b, stacked):
        pos = lambda *tail: pl.BlockSpec((1,) + tail, lambda g: (first + g, 0, 0))
        return call(
            functools.partial(state_back_kernel, scale, heads),
            (2,),
            (),
            [
                (ga_a, full(BLOCK, width)),
                (ga_b, full(BLOCK, width)),
                (w_output, full(lw, width)),
                (qkv, pl.BlockSpec((BLOCK, lw), lambda g: (first + g, 0))),
                (mixed_all, pos(BLOCK, lw)),
                (used_low, pos(NS, lw)),
                (stats_f, pos(BLOCK, 128)),
            ],
            [
                ((nb, BLOCK, lw), bf16, pos(BLOCK, lw)),
                ((nb, BLOCK, 128), f32, pos(BLOCK, 128)),
                ((nb, BLOCK, lw), f32, pos(BLOCK, lw)),
                ((nb, NS, lw), f32, pos(NS, lw)),
            ],
            [] if stacked is None else [(array, n) for n, array in enumerate(stacked)],
            flops=4 * BLOCK * lw * width + 20 * BLOCK * NS * lw,
            nbytes=2 * BLOCK * (width * 4 + lw * 16),
            exps=2 * heads * BLOCK * NS,
        )

    stacked = attend_back(2, ga2, ga3, None)
    home2, away, stay, hidden_got, *stacked = lax.optimization_barrier(
        (home2, away, stay, hidden_got, *stacked)
    )
    hidden_sum = (feed_grads[0].astype(f32) + hidden_got.astype(f32)).astype(bf16)
    grad_residual, ga0 = norm_mlp_back(cots[0], back0, home2, residual0)
    ga1 = core(ga0)
    near_out = core(hold(away, home2))
    far_out = cross(pair_sum(stay[:BLOCK], near_out[:BLOCK]))
    gas = [ga0, ga1, ga2, ga3]
    hidden_sum, *stacked = lax.optimization_barrier((hidden_sum, *stacked))
    hidden_sum = over_columns(hidden_sum.reshape(width // 2, ff))
    stacked = list(attend_back(0, ga0, ga1, stacked))
    gm_all, stats_b, dq_state, direct = stacked

    (local_grad,) = call(
        chain_back_kernel,
        (1,),
        (t_pre,),
        [
            (direct, full(nb, NS, lw)),
            (gate_row, full(1, lw)),
            (keep_rows, full(nb, 1, lw)),
        ],
        [((NS, lw), bf16, full(NS, lw))],
        flops=nb * NS * lw * 2,
        nbytes=nb * NS * lw * 4,
    )
    local_grads = swap(local_grad.reshape(groups, share, lw))
    turn = lambda j: nb - 1 - j
    at = lambda col: pl.BlockSpec((BLOCK, lw), lambda j, t: (turn(j) ^ t[0], col))
    prev = lambda col: pl.BlockSpec(
        (BLOCK, lw), lambda j, t: (jnp.maximum(turn(j) - 1, 0) ^ t[0], col)
    )
    pos = lambda *tail: pl.BlockSpec((1,) + tail, lambda j, t: (turn(j) ^ t[0], 0, 0))
    dq, dk, dv, back_kv, bias_grad = call(
        functools.partial(window_back_kernel, scale, heads),
        (nb,),
        (t_pre,),
        [
            (qkv, at(0)),
            (qkv, at(1)),
            (qkv, at(2)),
            (qkv, prev(1)),
            (qkv, prev(2)),
            (edge, pl.BlockSpec((BLOCK, lw), lambda j, t: (0, 0))),
            (edge, pl.BlockSpec((BLOCK, lw), lambda j, t: (0, 1))),
            (id_cols, pl.BlockSpec((BLOCK, 1), lambda j, t: (turn(j), 0))),
            (id_rows, pl.BlockSpec((1, 1, 2 * BLOCK), lambda j, t: (turn(j), 0, 0))),
            (bias, full(heads, TILE, SPAN)),
            (gm_all, pos(BLOCK, lw)),
            (stats_b, pos(BLOCK, 128)),
            (dq_state, pos(BLOCK, lw)),
        ],
        [
            ((rows_all, lw), bf16, pl.BlockSpec((BLOCK, lw), lambda j, t: (turn(j) ^ t[0], 0))),
            ((nb, BLOCK, lw), f32, pos(BLOCK, lw)),
            ((nb, BLOCK, lw), f32, pos(BLOCK, lw)),
            ((BLOCK, 2 * lw), bf16, full(BLOCK, 2 * lw)),
            ((heads, TILE, SPAN), f32, full(heads, TILE, SPAN)),
        ],
        scratch=[pltpu.VMEM((2 * BLOCK, lw), bf16)] * 2 + [pltpu.VMEM((2 * BLOCK, lw), f32)] * 2,
        flops=nb * 5 * pair_flops,
        nbytes=nb * BLOCK * lw * 24,
        exps=nb * heads * BLOCK * SPAN,
    )
    local_grads, dq, return_sum = lax.optimization_barrier((local_grads, dq, return_sum))
    odd = s_index & 1
    return_own = lax.dynamic_slice_in_dim(return_sum, odd * slab, slab, 0)
    return_other = lax.dynamic_slice_in_dim(return_sum, (1 - odd) * slab, slab, 0)
    return_got = lax.ppermute(return_other, "seq", flip)
    carries, grad_state = call(
        scan_back_kernel,
        (1,),
        (),
        [(local_grads, full(groups, share, lw)), (group_rows, full(groups, 1, lw))],
        [
            ((groups, share, lw), bf16, full(groups, share, lw)),
            ((share, lw), f32, full(share, lw)),
        ],
        flops=NS * lw * 2,
        nbytes=NS * lw * 4,
    )
    carried = swap(carries).reshape(NS, lw)

    next_kv = along(back_kv, -1)

    mid, row_part = call(
        functools.partial(query_grads_kernel, nb),
        (width // cut,),
        (),
        [(gas[r], pl.BlockSpec((BLOCK, cut), lambda g: (0, g))) for r in range(nb)]
        + [
            (mixed_all, full(nb, BLOCK, lw)),
            (normed_all, pl.BlockSpec((rows_all, cut), lambda g: (0, g))),
            (dq, full(rows_all, lw)),
            (w_query, pl.BlockSpec((cut, lw), lambda g: (g, 0))),
        ],
        [
            ((width, 2 * lw), bf16, pl.BlockSpec((cut, 2 * lw), lambda g: (g, 0))),
            ((8, width), f32, pl.BlockSpec((8, cut), lambda g: (0, g))),
        ],
        flops=4 * rows_all * width * lw,
        nbytes=rows_all * width * 4,
        mib=32,
        pin=range(16),
    )
    carried, mid, hidden_sum, return_got, *_ = lax.optimization_barrier(
        (carried, mid, hidden_sum, return_got, far_out)
    )
    mid = swap(mid.reshape(groups, width // groups, 2 * lw))
    result = (
        residual0 + stay[BLOCK:].astype(f32) + near_out[BLOCK:].astype(f32) + far_out.astype(f32)
    ).astype(bf16)

    gu_all, gate_sum = call(
        carry_kernel,
        (1,),
        (t_pre,),
        [
            (carried, full(NS, lw)),
            (direct, full(nb, NS, lw)),
            (entry, full(NS, lw)),
            (before, full(nb, NS, lw)),
            (carry_rows, full(nb, 1, lw)),
            (keep_rows, full(nb, 1, lw)),
            (gate_row, full(1, lw)),
        ],
        [((nb, NS, lw), bf16, full(nb, NS, lw)), ((1, lw), f32, full(1, lw))],
        flops=nb * NS * lw * 8,
        nbytes=nb * NS * lw * 10,
    )
    def learn_back(high, gu_all, grad_sq, dkv):
        pos = lambda *tail: pl.BlockSpec((1,) + tail, lambda g, t: (high - g, 0, 0))
        row = lambda cols, col=0: pl.BlockSpec((BLOCK, cols), lambda g, t: (high - g, col))
        return call(
            functools.partial(update_back_kernel, scale, heads, high, nb - 1),
            (2,),
            (t_pre,),
            [
                (gu_all, pos(NS, lw)),
                (qkv, row(lw, 1)),
                (qkv, row(lw, 2)),
                (state_queries, full(NS, lw)),
                (lse_u, pos(NS, 128)),
                (updates, pos(NS, lw)),
                (dq, row(lw)),
                (dk, pos(BLOCK, lw)),
                (dv, pos(BLOCK, lw)),
                (next_kv, pl.BlockSpec((BLOCK, lw), lambda g, t: (0, 0))),
                (next_kv, pl.BlockSpec((BLOCK, lw), lambda g, t: (0, 1))),
                (w_joined, full(width, 3 * lw)),
                (grad_sq, full(NS, lw)),
            ],
            [
                ((rows_all, 2 * lw), bf16, row(2 * lw)),
                ((BLOCK, width), bf16, full(BLOCK, width)),
                ((BLOCK, width), bf16, full(BLOCK, width)),
                ((NS, lw), f32, full(NS, lw)),
            ],
            [] if dkv is None else [(dkv, 0)],
            flops=20 * NS * BLOCK * lw + 12 * BLOCK * lw * width,
            nbytes=2 * BLOCK * (lw * 30 + width * 2),
            exps=2 * heads * NS * BLOCK,
        )

    dkv, part3, part2, grad_sq = learn_back(3, gu_all, jnp.zeros((NS, lw), f32), None)
    far = pair_sum(part2, core(part3))
    gu_all = hold(gu_all, far)
    far = cross(far)
    dkv, part1, part0, grad_sq = learn_back(1, gu_all, grad_sq, dkv)
    near = core(part1)

    late, gain_attn_part = call(
        key_grads_kernel,
        (width // cut,),
        (),
        [
            (normed_all, pl.BlockSpec((rows_all, cut), lambda g: (0, g))),
            (dkv, full(rows_all, 2 * lw)),
            (w_key, pl.BlockSpec((cut, lw), lambda g: (g, 0))),
            (w_value, pl.BlockSpec((cut, lw), lambda g: (g, 0))),
            (grad_sq, pl.BlockSpec((per * share, lw), lambda g: (g, 0))),
            (row_part, pl.BlockSpec((8, cut), lambda g: (0, g))),
        ],
        [
            (
                (groups, slab + share // 2, 2 * lw),
                bf16,
                pl.BlockSpec((per, slab + share // 2, 2 * lw), lambda g: (g, 0, 0)),
            ),
            ((8, width), f32, pl.BlockSpec((8, cut), lambda g: (0, g))),
        ],
        flops=4 * rows_all * width * lw,
        nbytes=rows_all * width * 4,
        mib=32,
    )
    (bias_line,) = call(
        bias_sum_kernel,
        (1,),
        (),
        [(hold(bias_grad, late), full(heads, TILE, SPAN))],
        [((heads, SPAN), f32, full(heads, SPAN))],
    )
    bias_local = jnp.dot(bias_line, onehot, precision=lax.Precision.HIGHEST)
    late = swap(hold(late, far))

    bias_full = lax.dynamic_update_slice(
        jnp.zeros((H, BUCKETS), f32), bias_local, (t_index * heads, 0)
    )
    gate_full = lax.dynamic_update_slice(
        jnp.zeros((D,), f32), gate_sum[0] * gates * (1.0 - gates), (t_index * lw,)
    )
    small = jnp.concatenate(
        [
            gain_attn_part[0] / gain_attn,
            gain_mlp_part[0] / gain_mlp,
            gate_full,
            bias_full.reshape(-1),
        ]
    ).reshape(-1, 128)
    small = hold(small, mid)
    (grad_tokens,) = call(
        final_kernel,
        (2,),
        (),
        [(x, tall(width)) for x in (tokens, part0, near, far, grad_residual)]
        + [(gain_attn[None, :], full(1, width))],
        [((BLOCK, width), f32, tall(width))],
        flops=BLOCK * width * 12,
        nbytes=BLOCK * width * 16,
        pin=(0, 4),
    )

    small = small + core(small)
    small = small + cross(small)
    small, grad_tokens = lax.optimization_barrier((small, grad_tokens))
    step = 1
    while step < groups:
        small = small + lax.ppermute(small, "seq", [(i, i ^ step) for i in range(groups)])
        step *= 2
    small = small.reshape(-1)

    mid = jnp.sum(mid.astype(f32), axis=0)
    late = jnp.sum(late.astype(f32), axis=0)
    queries_sent = jnp.concatenate([late[slab:, :lw], late[slab:, lw:]])
    return (
        result,
        block_states,
        grad_tokens,
        grad_state,
        small[:D],
        mid[:, :lw],
        late[:slab, :lw],
        late[:slab, lw:],
        mid[:, lw:].T,
        small[3 * D :].reshape(H, BUCKETS),
        queries_sent,
        small[2 * D : 3 * D],
        small[D : 2 * D],
        hidden_sum.astype(f32),
        (return_own.astype(f32) + return_got.astype(f32)).T,
    )


def solution(mesh):
    return jax.shard_map(
        local,
        mesh=mesh,
        in_specs=(
            P(("seq", "tp"), None),
            P("seq"),
            P("seq"),
            P(None, "tp"),
            P(),
            P(None, "tp"),
            P(None, "tp"),
            P(None, "tp"),
            P("tp", None),
            P("tp", None),
            P(None, "tp"),
            P("tp"),
            P(),
            P(None, "tp"),
            P("tp", None),
            P(("seq", "tp"), None),
        ),
        out_specs=(
            P(("seq", "tp"), None),
            P("seq", None, "tp"),
            P(("seq", "tp"), None),
            P("seq", "tp"),
            P(),
            P("seq", "tp"),
            P("seq", "tp"),
            P("seq", "tp"),
            P("tp", "seq"),
            P(),
            P("seq", "tp"),
            P(),
            P(),
            P("seq", "tp"),
            P("tp", "seq"),
        ),
        check_vma=False,
    )
```

```python
import functools
import math

import jax
import jax.numpy as jnp
import numpy as np
from jax import lax
from jax.experimental import pallas as pl
from jax.experimental.pallas import tpu as pltpu
from jax.sharding import PartitionSpec as P

D = 1024
H = 8
NS = 512
BLOCK = 512
BUCKETS = 32
FAR = 128
TILE = 128
SPAN = BLOCK + TILE
HEAD = 128

eps = 1e-06
negative_fill = -1e30
LOG2E = math.log2(math.e)
WEIGHT = 0.05
HEAVY = 1.0
f32 = jnp.float32
bf16 = jnp.bfloat16


def nn(a, b):
    return lax.dot_general(a, b, (((1,), (0,)), ((), ())), preferred_element_type=f32)


def nt(a, b):
    return lax.dot_general(a, b, (((1,), (1,)), ((), ())), preferred_element_type=f32)


def tn(a, b):
    return lax.dot_general(a, b, (((0,), (0,)), ((), ())), preferred_element_type=f32)


def pinned(array):
    return pltpu.with_memory_space_constraint(array, pltpu.HBM)


def call(
    kernel, grid, prefetch, ins, outs, aliases=(), scratch=(), flops=0, nbytes=0, exps=0, mib=24,
    hbm=(), pin=(), weight=WEIGHT,
):
    any_spec = pl.BlockSpec(memory_space=pl.ANY)
    arrays = [
        pinned(array) if n in pin or array.ndim == 3 or array.shape[0] > D else array
        for n, (array, _) in enumerate(ins)
    ]
    arrays += [pinned(array) for array, _ in aliases]
    specs = [spec for _, spec in ins] + [any_spec for _ in aliases]
    first = len(prefetch) + len(ins)
    alias_map = {first + n: out for n, (_, out) in enumerate(aliases)}
    n_pre, n_in, n_alias = len(prefetch), len(ins), len(aliases)

    def body(*refs):
        kept = refs[: n_pre + n_in] + refs[n_pre + n_in + n_alias :]
        kernel(*kept)

    return pl.pallas_call(
        body,
        name=getattr(kernel, 'func', kernel).__name__,
        out_shape=[
            pltpu.HBM(shape, dtype)
            if len(shape) == 3 or shape[0] > D or n in hbm
            else jax.ShapeDtypeStruct(shape, dtype)
            for n, (shape, dtype, _) in enumerate(outs)
        ],
        grid_spec=pltpu.PrefetchScalarGridSpec(
            num_scalar_prefetch=n_pre,
            grid=grid,
            in_specs=specs,
            out_specs=[spec for _, _, spec in outs],
            scratch_shapes=list(scratch),
        ),
        input_output_aliases=alias_map,
        compiler_params=pltpu.CompilerParams(
            dimension_semantics=("arbitrary",) * len(grid), vmem_limit_bytes=mib * 1024 * 1024
        ),
        cost_estimate=pl.CostEstimate(
            flops=int(flops * weight),
            bytes_accessed=int(nbytes * weight),
            transcendentals=int(exps * weight),
        ),
    )(*prefetch, *arrays)


def lanes(*columns):
    rows = columns[0].shape[0]
    lane = lax.broadcasted_iota(jnp.int32, (rows, 128), 1)
    packed = jnp.broadcast_to(columns[0], (rows, 128))
    for n, column in enumerate(columns[1:], 1):
        packed = jnp.where(lane == n, column, packed)
    return packed


def pick(*columns):
    lane = lax.broadcasted_iota(jnp.int32, columns[0].shape, 1)
    packed = columns[0]
    for n, column in enumerate(columns[1:], 1):
        packed = jnp.where(lane == n, column, packed)
    return packed


def with_ones(values):
    return jnp.concatenate([values, jnp.ones((values.shape[0], HEAD), bf16)], axis=1)


def head_of(h):
    return slice(h * HEAD, (h + 1) * HEAD)


def bias_kernel(base_ref, out_ref):
    for h in range(out_ref.shape[0]):
        row = jnp.broadcast_to(base_ref[h : h + 1, :], (TILE, SPAN))
        out_ref[h] = pltpu.roll(row, 0, 1, stride=1, stride_axis=0)


def bias_sum_kernel(grad_ref, out_ref):
    rows = lax.broadcasted_iota(jnp.int32, (TILE, SPAN), 0)
    for h in range(grad_ref.shape[0]):
        value = grad_ref[h]
        step = 1
        while step < TILE:
            moved = pltpu.roll(value, SPAN - step, 1)
            value = jnp.where((rows & step) != 0, moved, value)
            step *= 2
        out_ref[h : h + 1, :] = jnp.sum(value, axis=0, keepdims=True)


def front_kernel(scale, heads, tok_a, tok_b, gain, w, sq, normed_out, qkv_out, u_out, lse_out):
    width = heads * HEAD
    first = pl.program_id(0) == 0
    rows = 256
    for i in range(BLOCK // rows):
        part = slice(i * rows, (i + 1) * rows)
        x = jnp.where(first, tok_a[part, :].astype(f32), tok_b[part, :].astype(f32))
        r = lax.rsqrt(jnp.mean(x * x, axis=-1, keepdims=True) + eps)
        n = (x * r * gain[...]).astype(bf16)
        normed_out[part, :] = n
        qkv_out[part, :] = nn(n, w[...]).astype(bf16)
    values = [
        with_ones(qkv_out[:, 2 * width + h * HEAD : 2 * width + (h + 1) * HEAD])
        for h in range(heads)
    ]

    def scores_of(i, h):
        k = qkv_out[:, width + h * HEAD : width + (h + 1) * HEAD]
        return nt(sq[i * rows : (i + 1) * rows, head_of(h)], k)

    work = [(i, h) for i in range(BLOCK // rows) for h in range(heads)]
    ready = scores_of(*work[0])
    stats = []
    for n, (i, h) in enumerate(work):
        s = ready * (scale * LOG2E)
        if n + 1 < len(work):
            ready = scores_of(*work[n + 1])
        part = slice(i * rows, (i + 1) * rows)
        m = jnp.max(s, axis=1, keepdims=True)
        p = jnp.exp2(s - m)
        both = nn(p.astype(bf16), values[h])
        total = both[:, HEAD:]
        u_out[0, part, head_of(h)] = both[:, :HEAD] / total
        stats.append(m + jnp.log(total) * LOG2E)
        if h == heads - 1:
            lse_out[0, part, :] = pick(*stats)
            stats = []


def masked(scale, h, raw, qid, kid, bias):
    return jnp.where(qid == kid, raw * (scale * LOG2E) + bias[h], negative_fill)


def window_kernel(scale, heads, t, q, kc, vc, kp, vp, qid, kid, bias, acc, ml, keys, values):
    keys[:BLOCK] = kp[...]
    keys[BLOCK:] = kc[...]
    values[:BLOCK] = vp[...]
    values[BLOCK:] = vc[...]

    def scores_of(i, h):
        part = slice(i * TILE, (i + 1) * TILE)
        return nt(q[part, head_of(h)], keys[i * TILE : i * TILE + SPAN, head_of(h)])

    work = [(i, h) for i in range(BLOCK // TILE) for h in range(heads)]
    ready = scores_of(*work[0])
    peaks, sums = [], []
    for n, (i, h) in enumerate(work):
        raw = ready
        if n + 1 < len(work):
            ready = scores_of(*work[n + 1])
        part = slice(i * TILE, (i + 1) * TILE)
        span = slice(i * TILE, i * TILE + SPAN)
        s = masked(scale, h, raw, qid[part, :], kid[0, :, span], bias)
        m = jnp.max(s, axis=1, keepdims=True)
        p = jnp.exp2(s - m)
        both = nn(p.astype(bf16), with_ones(values[span, head_of(h)]))
        acc[0, part, head_of(h)] = both[:, :HEAD]
        peaks.append(jnp.broadcast_to(m, (TILE, HEAD)))
        sums.append(both[:, HEAD:])
        if h == heads - 1:
            ml[0, part, :] = pick(*peaks, *sums)
            peaks, sums = [], []


def chain_kernel(t, updates, factors, before_out, total_out):
    state = jnp.zeros(total_out.shape, f32)
    for j in range(updates.shape[0]):
        before_out[j] = state
        state = factors[j] * state + updates[t[0] ^ j]
    total_out[...] = state.astype(bf16)


def scan_kernel(s, totals, factors, init, out):
    state = init[...]
    for g in range(totals.shape[0]):
        out[g] = state.astype(bf16)
        state = factors[g] * state + totals[g].astype(f32)


def chain_back_kernel(t, direct, gates, keep_rows, out):
    state = jnp.zeros(out.shape, f32)
    for j in reversed(range(direct.shape[0])):
        state = keep_rows[j] * (direct[t[0] ^ j] + gates[...] * state)
    out[...] = state.astype(bf16)


def scan_back_kernel(totals, factors, out, first_out):
    state = jnp.zeros(first_out.shape, f32)
    for g in reversed(range(totals.shape[0])):
        out[g] = state.astype(bf16)
        state = factors[g] * state + totals[g].astype(f32)
    first_out[...] = state


def carry_kernel(
    t, carried0, direct, entry, before, carry_rows, keep_rows, gates, gu_out, gate_out
):
    now = carried0[...].astype(f32)
    start = entry[...].astype(f32)
    total = jnp.zeros(gate_out.shape, f32)
    for j in reversed(range(direct.shape[0])):
        used = carry_rows[j] * start + keep_rows[j] * before[j]
        total = total + jnp.sum(now * used, axis=0, keepdims=True)
        gu_out[t[0] ^ j] = now.astype(bf16)
        now = keep_rows[j] * (direct[t[0] ^ j] + gates[...] * now)
    gate_out[...] = total


def state_kernel(
    scale, heads, t, q, entry, before, carry_row, keep_row, acc, ml, w,
    mixed_out, stats_out, used_out, first_out, second_out,
):
    used_out[0] = (carry_row[0] * entry[...].astype(f32) + keep_row[0] * before[0]).astype(bf16)
    values = [with_ones(used_out[0, :, head_of(h)]) for h in range(heads)]
    rows = 256
    for i in range(BLOCK // rows):
        part = slice(i * rows, (i + 1) * rows)
        stats = []
        for h in range(heads):
            m = ml[0, part, h : h + 1]
            l = ml[0, part, heads + h : heads + h + 1]
            s = nt(q[part, head_of(h)], used_out[0, :, head_of(h)]) * (scale * LOG2E)
            top = jnp.maximum(m, jnp.max(s, axis=1, keepdims=True))
            p = jnp.exp2(s - top)
            shrink = jnp.exp2(m - top)
            both = nn(p.astype(bf16), values[h])
            total = l * shrink + both[:, HEAD:]
            value = (acc[0, part, head_of(h)] * shrink + both[:, :HEAD]) / total
            mixed_out[0, part, head_of(h)] = value.astype(bf16)
            stats.append(top + jnp.log(total) * LOG2E)
        stats_out[0, part, :] = pick(*stats)
    result = nn(mixed_out[0], w[...]).astype(bf16)
    first = pl.program_id(0) == 0

    @pl.when(first)
    def _():
        first_out[...] = result

    @pl.when(jnp.logical_not(first))
    def _():
        second_out[...] = result


def states_kernel(t, entry, before, carry_row, keep_row, gates, u, next_out):
    used = carry_row[0] * entry[...].astype(f32) + keep_row[0] * before[0]
    next_out[0] = gates[...] * used + u[0]


def return_kernel(hidden, w, away_out, stay_out):
    even = pl.program_id(0) % 2 == 0

    @pl.when(even)
    def _():
        away_out[...] = nn(hidden[...], w[...]).astype(bf16)

    @pl.when(jnp.logical_not(even))
    def _():
        stay_out[...] = nn(hidden[...], w[...]).astype(bf16)


def norm_kernel(tok, mine, theirs, gain, residual_out, nm_out):
    residual = tok[...].astype(f32) + (mine[...].astype(f32) + theirs[...].astype(f32))
    residual_out[...] = residual
    inverse = lax.rsqrt(jnp.mean(residual * residual, axis=-1, keepdims=True) + eps)
    nm_out[...] = (residual * inverse * gain[...]).astype(bf16)


def norm_back_kernel(
    cot, mine, theirs, residual, gain, grad_out, low_out, upper_out, lower_out
):
    r = residual[...]
    inverse = lax.rsqrt(jnp.mean(r * r, axis=-1, keepdims=True) + eps)
    scaled = r * inverse
    grad = (mine[...].astype(f32) + theirs[...].astype(f32)) * gain[...]
    inner = jnp.mean(grad * scaled, axis=-1, keepdims=True)
    result = cot[...].astype(f32) + inverse * (grad - scaled * inner)
    grad_out[...] = result
    low = result.astype(bf16)
    low_out[...] = low
    upper = pl.program_id(0) == 0

    @pl.when(upper)
    def _():
        upper_out[...] = low

    @pl.when(jnp.logical_not(upper))
    def _():
        lower_out[...] = low


def final_kernel(tok, mine, near, far, residual_grad, gain, out):
    x = tok[...].astype(f32)
    inverse = lax.rsqrt(jnp.mean(x * x, axis=-1, keepdims=True) + eps)
    scaled = x * inverse
    grad = mine[...].astype(f32) + near[...].astype(f32) + far[...].astype(f32)
    grad = grad * gain[...]
    inner = jnp.mean(grad * scaled, axis=-1, keepdims=True)
    out[...] = residual_grad[...] + inverse * (grad - scaled * inner)


def row_sums(value):
    sums = jnp.broadcast_to(jnp.sum(value, axis=1, keepdims=True), (value.shape[0], HEAD))
    return sums.T[:8]


def feed_grads_kernel(n, s, *refs):
    nms, cots = refs[:n], refs[n : 2 * n]
    gpre, hidden, w, kept_out, sent_out, return_out, gain_out = refs[2 * n :]
    odd = s[0] % 2 == 1
    rows = nms[0].shape[0]
    ff = w.shape[1]
    for which, left, right in ((0, nms, gpre), (1, cots, hidden)):
        total = None
        for r in range(n):
            piece = tn(left[r][...], right[r * rows : (r + 1) * rows, :])
            total = piece if total is None else total + piece
        low = total.astype(bf16)
        if which == 0:
            slab = kept_out.shape[1]
            for g in range(kept_out.shape[0]):
                even_rows = low[2 * g * slab : (2 * g + 1) * slab]
                odd_rows = low[(2 * g + 1) * slab : (2 * g + 2) * slab]
                kept_out[g] = jnp.where(odd, odd_rows, even_rows)
                sent_out[g] = jnp.where(odd, even_rows, odd_rows)
        else:
            return_out[...] = low
        if which == 0:
            gain_out[...] = row_sums(total * w[...].astype(f32))


def query_grads_kernel(n, *refs):
    gas = refs[:n]
    mixed, normed, dq, w, out, row_out = refs[n:]
    lw = dq.shape[1]
    total, at = None, 0
    for ga in gas:
        first = at % BLOCK
        piece = tn(ga[...], mixed[at // BLOCK, first : first + ga.shape[0]])
        total = piece if total is None else total + piece
        at += ga.shape[0]
    out[:, lw:] = total.astype(bf16)
    grad = tn(normed[...], dq[...])
    out[:, :lw] = grad.astype(bf16)
    row_out[...] = row_sums(grad * w[...].astype(f32))


def key_grads_kernel(normed, dkv, wk, wv, dsq, row, out, row_out):
    grad = tn(normed[...], dkv[...])
    rows, lw = grad.shape[0], wk.shape[1]
    slab = rows // out.shape[0]
    part = dsq.shape[0] // out.shape[0] // 2
    low = grad.astype(bf16)
    for g in range(out.shape[0]):
        out[g, :slab] = low[g * slab : (g + 1) * slab]
        out[g, slab:, :lw] = dsq[2 * g * part : (2 * g + 1) * part].astype(bf16)
        out[g, slab:, lw:] = dsq[(2 * g + 1) * part : (2 * g + 2) * part].astype(bf16)
    both = jnp.concatenate([wk[...].astype(f32), wv[...].astype(f32)], axis=1)
    row_out[...] = row[...] + row_sums(grad * both)


def mlp_kernel(steps, nm_a, nm_b, gact_a, gact_b, w, hidden_out, gpre_out, first_out, second_out):
    first = pl.program_id(0) < steps
    cols = 256
    x = jnp.where(first, nm_a[...], nm_b[...])
    for c in range(w.shape[1] // cols):
        cut = slice(c * cols, (c + 1) * cols)
        pre = nn(x, w[:, cut])
        cumulative = 0.5 * (1.0 + lax.erf(pre * (1.0 / math.sqrt(2.0))))
        density = jnp.exp2(pre * pre * (-0.5 * LOG2E)) * (1.0 / math.sqrt(2.0 * math.pi))
        hidden_out[:, cut] = (pre * cumulative).astype(bf16)
        gact = jnp.where(first, gact_a[:, cut].astype(f32), gact_b[:, cut].astype(f32))
        gpre_out[:, cut] = (gact * (cumulative + pre * density)).astype(bf16)
    result = nt(gpre_out[...], w[...]).astype(bf16)

    @pl.when(first)
    def _():
        first_out[...] = result

    @pl.when(jnp.logical_not(first))
    def _():
        second_out[...] = result


def state_back_kernel(
    scale, heads, ga_a, ga_b, ga_c, w, q, mixed, used, stats, gm_out, stats_out, dq_out, direct_out
):
    first = pl.program_id(0) == 0
    gm_out[0] = nt(jnp.where(first, ga_a[...], jnp.concatenate([ga_b[...], ga_c[...]])), w[...]).astype(bf16)
    raws = [
        (nt(q[:, head_of(h)], used[0, :, head_of(h)]), nt(gm_out[0, :, head_of(h)], used[0, :, head_of(h)]))
        for h in range(heads)
    ]
    logs, deltas = [], []
    for h, (raw, grad_p) in enumerate(raws):
        hs = head_of(h)
        gm = gm_out[0, :, hs]
        delta = jnp.sum(gm.astype(f32) * mixed[0, :, hs].astype(f32), axis=1, keepdims=True)
        lse = stats[0, :, h : h + 1]
        p = jnp.exp2(raw * (scale * LOG2E) - lse)
        ds = (p * (grad_p - delta)).astype(bf16)
        dq_out[0, :, hs] = nn(ds, used[0, :, hs]) * scale
        direct_out[0, :, hs] = tn(ds, q[:, hs]) * scale + tn(p.astype(bf16), gm)
        logs.append(lse)
        deltas.append(delta)
    stats_out[0] = lanes(*logs, *deltas)


def window_back_kernel(
    scale, heads, t, q, kc, vc, kb, vb, hk, hv, qid, kid, bias, gm, stats, dqs,
    dq_out, dk_out, dv_out, edge_out, grad_bias, keys, values, dkeys, dvalues,
):
    step = pl.program_id(0)
    last = pl.num_programs(0) - 1

    @pl.when(step == last)
    def _():
        keys[:BLOCK] = hk[...]
        values[:BLOCK] = hv[...]

    @pl.when(step != last)
    def _():
        keys[:BLOCK] = kb[...]
        values[:BLOCK] = vb[...]

    keys[BLOCK:] = kc[...]
    values[BLOCK:] = vc[...]

    @pl.when(step == 0)
    def _():
        dkeys[...] = jnp.zeros_like(dkeys)
        dvalues[...] = jnp.zeros_like(dvalues)
        grad_bias[...] = jnp.zeros_like(grad_bias)

    @pl.when(step != 0)
    def _():
        for total in (dkeys, dvalues):
            total[BLOCK:] = total[:BLOCK]
            total[:BLOCK] = jnp.zeros((BLOCK, total.shape[1]), f32)

    def scores_of(i, h):
        part = slice(i * TILE, (i + 1) * TILE)
        span = slice(i * TILE, i * TILE + SPAN)
        hs = head_of(h)
        return nt(q[part, hs], keys[span, hs]), nt(gm[0, part, hs], values[span, hs])

    work = [(i, h) for i in range(BLOCK // TILE) for h in range(heads)]
    ready = scores_of(*work[0])
    for n, (i, h) in enumerate(work):
        raw, grad_p = ready
        if n + 1 < len(work):
            ready = scores_of(*work[n + 1])
        part = slice(i * TILE, (i + 1) * TILE)
        span = slice(i * TILE, i * TILE + SPAN)
        hs = head_of(h)
        qt = q[part, hs]
        g = gm[0, part, hs]
        lse = stats[0, part, h : h + 1]
        delta = stats[0, part, heads + h : heads + h + 1]
        p = jnp.exp2(masked(scale, h, raw, qid[part, :], kid[0, :, span], bias) - lse)
        ds = p * (grad_p - delta)
        low = ds.astype(bf16)
        zero = jnp.zeros_like(qt)
        sides = jnp.concatenate(
            [jnp.concatenate([qt, zero], axis=1), jnp.concatenate([zero, g], axis=1)]
        )
        both = tn(jnp.concatenate([low, p.astype(bf16)]), sides)
        dq = nn(low, keys[span, hs]) * scale + dqs[0, part, hs]
        grad_bias[h] += ds
        dq_out[part, hs] = dq.astype(bf16)
        dkeys[span, hs] += both[:, :HEAD] * scale
        dvalues[span, hs] += both[:, HEAD:]
    dk_out[0] = dkeys[BLOCK:]
    dv_out[0] = dvalues[BLOCK:]

    @pl.when(step == last)
    def _():
        width = heads * HEAD
        edge_out[:, :width] = dkeys[:BLOCK].astype(bf16)
        edge_out[:, width:] = dvalues[:BLOCK].astype(bf16)


def update_back_kernel(
    scale, heads, high, last, t, gu_all, k, v, sq, lse_u, u, dq, dk, dv, hk, hv, w, dsq_in,
    dkv_out, first_out, second_out, dsq_out,
):
    width = heads * HEAD
    step = pl.program_id(0)
    edge = jnp.where((t[0] ^ (high - step)) == last, 1.0, 0.0)

    @pl.when(step == 0)
    def _():
        dsq_out[...] = dsq_in[...]

    raws = [
        (nt(sq[:, head_of(h)], k[:, head_of(h)]), nt(gu_all[0, :, head_of(h)], v[:, head_of(h)]))
        for h in range(heads)
    ]
    for h, (raw, grad_p) in enumerate(raws):
        hs = head_of(h)
        gu = gu_all[0, :, hs]
        sqh = sq[:, hs]
        kh = k[:, hs]
        delta = jnp.sum(gu.astype(f32) * u[0, :, hs], axis=1, keepdims=True)
        p = jnp.exp2(raw * (scale * LOG2E) - lse_u[0, :, h : h + 1])
        ds = (p * (grad_p - delta)).astype(bf16)
        dsq_out[:, hs] += nn(ds, kh) * scale
        dkh = dk[0, :, hs] + tn(ds, sqh) * scale + edge * hk[:, hs].astype(f32)
        dvh = dv[0, :, hs] + tn(p.astype(bf16), gu) + edge * hv[:, hs].astype(f32)
        dkv_out[:, hs] = dkh.astype(bf16)
        dkv_out[:, width + h * HEAD : width + (h + 1) * HEAD] = dvh.astype(bf16)
    part = nt(dq[...], w[:, :width]) + nt(dkv_out[...], w[:, width:])
    result = part.astype(bf16)

    @pl.when(step == 0)
    def _():
        first_out[...] = result

    @pl.when(step != 0)
    def _():
        second_out[...] = result


def bucket_of(distance):
    half = BUCKETS // 2
    limits = [math.ceil(half * (FAR / half) ** (level / half)) for level in range(1, half)]
    clipped = np.maximum(distance, 0)
    extra = sum((clipped >= limit).astype(np.int32) for limit in limits)
    return np.where(clipped < half, clipped, half + extra)


def local(
    tokens,
    doc_flags,
    reset_flags,
    state_init,
    gain_attn,
    w_query,
    w_key,
    w_value,
    w_output,
    bias_table,
    state_queries,
    gate_logits,
    gain_mlp,
    w_hidden,
    w_return,
    cotangent,
):
    heads = bias_table.shape[0]
    lw = w_query.shape[1]
    width = tokens.shape[1]
    nb = reset_flags.shape[0]
    ff = w_hidden.shape[1]
    scale = 1.0 / math.sqrt(HEAD)
    groups = lax.axis_size("seq")
    s_index = lax.axis_index("seq")
    t_index = lax.axis_index("tp")
    t_pre = t_index.astype(jnp.int32)[None]
    s_pre = s_index.astype(jnp.int32)[None]
    rows_all = nb * BLOCK

    def core(value):
        return lax.ppermute(value, "tp", [(i, i ^ 1) for i in range(nb)])

    def cross(value):
        return lax.ppermute(value, "tp", [(i, i ^ 2) for i in range(nb)])

    def along(value, step):
        pairs = [(i, i + step) for i in range(groups) if 0 <= i + step < groups]
        return lax.ppermute(value, "seq", pairs)

    def swap(value):
        return lax.all_to_all(value, "seq", 0, 0, tiled=True)

    def hold(value, *others):
        return lax.optimization_barrier((value, *others))[0]

    full = lambda *shape: pl.BlockSpec(shape, lambda *_: (0,) * len(shape))
    half = BLOCK // 2
    tall = lambda *tail: pl.BlockSpec((half,) + tail, lambda g, *_: (g, 0))
    share = NS // groups

    tok2 = cross(tokens)
    tok1 = core(tokens)

    gates = jax.nn.sigmoid(gate_logits)
    keeps = (1 - reset_flags).astype(f32)
    gate_row = gates[None, :]
    gate_group = gates
    for _ in range(nb - 1):
        gate_group = gate_group * gates
    apart = BLOCK - np.arange(SPAN)
    shown = (apart >= 0) & (apart < BLOCK)
    onehot = (bucket_of(apart)[:, None] == np.arange(BUCKETS)[None, :]) & shown[:, None]
    onehot = jnp.asarray(onehot.astype(np.float32))
    base = jnp.dot(bias_table * LOG2E, onehot.T, precision=lax.Precision.HIGHEST)
    base = jnp.where(jnp.asarray(shown)[None, :], base, negative_fill)
    (bias,) = call(
        bias_kernel,
        (1,),
        (),
        [(base, full(heads, SPAN))],
        [((heads, TILE, SPAN), f32, full(heads, TILE, SPAN))],
    )

    w_joined = jnp.concatenate([w_query, w_key, w_value], axis=1)
    def front(first, tok_a, tok_b, stacked):
        row = lambda cols: pl.BlockSpec((BLOCK, cols), lambda g: (first + g, 0))
        pos = lambda *tail: pl.BlockSpec((1,) + tail, lambda g: (first + g, 0, 0))
        return call(
            functools.partial(front_kernel, scale, heads),
            (2,),
            (),
            [
                (tok_a, full(BLOCK, width)),
                (tok_b, full(BLOCK, width)),
                (gain_attn[None, :], full(1, width)),
                (w_joined, full(width, 3 * lw)),
                (state_queries, full(NS, lw)),
            ],
            [
                ((rows_all, width), bf16, row(width)),
                ((rows_all, 3 * lw), bf16, row(3 * lw)),
                ((nb, NS, lw), f32, pos(NS, lw)),
                ((nb, NS, 128), f32, pos(NS, 128)),
            ],
            [] if stacked is None else [(array, n) for n, array in enumerate(stacked)],
            flops=4 * BLOCK * width * 3 * lw + 8 * NS * BLOCK * lw,
            nbytes=12 * BLOCK * width * 2,
            exps=2 * heads * NS * BLOCK,
        )

    starts = [jnp.ones_like(gates)]
    for j in range(nb - 1):
        starts.append(starts[j] * (gates * keeps[j]))
    carry_rows = (jnp.stack(starts) * keeps[:, None])[:, None, :]
    keep_rows = jnp.broadcast_to(keeps[:, None, None], (nb, 1, lw))
    block_rows = (keeps[:, None] * gates[None, :])[:, None, :]
    stacked = front(0, tokens, tok1, None)
    reset_sent, flags_sent, *stacked = lax.optimization_barrier((reset_flags, doc_flags, *stacked))
    every = swap(jnp.broadcast_to(reset_sent.reshape(1, nb), (groups, nb)))
    flag_prev = along(flags_sent[rows_all - BLOCK :], 1)
    tok2, bias, every, flag_prev, *stacked = lax.optimization_barrier(
        (tok2, bias, every, flag_prev, *stacked)
    )
    toks = [tokens, tok1, tok2, core(tok2)]
    cot1 = core(cotangent)
    stacked = list(front(2, toks[2], toks[3], stacked))
    every, flag_prev, *stacked = lax.optimization_barrier((every, flag_prev, *stacked))
    group_keep = jnp.prod((1 - every).astype(f32), axis=1)

    group_rows = (group_keep[:, None] * gate_group[None, :])[:, None, :]

    ids = jnp.cumsum(jnp.concatenate([flag_prev, doc_flags]))
    ids = jnp.where((jnp.arange(rows_all + BLOCK) < BLOCK) & (s_index == 0), -1, ids)
    id_rows = ids.reshape(nb + 1, 1, BLOCK)
    id_rows = jnp.concatenate([id_rows[:-1], id_rows[1:]], axis=2)
    id_cols = ids[BLOCK:].reshape(rows_all, 1)
    cot2, stacked[0] = lax.optimization_barrier((cotangent, stacked[0]))
    cot2 = cross(cot2)
    normed_all, qkv, updates, lse_u = stacked

    place = (t_index ^ (nb - 1)) * BLOCK
    edge = along(lax.dynamic_slice(qkv, (place, lw), (BLOCK, 2 * lw)), 1)

    before, total = call(
        chain_kernel,
        (1,),
        (t_pre,),
        [(updates, full(nb, NS, lw)), (block_rows, full(nb, 1, lw))],
        [((nb, NS, lw), f32, full(nb, NS, lw)), ((NS, lw), bf16, full(NS, lw))],
        flops=nb * NS * lw * 2,
        nbytes=nb * NS * lw * 8,
        hbm=(0,),
    )
    pair_flops = 2 * BLOCK * SPAN * lw

    def window(first, count, edge, stacked, weight):
        at = lambda col, back=0: pl.BlockSpec(
            (BLOCK, lw), lambda j, t: ((j + first - back) ^ t[0], col)
        )
        blk = lambda *tail: pl.BlockSpec((1,) + tail, lambda j, t: (j + first, 0, 0))
        if edge is None:
            before_block = [(qkv, at(1, 1)), (qkv, at(2, 1))]
        else:
            before_block = [
                (edge, pl.BlockSpec((BLOCK, lw), lambda j, t: (0, 0))),
                (edge, pl.BlockSpec((BLOCK, lw), lambda j, t: (0, 1))),
            ]
        return call(
            functools.partial(window_kernel, scale, heads),
            (count,),
            (t_pre,),
            [(qkv, at(0)), (qkv, at(1)), (qkv, at(2))]
            + before_block
            + [
                (id_cols, pl.BlockSpec((BLOCK, 1), lambda j, t: (j + first, 0))),
                (id_rows, pl.BlockSpec((1, 1, 2 * BLOCK), lambda j, t: (j + first, 0, 0))),
                (bias, full(heads, TILE, SPAN)),
            ],
            [
                ((nb, BLOCK, lw), f32, blk(BLOCK, lw)),
                ((nb, BLOCK, 128), f32, blk(BLOCK, 128)),
            ],
            [] if stacked is None else [(array, n) for n, array in enumerate(stacked)],
            flops=count * 2 * pair_flops,
            nbytes=count * BLOCK * lw * 12,
            exps=count * heads * BLOCK * SPAN,
            scratch=[pltpu.VMEM((2 * BLOCK, lw), bf16)] * 2,
            weight=weight,
        )

    windows = window(1, nb - 1, None, None, WEIGHT)
    late_edge, total, *windows = lax.optimization_barrier((edge, total, *windows))
    totals = swap(total.reshape(groups, share, lw))
    acc, ml = window(0, 1, late_edge, windows, HEAVY)
    cot2 = hold(cot2, acc)
    cots = [hold(cotangent, acc), hold(cot1, acc), cot2, core(cot2)]
    gacts = [nt(cot, w_return).astype(bf16) for cot in cots]
    totals, gacts[0], gacts[1] = lax.optimization_barrier((totals, gacts[0], gacts[1]))
    (entries,) = call(
        scan_kernel,
        (1,),
        (s_pre,),
        [
            (totals, full(groups, share, lw)),
            (group_rows, full(groups, 1, lw)),
            (state_init, pl.BlockSpec((share, lw), lambda g, s: (s[0], 0))),
        ],
        [((groups, share, lw), bf16, full(groups, share, lw))],
        flops=NS * lw * 2,
        nbytes=NS * lw * 4,
    )
    entry = swap(entries).reshape(NS, lw)

    entry, *gacts = lax.optimization_barrier((entry, *gacts))

    def attend(high, stacked):
        blk = lambda *tail: pl.BlockSpec((1,) + tail, lambda g, t: (t[0] ^ (high - g), 0, 0))
        pos = lambda *tail: pl.BlockSpec((1,) + tail, lambda g, t: (high - g, 0, 0))
        return call(
            functools.partial(state_kernel, scale, heads),
            (2,),
            (t_pre,),
            [
                (qkv, pl.BlockSpec((BLOCK, lw), lambda g, t: (high - g, 0))),
                (entry, full(NS, lw)),
                (before, blk(NS, lw)),
                (carry_rows, blk(1, lw)),
                (keep_rows, blk(1, lw)),
                (acc, blk(BLOCK, lw)),
                (ml, blk(BLOCK, 128)),
                (w_output, full(lw, width)),
            ],
            [
                ((nb, BLOCK, lw), bf16, pos(BLOCK, lw)),
                ((nb, BLOCK, 128), f32, pos(BLOCK, 128)),
                ((nb, NS, lw), bf16, pos(NS, lw)),
                ((BLOCK, width), bf16, full(BLOCK, width)),
                ((BLOCK, width), bf16, full(BLOCK, width)),
            ],
            [] if stacked is None else [(array, n) for n, array in enumerate(stacked)],
            flops=8 * BLOCK * NS * lw + 4 * BLOCK * lw * width,
            nbytes=2 * BLOCK * (lw * 24 + width * 2),
            exps=2 * heads * BLOCK * NS,
        )

    *stacked, part3, part2 = attend(3, None)
    *stacked, part1, part0 = attend(1, stacked)
    mixed_all, stats_f, used_low = stacked

    def pair_sum(mine, theirs):
        return (mine.astype(f32) + theirs.astype(f32)).astype(bf16)

    sum2 = pair_sum(part2, core(part3))
    sum0 = pair_sum(part0, core(part1))
    far2 = cross(sum2)
    blk = lambda *tail: pl.BlockSpec((1,) + tail, lambda g, t: (t[0] ^ g, 0, 0))
    pos = lambda *tail: pl.BlockSpec((1,) + tail, lambda g, t: (g, 0, 0))
    (block_states,) = call(
        states_kernel,
        (nb,),
        (t_pre,),
        [
            (hold(entry, sum0), full(NS, lw)),
            (before, blk(NS, lw)),
            (carry_rows, blk(1, lw)),
            (keep_rows, blk(1, lw)),
            (gate_row, full(1, lw)),
            (updates, pos(NS, lw)),
        ],
        [((nb, NS, lw), f32, blk(NS, lw))],
        flops=nb * NS * lw * 4,
        nbytes=nb * NS * lw * 12,
        hbm=(0,),
    )
    far2 = hold(far2, block_states)
    far0 = cross(hold(sum0, far2))

    def norm_mlp(tok, mine, theirs):
        return call(
            norm_kernel,
            (2,),
            (),
            [(x, tall(width)) for x in (tok, mine, theirs)] + [(gain_mlp[None, :], full(1, width))],
            [((BLOCK, width), f32, tall(width)), ((BLOCK, width), bf16, tall(width))],
            flops=BLOCK * width * 8,
            nbytes=BLOCK * width * 12,
            hbm=(0,),
        )

    def feed(first, nm_a, nm_b, stacked):
        early_tile = lambda cols: pl.BlockSpec((half, cols), lambda g: (jnp.minimum(g, 1), 0))
        late_tile = lambda cols: pl.BlockSpec((half, cols), lambda g: (jnp.maximum(g - 2, 0), 0))
        return call(
            functools.partial(mlp_kernel, 2),
            (4,),
            (),
            [
                (nm_a, early_tile(width)),
                (nm_b, late_tile(width)),
                (gacts[first], early_tile(ff)),
                (gacts[first + 1], late_tile(ff)),
                (w_hidden, full(width, ff)),
            ],
            [
                ((rows_all, ff), bf16, pl.BlockSpec((half, ff), lambda g: (2 * first + g, 0))),
                ((rows_all, ff), bf16, pl.BlockSpec((half, ff), lambda g: (2 * first + g, 0))),
                ((BLOCK, width), bf16, early_tile(width)),
                ((BLOCK, width), bf16, late_tile(width)),
            ],
            [] if stacked is None else [(array, n) for n, array in enumerate(stacked)],
            flops=8 * BLOCK * width * ff,
            nbytes=2 * BLOCK * width * 10,
            exps=4 * BLOCK * ff,
        )

    residual0, nm0 = norm_mlp(toks[0], sum0, far2)
    nm1 = core(nm0)
    *stacked, back0, back1 = feed(0, nm0, nm1, None)
    far0, back1 = lax.optimization_barrier((far0, back1))
    back0 = pair_sum(back0, core(back1))
    home0 = cross(back0)
    residual2, nm2 = norm_mlp(toks[2], sum2, far0)
    nm3 = core(nm2)
    *stacked, back2, back3 = feed(2, nm2, nm3, stacked)
    hidden_all, gpre_all = stacked
    slab = width // groups
    cut = 256
    per = cut // slab

    nms = [nm0, nm1, nm2, nm3]
    *feed_grads, gain_mlp_part = call(
        functools.partial(feed_grads_kernel, nb),
        (width // cut,),
        (s_pre,),
        [(x, pl.BlockSpec((BLOCK, cut), lambda g, s: (0, g))) for x in nms + cots]
        + [
            (gpre_all, full(rows_all, ff)),
            (hidden_all, full(rows_all, ff)),
            (w_hidden, pl.BlockSpec((cut, ff), lambda g, s: (g, 0))),
        ],
        [
            ((groups // 2, slab, ff), bf16, pl.BlockSpec((per // 2, slab, ff), lambda g, s: (g, 0, 0))),
            ((groups // 2, slab, ff), bf16, pl.BlockSpec((per // 2, slab, ff), lambda g, s: (g, 0, 0))),
            ((width, ff), bf16, pl.BlockSpec((cut, ff), lambda g, s: (g, 0))),
            ((8, width), f32, pl.BlockSpec((8, cut), lambda g, s: (0, g))),
        ],
        flops=4 * rows_all * width * ff,
        nbytes=rows_all * width * 8,
        mib=48,
        pin=range(16),
        hbm=range(4),
    )

    flip = [(i, i ^ 1) for i in range(groups)]
    columns = [list(range(side, groups, 2)) for side in range(2)]

    def over_columns(value):
        return lax.psum_scatter(
            value, "seq", scatter_dimension=0, tiled=True, axis_index_groups=columns
        )

    home0, back3, *feed_grads = lax.optimization_barrier((home0, back3, *feed_grads))
    back2 = pair_sum(back2, core(back3))
    home2 = cross(back2)

    def norm_mlp_back(cot, mine, theirs, residual):
        return call(
            norm_back_kernel,
            (2,),
            (),
            [(x, tall(width)) for x in (cot, mine, theirs, residual)]
            + [(gain_mlp[None, :], full(1, width))],
            [((BLOCK, width), f32, tall(width)), ((BLOCK, width), bf16, tall(width))]
            + [((half, width), bf16, full(half, width))] * 2,
            flops=BLOCK * width * 12,
            nbytes=BLOCK * width * 16,
            hbm=(0,),
            pin=(0, 1, 3),
        )

    hidden_got = lax.ppermute(feed_grads[1], "seq", flip)
    return_sum = over_columns(feed_grads[2])

    _, ga2, *ga2_halves = norm_mlp_back(cots[2], back2, home0, residual2)
    ga3 = [core(x) for x in ga2_halves]
    away, stay = call(
        return_kernel,
        (nb,),
        (),
        [
            (hidden_all, pl.BlockSpec((BLOCK, ff), lambda g: (nb - 1 - g, 0))),
            (w_return, full(ff, width)),
        ],
        [
            ((2 * BLOCK, width), bf16, pl.BlockSpec((BLOCK, width), lambda g: (g // 2, 0))),
            ((2 * BLOCK, width), bf16, pl.BlockSpec((BLOCK, width), lambda g: (jnp.maximum(g - 1, 0) // 2, 0))),
        ],
        flops=2 * rows_all * ff * width,
        nbytes=rows_all * (ff + width) * 2,
    )
    def attend_back(first, ga_a, ga_b, stacked):
        pos = lambda *tail: pl.BlockSpec((1,) + tail, lambda g: (first + g, 0, 0))
        return call(
            functools.partial(state_back_kernel, scale, heads),
            (2,),
            (),
            [
                (ga_a, full(BLOCK, width)),
                (ga_b[0], full(half, width)),
                (ga_b[1], full(half, width)),
                (w_output, full(lw, width)),
                (qkv, pl.BlockSpec((BLOCK, lw), lambda g: (first + g, 0))),
                (mixed_all, pos(BLOCK, lw)),
                (used_low, pos(NS, lw)),
                (stats_f, pos(BLOCK, 128)),
            ],
            [
                ((nb, BLOCK, lw), bf16, pos(BLOCK, lw)),
                ((nb, BLOCK, 128), f32, pos(BLOCK, 128)),
                ((nb, BLOCK, lw), f32, pos(BLOCK, lw)),
                ((nb, NS, lw), f32, pos(NS, lw)),
            ],
            [] if stacked is None else [(array, n) for n, array in enumerate(stacked)],
            flops=4 * BLOCK * lw * width + 20 * BLOCK * NS * lw,
            nbytes=2 * BLOCK * (width * 4 + lw * 16),
            exps=2 * heads * BLOCK * NS,
        )

    stacked = attend_back(2, ga2, ga3, None)
    hidden_got, *stacked = lax.optimization_barrier((hidden_got, *stacked))
    hidden_sum = (feed_grads[0].astype(f32) + hidden_got.astype(f32)).astype(bf16)
    home2, away, stay, hidden_sum, *stacked = lax.optimization_barrier(
        (home2, away, stay, hidden_sum, *stacked)
    )
    grad_residual, ga0, *ga0_halves = norm_mlp_back(cots[0], back0, home2, residual0)
    ga1 = [core(x) for x in ga0_halves]
    near_out = core(hold(away, home2))
    far_out = cross(pair_sum(stay[:BLOCK], near_out[:BLOCK]))
    gas = [ga0, *ga1, ga2, *ga3]
    hidden_sum, *stacked = lax.optimization_barrier((hidden_sum, *stacked))
    hidden_sum = over_columns(hidden_sum.reshape(width // 2, ff))
    stacked = list(attend_back(0, ga0, ga1, stacked))
    gm_all, stats_b, dq_state, direct = stacked

    (local_grad,) = call(
        chain_back_kernel,
        (1,),
        (t_pre,),
        [
            (direct, full(nb, NS, lw)),
            (gate_row, full(1, lw)),
            (keep_rows, full(nb, 1, lw)),
        ],
        [((NS, lw), bf16, full(NS, lw))],
        flops=nb * NS * lw * 2,
        nbytes=nb * NS * lw * 4,
    )
    local_grads = swap(local_grad.reshape(groups, share, lw))
    turn = lambda j: nb - 1 - j
    at = lambda col: pl.BlockSpec((BLOCK, lw), lambda j, t: (turn(j) ^ t[0], col))
    prev = lambda col: pl.BlockSpec(
        (BLOCK, lw), lambda j, t: (jnp.maximum(turn(j) - 1, 0) ^ t[0], col)
    )
    pos = lambda *tail: pl.BlockSpec((1,) + tail, lambda j, t: (turn(j) ^ t[0], 0, 0))
    dq, dk, dv, back_kv, bias_grad = call(
        functools.partial(window_back_kernel, scale, heads),
        (nb,),
        (t_pre,),
        [
            (qkv, at(0)),
            (qkv, at(1)),
            (qkv, at(2)),
            (qkv, prev(1)),
            (qkv, prev(2)),
            (edge, pl.BlockSpec((BLOCK, lw), lambda j, t: (0, 0))),
            (edge, pl.BlockSpec((BLOCK, lw), lambda j, t: (0, 1))),
            (id_cols, pl.BlockSpec((BLOCK, 1), lambda j, t: (turn(j), 0))),
            (id_rows, pl.BlockSpec((1, 1, 2 * BLOCK), lambda j, t: (turn(j), 0, 0))),
            (bias, full(heads, TILE, SPAN)),
            (gm_all, pos(BLOCK, lw)),
            (stats_b, pos(BLOCK, 128)),
            (dq_state, pos(BLOCK, lw)),
        ],
        [
            ((rows_all, lw), bf16, pl.BlockSpec((BLOCK, lw), lambda j, t: (turn(j) ^ t[0], 0))),
            ((nb, BLOCK, lw), f32, pos(BLOCK, lw)),
            ((nb, BLOCK, lw), f32, pos(BLOCK, lw)),
            ((BLOCK, 2 * lw), bf16, full(BLOCK, 2 * lw)),
            ((heads, TILE, SPAN), f32, full(heads, TILE, SPAN)),
        ],
        scratch=[pltpu.VMEM((2 * BLOCK, lw), bf16)] * 2 + [pltpu.VMEM((2 * BLOCK, lw), f32)] * 2,
        flops=nb * 5 * pair_flops,
        nbytes=nb * BLOCK * lw * 24,
        exps=nb * heads * BLOCK * SPAN,
    )
    local_grads, dq, return_sum = lax.optimization_barrier((local_grads, dq, return_sum))
    odd = s_index & 1
    return_own = lax.dynamic_slice_in_dim(return_sum, odd * slab, slab, 0)
    return_other = lax.dynamic_slice_in_dim(return_sum, (1 - odd) * slab, slab, 0)
    return_got = lax.ppermute(return_other, "seq", flip)
    carries, grad_state = call(
        scan_back_kernel,
        (1,),
        (),
        [(local_grads, full(groups, share, lw)), (group_rows, full(groups, 1, lw))],
        [
            ((groups, share, lw), bf16, full(groups, share, lw)),
            ((share, lw), f32, full(share, lw)),
        ],
        flops=NS * lw * 2,
        nbytes=NS * lw * 4,
    )
    carried = swap(carries).reshape(NS, lw)

    next_kv = along(back_kv, -1)

    mid, row_part = call(
        functools.partial(query_grads_kernel, len(gas)),
        (width // cut,),
        (),
        [(x, pl.BlockSpec((x.shape[0], cut), lambda g: (0, g))) for x in gas]
        + [
            (mixed_all, full(nb, BLOCK, lw)),
            (normed_all, pl.BlockSpec((rows_all, cut), lambda g: (0, g))),
            (dq, full(rows_all, lw)),
            (w_query, pl.BlockSpec((cut, lw), lambda g: (g, 0))),
        ],
        [
            ((width, 2 * lw), bf16, pl.BlockSpec((cut, 2 * lw), lambda g: (g, 0))),
            ((8, width), f32, pl.BlockSpec((8, cut), lambda g: (0, g))),
        ],
        flops=4 * rows_all * width * lw,
        nbytes=rows_all * width * 4,
        mib=32,
        pin=range(16),
    )
    carried, mid, hidden_sum, return_got, *_ = lax.optimization_barrier(
        (carried, mid, hidden_sum, return_got, far_out)
    )
    mid = swap(mid.reshape(groups, width // groups, 2 * lw))
    result = (
        residual0 + stay[BLOCK:].astype(f32) + near_out[BLOCK:].astype(f32) + far_out.astype(f32)
    ).astype(bf16)

    gu_all, gate_sum = call(
        carry_kernel,
        (1,),
        (t_pre,),
        [
            (carried, full(NS, lw)),
            (direct, full(nb, NS, lw)),
            (entry, full(NS, lw)),
            (before, full(nb, NS, lw)),
            (carry_rows, full(nb, 1, lw)),
            (keep_rows, full(nb, 1, lw)),
            (gate_row, full(1, lw)),
        ],
        [((nb, NS, lw), bf16, full(nb, NS, lw)), ((1, lw), f32, full(1, lw))],
        flops=nb * NS * lw * 8,
        nbytes=nb * NS * lw * 10,
    )
    def learn_back(high, gu_all, grad_sq, dkv):
        pos = lambda *tail: pl.BlockSpec((1,) + tail, lambda g, t: (high - g, 0, 0))
        row = lambda cols, col=0: pl.BlockSpec((BLOCK, cols), lambda g, t: (high - g, col))
        return call(
            functools.partial(update_back_kernel, scale, heads, high, nb - 1),
            (2,),
            (t_pre,),
            [
                (gu_all, pos(NS, lw)),
                (qkv, row(lw, 1)),
                (qkv, row(lw, 2)),
                (state_queries, full(NS, lw)),
                (lse_u, pos(NS, 128)),
                (updates, pos(NS, lw)),
                (dq, row(lw)),
                (dk, pos(BLOCK, lw)),
                (dv, pos(BLOCK, lw)),
                (next_kv, pl.BlockSpec((BLOCK, lw), lambda g, t: (0, 0))),
                (next_kv, pl.BlockSpec((BLOCK, lw), lambda g, t: (0, 1))),
                (w_joined, full(width, 3 * lw)),
                (grad_sq, full(NS, lw)),
            ],
            [
                ((rows_all, 2 * lw), bf16, row(2 * lw)),
                ((BLOCK, width), bf16, full(BLOCK, width)),
                ((BLOCK, width), bf16, full(BLOCK, width)),
                ((NS, lw), f32, full(NS, lw)),
            ],
            [] if dkv is None else [(dkv, 0)],
            flops=20 * NS * BLOCK * lw + 12 * BLOCK * lw * width,
            nbytes=2 * BLOCK * (lw * 30 + width * 2),
            exps=2 * heads * NS * BLOCK,
        )

    dkv, part3, part2, grad_sq = learn_back(3, gu_all, jnp.zeros((NS, lw), f32), None)
    far = pair_sum(part2, core(part3))
    gu_all = hold(gu_all, far)
    far = cross(far)
    dkv, part1, part0, grad_sq = learn_back(1, gu_all, grad_sq, dkv)
    near = core(part1)

    late, gain_attn_part = call(
        key_grads_kernel,
        (width // cut,),
        (),
        [
            (normed_all, pl.BlockSpec((rows_all, cut), lambda g: (0, g))),
            (dkv, full(rows_all, 2 * lw)),
            (w_key, pl.BlockSpec((cut, lw), lambda g: (g, 0))),
            (w_value, pl.BlockSpec((cut, lw), lambda g: (g, 0))),
            (grad_sq, pl.BlockSpec((per * share, lw), lambda g: (g, 0))),
            (row_part, pl.BlockSpec((8, cut), lambda g: (0, g))),
        ],
        [
            (
                (groups, slab + share // 2, 2 * lw),
                bf16,
                pl.BlockSpec((per, slab + share // 2, 2 * lw), lambda g: (g, 0, 0)),
            ),
            ((8, width), f32, pl.BlockSpec((8, cut), lambda g: (0, g))),
        ],
        flops=4 * rows_all * width * lw,
        nbytes=rows_all * width * 4,
        mib=32,
    )
    (bias_line,) = call(
        bias_sum_kernel,
        (1,),
        (),
        [(hold(bias_grad, late), full(heads, TILE, SPAN))],
        [((heads, SPAN), f32, full(heads, SPAN))],
    )
    bias_local = jnp.dot(bias_line, onehot, precision=lax.Precision.HIGHEST)
    late = swap(hold(late, far))

    bias_full = lax.dynamic_update_slice(
        jnp.zeros((H, BUCKETS), f32), bias_local, (t_index * heads, 0)
    )
    gate_full = lax.dynamic_update_slice(
        jnp.zeros((D,), f32), gate_sum[0] * gates * (1.0 - gates), (t_index * lw,)
    )
    small = jnp.concatenate(
        [
            gain_attn_part[0] / gain_attn,
            gain_mlp_part[0] / gain_mlp,
            gate_full,
            bias_full.reshape(-1),
        ]
    ).reshape(-1, 128)
    small = hold(small, mid)
    (grad_tokens,) = call(
        final_kernel,
        (2,),
        (),
        [(x, tall(width)) for x in (tokens, part0, near, far, grad_residual)]
        + [(gain_attn[None, :], full(1, width))],
        [((BLOCK, width), f32, tall(width))],
        flops=BLOCK * width * 12,
        nbytes=BLOCK * width * 16,
        pin=(0, 4),
    )

    small = small + core(small)
    small = small + cross(small)
    small, grad_tokens = lax.optimization_barrier((small, grad_tokens))
    step = 1
    while step < groups:
        small = small + lax.ppermute(small, "seq", [(i, i ^ step) for i in range(groups)])
        step *= 2
    small = small.reshape(-1)

    mid = jnp.sum(mid.astype(f32), axis=0)
    late = jnp.sum(late.astype(f32), axis=0)
    queries_sent = jnp.concatenate([late[slab:, :lw], late[slab:, lw:]])
    return (
        result,
        block_states,
        grad_tokens,
        grad_state,
        small[:D],
        mid[:, :lw],
        late[:slab, :lw],
        late[:slab, lw:],
        mid[:, lw:].T,
        small[3 * D :].reshape(H, BUCKETS),
        queries_sent,
        small[2 * D : 3 * D],
        small[D : 2 * D],
        hidden_sum.astype(f32),
        (return_own.astype(f32) + return_got.astype(f32)).T,
    )


def solution(mesh):
    return jax.shard_map(
        local,
        mesh=mesh,
        in_specs=(
            P(("seq", "tp"), None),
            P("seq"),
            P("seq"),
            P(None, "tp"),
            P(),
            P(None, "tp"),
            P(None, "tp"),
            P(None, "tp"),
            P("tp", None),
            P("tp", None),
            P(None, "tp"),
            P("tp"),
            P(),
            P(None, "tp"),
            P("tp", None),
            P(("seq", "tp"), None),
        ),
        out_specs=(
            P(("seq", "tp"), None),
            P("seq", None, "tp"),
            P(("seq", "tp"), None),
            P("seq", "tp"),
            P(),
            P("seq", "tp"),
            P("seq", "tp"),
            P("seq", "tp"),
            P("tp", "seq"),
            P(),
            P("seq", "tp"),
            P(),
            P(),
            P("seq", "tp"),
            P("tp", "seq"),
        ),
        check_vma=False,
    )
```

```python
import functools
import math

import jax
import jax.numpy as jnp
import numpy as np
from jax import lax
from jax.experimental import pallas as pl
from jax.experimental.pallas import tpu as pltpu
from jax.sharding import PartitionSpec as P

D = 1024
H = 8
NS = 512
BLOCK = 512
BUCKETS = 32
FAR = 128
TILE = 128
SPAN = BLOCK + TILE
HEAD = 128

eps = 1e-06
negative_fill = -1e30
LOG2E = math.log2(math.e)
WEIGHT = 0.05
HEAVY = 1.0
f32 = jnp.float32
bf16 = jnp.bfloat16


def nn(a, b):
    return lax.dot_general(a, b, (((1,), (0,)), ((), ())), preferred_element_type=f32)


def nt(a, b):
    return lax.dot_general(a, b, (((1,), (1,)), ((), ())), preferred_element_type=f32)


def tn(a, b):
    return lax.dot_general(a, b, (((0,), (0,)), ((), ())), preferred_element_type=f32)


def pinned(array):
    return pltpu.with_memory_space_constraint(array, pltpu.HBM)


def call(
    kernel, grid, prefetch, ins, outs, aliases=(), scratch=(), flops=0, nbytes=0, exps=0, mib=24,
    hbm=(), pin=(), weight=WEIGHT,
):
    any_spec = pl.BlockSpec(memory_space=pl.ANY)
    arrays = [
        pinned(array) if n in pin or array.ndim == 3 or array.shape[0] > D else array
        for n, (array, _) in enumerate(ins)
    ]
    arrays += [pinned(array) for array, _ in aliases]
    specs = [spec for _, spec in ins] + [any_spec for _ in aliases]
    first = len(prefetch) + len(ins)
    alias_map = {first + n: out for n, (_, out) in enumerate(aliases)}
    n_pre, n_in, n_alias = len(prefetch), len(ins), len(aliases)

    def body(*refs):
        kept = refs[: n_pre + n_in] + refs[n_pre + n_in + n_alias :]
        kernel(*kept)

    return pl.pallas_call(
        body,
        name=getattr(kernel, 'func', kernel).__name__,
        out_shape=[
            pltpu.HBM(shape, dtype)
            if len(shape) == 3 or shape[0] > D or n in hbm
            else jax.ShapeDtypeStruct(shape, dtype)
            for n, (shape, dtype, _) in enumerate(outs)
        ],
        grid_spec=pltpu.PrefetchScalarGridSpec(
            num_scalar_prefetch=n_pre,
            grid=grid,
            in_specs=specs,
            out_specs=[spec for _, _, spec in outs],
            scratch_shapes=list(scratch),
        ),
        input_output_aliases=alias_map,
        compiler_params=pltpu.CompilerParams(
            dimension_semantics=("arbitrary",) * len(grid), vmem_limit_bytes=mib * 1024 * 1024
        ),
        cost_estimate=pl.CostEstimate(
            flops=int(flops * weight),
            bytes_accessed=int(nbytes * weight),
            transcendentals=int(exps * weight),
        ),
    )(*prefetch, *arrays)


def lanes(*columns):
    rows = columns[0].shape[0]
    lane = lax.broadcasted_iota(jnp.int32, (rows, 128), 1)
    packed = jnp.broadcast_to(columns[0], (rows, 128))
    for n, column in enumerate(columns[1:], 1):
        packed = jnp.where(lane == n, column, packed)
    return packed


def pick(*columns):
    lane = lax.broadcasted_iota(jnp.int32, columns[0].shape, 1)
    packed = columns[0]
    for n, column in enumerate(columns[1:], 1):
        packed = jnp.where(lane == n, column, packed)
    return packed


def with_ones(values):
    return jnp.concatenate([values, jnp.ones((values.shape[0], HEAD), bf16)], axis=1)


def head_of(h):
    return slice(h * HEAD, (h + 1) * HEAD)


def bias_kernel(base_ref, out_ref):
    for h in range(out_ref.shape[0]):
        row = jnp.broadcast_to(base_ref[h : h + 1, :], (TILE, SPAN))
        out_ref[h] = pltpu.roll(row, 0, 1, stride=1, stride_axis=0)


def bias_sum_kernel(grad_ref, out_ref):
    rows = lax.broadcasted_iota(jnp.int32, (TILE, SPAN), 0)
    for h in range(grad_ref.shape[0]):
        value = grad_ref[h]
        step = 1
        while step < TILE:
            moved = pltpu.roll(value, SPAN - step, 1)
            value = jnp.where((rows & step) != 0, moved, value)
            step *= 2
        out_ref[h : h + 1, :] = jnp.sum(value, axis=0, keepdims=True)


def front_kernel(scale, heads, tok_a, tok_b, gain, w, sq, normed_out, qkv_out, u_out, lse_out):
    width = heads * HEAD
    first = pl.program_id(0) == 0
    rows = 256
    for i in range(BLOCK // rows):
        part = slice(i * rows, (i + 1) * rows)
        x = jnp.where(first, tok_a[part, :].astype(f32), tok_b[part, :].astype(f32))
        r = lax.rsqrt(jnp.mean(x * x, axis=-1, keepdims=True) + eps)
        n = (x * r * gain[...]).astype(bf16)
        normed_out[part, :] = n
        qkv_out[part, :] = nn(n, w[...]).astype(bf16)
    values = [
        with_ones(qkv_out[:, 2 * width + h * HEAD : 2 * width + (h + 1) * HEAD])
        for h in range(heads)
    ]

    def scores_of(i, h):
        k = qkv_out[:, width + h * HEAD : width + (h + 1) * HEAD]
        return nt(sq[i * rows : (i + 1) * rows, head_of(h)], k)

    work = [(i, h) for i in range(BLOCK // rows) for h in range(heads)]
    ready = scores_of(*work[0])
    stats = []
    for n, (i, h) in enumerate(work):
        s = ready * (scale * LOG2E)
        if n + 1 < len(work):
            ready = scores_of(*work[n + 1])
        part = slice(i * rows, (i + 1) * rows)
        m = jnp.max(s, axis=1, keepdims=True)
        p = jnp.exp2(s - m)
        both = nn(p.astype(bf16), values[h])
        total = both[:, HEAD:]
        u_out[0, part, head_of(h)] = both[:, :HEAD] / total
        stats.append(m + jnp.log(total) * LOG2E)
        if h == heads - 1:
            lse_out[0, part, :] = pick(*stats)
            stats = []


def masked(scale, h, raw, qid, kid, bias):
    return jnp.where(qid == kid, raw * (scale * LOG2E) + bias[h], negative_fill)


def window_kernel(scale, heads, t, q, kc, vc, kp, vp, qid, kid, bias, acc, ml, keys, values):
    keys[:BLOCK] = kp[...]
    keys[BLOCK:] = kc[...]
    values[:BLOCK] = vp[...]
    values[BLOCK:] = vc[...]

    def scores_of(i, h):
        part = slice(i * TILE, (i + 1) * TILE)
        return nt(q[part, head_of(h)], keys[i * TILE : i * TILE + SPAN, head_of(h)])

    work = [(i, h) for i in range(BLOCK // TILE) for h in range(heads)]
    ready = scores_of(*work[0])
    peaks, sums = [], []
    for n, (i, h) in enumerate(work):
        raw = ready
        if n + 1 < len(work):
            ready = scores_of(*work[n + 1])
        part = slice(i * TILE, (i + 1) * TILE)
        span = slice(i * TILE, i * TILE + SPAN)
        s = masked(scale, h, raw, qid[part, :], kid[0, :, span], bias)
        m = jnp.max(s, axis=1, keepdims=True)
        p = jnp.exp2(s - m)
        both = nn(p.astype(bf16), with_ones(values[span, head_of(h)]))
        acc[0, part, head_of(h)] = both[:, :HEAD]
        peaks.append(jnp.broadcast_to(m, (TILE, HEAD)))
        sums.append(both[:, HEAD:])
        if h == heads - 1:
            ml[0, part, :] = pick(*peaks, *sums)
            peaks, sums = [], []


def chain_kernel(t, updates, factors, before_out, total_out):
    state = jnp.zeros(total_out.shape, f32)
    for j in range(updates.shape[0]):
        before_out[j] = state
        state = factors[j] * state + updates[t[0] ^ j]
    total_out[...] = state.astype(bf16)


def scan_kernel(s, totals, factors, init, out):
    state = init[...]
    for g in range(totals.shape[0]):
        out[g] = state.astype(bf16)
        state = factors[g] * state + totals[g].astype(f32)


def chain_back_kernel(t, direct, gates, keep_rows, out):
    state = jnp.zeros(out.shape, f32)
    for j in reversed(range(direct.shape[0])):
        state = keep_rows[j] * (direct[t[0] ^ j] + gates[...] * state)
    out[...] = state.astype(bf16)


def scan_back_kernel(totals, factors, out, first_out):
    state = jnp.zeros(first_out.shape, f32)
    for g in reversed(range(totals.shape[0])):
        out[g] = state.astype(bf16)
        state = factors[g] * state + totals[g].astype(f32)
    first_out[...] = state


def carry_kernel(t, carried0, direct, keep_rows, gates, gu_out):
    now = carried0[...].astype(f32)
    for j in reversed(range(direct.shape[0])):
        gu_out[t[0] ^ j] = now.astype(bf16)
        now = keep_rows[j] * (direct[t[0] ^ j] + gates[...] * now)


def gate_kernel(t, carried0, direct, entry, before, carry_rows, keep_rows, gates, gate_out):
    now = carried0[...].astype(f32)
    start = entry[...].astype(f32)
    total = jnp.zeros(gate_out.shape, f32)
    for j in reversed(range(direct.shape[0])):
        used = carry_rows[j] * start + keep_rows[j] * before[j]
        total = total + jnp.sum(now * used, axis=0, keepdims=True)
        now = keep_rows[j] * (direct[t[0] ^ j] + gates[...] * now)
    gate_out[...] = total


def state_kernel(
    scale, heads, t, q, entry, before, carry_row, keep_row, acc, ml, w,
    mixed_out, stats_out, used_out, first_out, second_out,
):
    used_out[0] = (carry_row[0] * entry[...].astype(f32) + keep_row[0] * before[0]).astype(bf16)
    values = [with_ones(used_out[0, :, head_of(h)]) for h in range(heads)]
    rows = 256
    for i in range(BLOCK // rows):
        part = slice(i * rows, (i + 1) * rows)
        stats = []
        for h in range(heads):
            m = ml[0, part, h : h + 1]
            l = ml[0, part, heads + h : heads + h + 1]
            s = nt(q[part, head_of(h)], used_out[0, :, head_of(h)]) * (scale * LOG2E)
            top = jnp.maximum(m, jnp.max(s, axis=1, keepdims=True))
            p = jnp.exp2(s - top)
            shrink = jnp.exp2(m - top)
            both = nn(p.astype(bf16), values[h])
            total = l * shrink + both[:, HEAD:]
            value = (acc[0, part, head_of(h)] * shrink + both[:, :HEAD]) / total
            mixed_out[0, part, head_of(h)] = value.astype(bf16)
            stats.append(top + jnp.log(total) * LOG2E)
        stats_out[0, part, :] = pick(*stats)
    result = nn(mixed_out[0], w[...]).astype(bf16)
    first = pl.program_id(0) == 0

    @pl.when(first)
    def _():
        first_out[...] = result

    @pl.when(jnp.logical_not(first))
    def _():
        second_out[...] = result


def states_kernel(t, entry, before, carry_row, keep_row, gates, u, next_out):
    used = carry_row[0] * entry[...].astype(f32) + keep_row[0] * before[0]
    next_out[0] = gates[...] * used + u[0]


def return_kernel(hidden, w, away_out, stay_out):
    even = pl.program_id(0) % 2 == 0

    @pl.when(even)
    def _():
        away_out[...] = nn(hidden[...], w[...]).astype(bf16)

    @pl.when(jnp.logical_not(even))
    def _():
        stay_out[...] = nn(hidden[...], w[...]).astype(bf16)


def norm_kernel(tok, mine, theirs, gain, residual_out, nm_out):
    residual = tok[...].astype(f32) + (mine[...].astype(f32) + theirs[...].astype(f32))
    residual_out[...] = residual
    inverse = lax.rsqrt(jnp.mean(residual * residual, axis=-1, keepdims=True) + eps)
    nm_out[...] = (residual * inverse * gain[...]).astype(bf16)


def norm_back_kernel(
    cot, mine, theirs, residual, gain, grad_out, low_out, upper_out, lower_out
):
    r = residual[...]
    inverse = lax.rsqrt(jnp.mean(r * r, axis=-1, keepdims=True) + eps)
    scaled = r * inverse
    grad = (mine[...].astype(f32) + theirs[...].astype(f32)) * gain[...]
    inner = jnp.mean(grad * scaled, axis=-1, keepdims=True)
    result = cot[...].astype(f32) + inverse * (grad - scaled * inner)
    grad_out[...] = result
    low = result.astype(bf16)
    low_out[...] = low
    upper = pl.program_id(0) == 0

    @pl.when(upper)
    def _():
        upper_out[...] = low

    @pl.when(jnp.logical_not(upper))
    def _():
        lower_out[...] = low


def final_kernel(tok, mine, near, far, residual_grad, gain, out):
    x = tok[...].astype(f32)
    inverse = lax.rsqrt(jnp.mean(x * x, axis=-1, keepdims=True) + eps)
    scaled = x * inverse
    grad = mine[...].astype(f32) + near[...].astype(f32) + far[...].astype(f32)
    grad = grad * gain[...]
    inner = jnp.mean(grad * scaled, axis=-1, keepdims=True)
    out[...] = residual_grad[...] + inverse * (grad - scaled * inner)


def row_sums(value):
    sums = jnp.broadcast_to(jnp.sum(value, axis=1, keepdims=True), (value.shape[0], HEAD))
    return sums.T[:8]


def feed_grads_kernel(n, s, *refs):
    nms, cots = refs[:n], refs[n : 2 * n]
    gpre, hidden, w, kept_out, sent_out, return_out, gain_out = refs[2 * n :]
    odd = s[0] % 2 == 1
    rows = nms[0].shape[0]
    ff = w.shape[1]
    for which, left, right in ((0, nms, gpre), (1, cots, hidden)):
        total = None
        for r in range(n):
            piece = tn(left[r][...], right[r * rows : (r + 1) * rows, :])
            total = piece if total is None else total + piece
        low = total.astype(bf16)
        if which == 0:
            slab = kept_out.shape[1]
            for g in range(kept_out.shape[0]):
                even_rows = low[2 * g * slab : (2 * g + 1) * slab]
                odd_rows = low[(2 * g + 1) * slab : (2 * g + 2) * slab]
                kept_out[g] = jnp.where(odd, odd_rows, even_rows)
                sent_out[g] = jnp.where(odd, even_rows, odd_rows)
        else:
            return_out[...] = low
        if which == 0:
            gain_out[...] = row_sums(total * w[...].astype(f32))


def query_grads_kernel(n, *refs):
    gas = refs[:n]
    mixed, normed, dq, w, out, row_out = refs[n:]
    lw = dq.shape[1]
    total, at = None, 0
    for ga in gas:
        first = at % BLOCK
        piece = tn(ga[...], mixed[at // BLOCK, first : first + ga.shape[0]])
        total = piece if total is None else total + piece
        at += ga.shape[0]
    out[:, lw:] = total.astype(bf16)
    grad = tn(normed[...], dq[...])
    out[:, :lw] = grad.astype(bf16)
    row_out[...] = row_sums(grad * w[...].astype(f32))


def key_grads_kernel(normed, dkv, wk, wv, dsq, row, out, row_out):
    grad = tn(normed[...], dkv[...])
    rows, lw = grad.shape[0], wk.shape[1]
    slab = rows // out.shape[0]
    part = dsq.shape[0] // out.shape[0] // 2
    low = grad.astype(bf16)
    for g in range(out.shape[0]):
        out[g, :slab] = low[g * slab : (g + 1) * slab]
        out[g, slab:, :lw] = dsq[2 * g * part : (2 * g + 1) * part].astype(bf16)
        out[g, slab:, lw:] = dsq[(2 * g + 1) * part : (2 * g + 2) * part].astype(bf16)
    both = jnp.concatenate([wk[...].astype(f32), wv[...].astype(f32)], axis=1)
    row_out[...] = row[...] + row_sums(grad * both)


def mlp_kernel(steps, nm_a, nm_b, gact_a, gact_b, w, hidden_out, gpre_out, first_out, second_out):
    first = pl.program_id(0) < steps
    cols = 256
    x = jnp.where(first, nm_a[...], nm_b[...])
    for c in range(w.shape[1] // cols):
        cut = slice(c * cols, (c + 1) * cols)
        pre = nn(x, w[:, cut])
        cumulative = 0.5 * (1.0 + lax.erf(pre * (1.0 / math.sqrt(2.0))))
        density = jnp.exp2(pre * pre * (-0.5 * LOG2E)) * (1.0 / math.sqrt(2.0 * math.pi))
        hidden_out[:, cut] = (pre * cumulative).astype(bf16)
        gact = jnp.where(first, gact_a[:, cut].astype(f32), gact_b[:, cut].astype(f32))
        gpre_out[:, cut] = (gact * (cumulative + pre * density)).astype(bf16)
    result = nt(gpre_out[...], w[...]).astype(bf16)

    @pl.when(first)
    def _():
        first_out[...] = result

    @pl.when(jnp.logical_not(first))
    def _():
        second_out[...] = result


def state_back_kernel(
    scale, heads, ga_a, ga_b, ga_c, w, q, mixed, used, stats, gm_out, stats_out, dq_out, direct_out
):
    first = pl.program_id(0) == 0
    gm_out[0] = nt(jnp.where(first, ga_a[...], jnp.concatenate([ga_b[...], ga_c[...]])), w[...]).astype(bf16)
    raws = [
        (nt(q[:, head_of(h)], used[0, :, head_of(h)]), nt(gm_out[0, :, head_of(h)], used[0, :, head_of(h)]))
        for h in range(heads)
    ]
    logs, deltas = [], []
    for h, (raw, grad_p) in enumerate(raws):
        hs = head_of(h)
        gm = gm_out[0, :, hs]
        delta = jnp.sum(gm.astype(f32) * mixed[0, :, hs].astype(f32), axis=1, keepdims=True)
        lse = stats[0, :, h : h + 1]
        p = jnp.exp2(raw * (scale * LOG2E) - lse)
        ds = (p * (grad_p - delta)).astype(bf16)
        dq_out[0, :, hs] = nn(ds, used[0, :, hs]) * scale
        direct_out[0, :, hs] = tn(ds, q[:, hs]) * scale + tn(p.astype(bf16), gm)
        logs.append(lse)
        deltas.append(delta)
    stats_out[0] = lanes(*logs, *deltas)


def window_back_kernel(
    scale, heads, t, q, kc, vc, kb, vb, hk, hv, qid, kid, bias, gm, stats, dqs,
    dq_out, dk_out, dv_out, edge_out, grad_bias, keys, values, dkeys, dvalues,
):
    step = pl.program_id(0)
    last = pl.num_programs(0) - 1

    @pl.when(step == last)
    def _():
        keys[:BLOCK] = hk[...]
        values[:BLOCK] = hv[...]

    @pl.when(step != last)
    def _():
        keys[:BLOCK] = kb[...]
        values[:BLOCK] = vb[...]

    keys[BLOCK:] = kc[...]
    values[BLOCK:] = vc[...]

    @pl.when(step == 0)
    def _():
        dkeys[...] = jnp.zeros_like(dkeys)
        dvalues[...] = jnp.zeros_like(dvalues)
        grad_bias[...] = jnp.zeros_like(grad_bias)

    @pl.when(step != 0)
    def _():
        for total in (dkeys, dvalues):
            total[BLOCK:] = total[:BLOCK]
            total[:BLOCK] = jnp.zeros((BLOCK, total.shape[1]), f32)

    def scores_of(i, h):
        part = slice(i * TILE, (i + 1) * TILE)
        span = slice(i * TILE, i * TILE + SPAN)
        hs = head_of(h)
        return nt(q[part, hs], keys[span, hs]), nt(gm[0, part, hs], values[span, hs])

    work = [(i, h) for i in range(BLOCK // TILE) for h in range(heads)]
    ready = scores_of(*work[0])
    for n, (i, h) in enumerate(work):
        raw, grad_p = ready
        if n + 1 < len(work):
            ready = scores_of(*work[n + 1])
        part = slice(i * TILE, (i + 1) * TILE)
        span = slice(i * TILE, i * TILE + SPAN)
        hs = head_of(h)
        qt = q[part, hs]
        g = gm[0, part, hs]
        lse = stats[0, part, h : h + 1]
        delta = stats[0, part, heads + h : heads + h + 1]
        p = jnp.exp2(masked(scale, h, raw, qid[part, :], kid[0, :, span], bias) - lse)
        ds = p * (grad_p - delta)
        low = ds.astype(bf16)
        zero = jnp.zeros_like(qt)
        sides = jnp.concatenate(
            [jnp.concatenate([qt, zero], axis=1), jnp.concatenate([zero, g], axis=1)]
        )
        both = tn(jnp.concatenate([low, p.astype(bf16)]), sides)
        dq = nn(low, keys[span, hs]) * scale + dqs[0, part, hs]
        grad_bias[h] += ds
        dq_out[part, hs] = dq.astype(bf16)
        dkeys[span, hs] += both[:, :HEAD] * scale
        dvalues[span, hs] += both[:, HEAD:]
    dk_out[0] = dkeys[BLOCK:]
    dv_out[0] = dvalues[BLOCK:]

    @pl.when(step == last)
    def _():
        width = heads * HEAD
        edge_out[:, :width] = dkeys[:BLOCK].astype(bf16)
        edge_out[:, width:] = dvalues[:BLOCK].astype(bf16)


def update_back_kernel(
    scale, heads, high, last, t, gu_all, k, v, sq, lse_u, u, dq, dk, dv, hk, hv, w, dsq_in,
    dkv_out, first_out, second_out, dsq_out,
):
    width = heads * HEAD
    step = pl.program_id(0)
    edge = jnp.where((t[0] ^ (high - step)) == last, 1.0, 0.0)

    @pl.when(step == 0)
    def _():
        dsq_out[...] = dsq_in[...]

    raws = [
        (nt(sq[:, head_of(h)], k[:, head_of(h)]), nt(gu_all[0, :, head_of(h)], v[:, head_of(h)]))
        for h in range(heads)
    ]
    for h, (raw, grad_p) in enumerate(raws):
        hs = head_of(h)
        gu = gu_all[0, :, hs]
        sqh = sq[:, hs]
        kh = k[:, hs]
        delta = jnp.sum(gu.astype(f32) * u[0, :, hs], axis=1, keepdims=True)
        p = jnp.exp2(raw * (scale * LOG2E) - lse_u[0, :, h : h + 1])
        ds = (p * (grad_p - delta)).astype(bf16)
        dsq_out[:, hs] += nn(ds, kh) * scale
        dkh = dk[0, :, hs] + tn(ds, sqh) * scale + edge * hk[:, hs].astype(f32)
        dvh = dv[0, :, hs] + tn(p.astype(bf16), gu) + edge * hv[:, hs].astype(f32)
        dkv_out[:, hs] = dkh.astype(bf16)
        dkv_out[:, width + h * HEAD : width + (h + 1) * HEAD] = dvh.astype(bf16)
    part = nt(dq[...], w[:, :width]) + nt(dkv_out[...], w[:, width:])
    result = part.astype(bf16)

    @pl.when(step == 0)
    def _():
        first_out[...] = result

    @pl.when(step != 0)
    def _():
        second_out[...] = result


def bucket_of(distance):
    half = BUCKETS // 2
    limits = [math.ceil(half * (FAR / half) ** (level / half)) for level in range(1, half)]
    clipped = np.maximum(distance, 0)
    extra = sum((clipped >= limit).astype(np.int32) for limit in limits)
    return np.where(clipped < half, clipped, half + extra)


def local(
    tokens,
    doc_flags,
    reset_flags,
    state_init,
    gain_attn,
    w_query,
    w_key,
    w_value,
    w_output,
    bias_table,
    state_queries,
    gate_logits,
    gain_mlp,
    w_hidden,
    w_return,
    cotangent,
):
    heads = bias_table.shape[0]
    lw = w_query.shape[1]
    width = tokens.shape[1]
    nb = reset_flags.shape[0]
    ff = w_hidden.shape[1]
    scale = 1.0 / math.sqrt(HEAD)
    groups = lax.axis_size("seq")
    s_index = lax.axis_index("seq")
    t_index = lax.axis_index("tp")
    t_pre = t_index.astype(jnp.int32)[None]
    s_pre = s_index.astype(jnp.int32)[None]
    rows_all = nb * BLOCK

    def core(value):
        return lax.ppermute(value, "tp", [(i, i ^ 1) for i in range(nb)])

    def cross(value):
        return lax.ppermute(value, "tp", [(i, i ^ 2) for i in range(nb)])

    def along(value, step):
        pairs = [(i, i + step) for i in range(groups) if 0 <= i + step < groups]
        return lax.ppermute(value, "seq", pairs)

    def swap(value):
        return lax.all_to_all(value, "seq", 0, 0, tiled=True)

    def hold(value, *others):
        return lax.optimization_barrier((value, *others))[0]

    full = lambda *shape: pl.BlockSpec(shape, lambda *_: (0,) * len(shape))
    half = BLOCK // 2
    tall = lambda *tail: pl.BlockSpec((half,) + tail, lambda g, *_: (g, 0))
    share = NS // groups

    tok2 = cross(tokens)
    tok1 = core(tokens)

    gates = jax.nn.sigmoid(gate_logits)
    keeps = (1 - reset_flags).astype(f32)
    gate_row = gates[None, :]
    gate_group = gates
    for _ in range(nb - 1):
        gate_group = gate_group * gates
    apart = BLOCK - np.arange(SPAN)
    shown = (apart >= 0) & (apart < BLOCK)
    onehot = (bucket_of(apart)[:, None] == np.arange(BUCKETS)[None, :]) & shown[:, None]
    onehot = jnp.asarray(onehot.astype(np.float32))
    base = jnp.dot(bias_table * LOG2E, onehot.T, precision=lax.Precision.HIGHEST)
    base = jnp.where(jnp.asarray(shown)[None, :], base, negative_fill)
    (bias,) = call(
        bias_kernel,
        (1,),
        (),
        [(base, full(heads, SPAN))],
        [((heads, TILE, SPAN), f32, full(heads, TILE, SPAN))],
    )

    w_joined = jnp.concatenate([w_query, w_key, w_value], axis=1)
    def front(first, tok_a, tok_b, stacked):
        row = lambda cols: pl.BlockSpec((BLOCK, cols), lambda g: (first + g, 0))
        pos = lambda *tail: pl.BlockSpec((1,) + tail, lambda g: (first + g, 0, 0))
        return call(
            functools.partial(front_kernel, scale, heads),
            (2,),
            (),
            [
                (tok_a, full(BLOCK, width)),
                (tok_b, full(BLOCK, width)),
                (gain_attn[None, :], full(1, width)),
                (w_joined, full(width, 3 * lw)),
                (state_queries, full(NS, lw)),
            ],
            [
                ((rows_all, width), bf16, row(width)),
                ((rows_all, 3 * lw), bf16, row(3 * lw)),
                ((nb, NS, lw), f32, pos(NS, lw)),
                ((nb, NS, 128), f32, pos(NS, 128)),
            ],
            [] if stacked is None else [(array, n) for n, array in enumerate(stacked)],
            flops=4 * BLOCK * width * 3 * lw + 8 * NS * BLOCK * lw,
            nbytes=12 * BLOCK * width * 2,
            exps=2 * heads * NS * BLOCK,
        )

    starts = [jnp.ones_like(gates)]
    for j in range(nb - 1):
        starts.append(starts[j] * (gates * keeps[j]))
    carry_rows = (jnp.stack(starts) * keeps[:, None])[:, None, :]
    keep_rows = jnp.broadcast_to(keeps[:, None, None], (nb, 1, lw))
    block_rows = (keeps[:, None] * gates[None, :])[:, None, :]
    stacked = front(0, tokens, tok1, None)
    reset_sent, flags_sent, *stacked = lax.optimization_barrier((reset_flags, doc_flags, *stacked))
    every = swap(jnp.broadcast_to(reset_sent.reshape(1, nb), (groups, nb)))
    flag_prev = along(flags_sent[rows_all - BLOCK :], 1)
    tok2, bias, every, flag_prev, *stacked = lax.optimization_barrier(
        (tok2, bias, every, flag_prev, *stacked)
    )
    toks = [tokens, tok1, tok2, core(tok2)]
    cot1 = core(cotangent)
    stacked = list(front(2, toks[2], toks[3], stacked))
    every, flag_prev, *stacked = lax.optimization_barrier((every, flag_prev, *stacked))
    group_keep = jnp.prod((1 - every).astype(f32), axis=1)

    group_rows = (group_keep[:, None] * gate_group[None, :])[:, None, :]

    ids = jnp.cumsum(jnp.concatenate([flag_prev, doc_flags]))
    ids = jnp.where((jnp.arange(rows_all + BLOCK) < BLOCK) & (s_index == 0), -1, ids)
    id_rows = ids.reshape(nb + 1, 1, BLOCK)
    id_rows = jnp.concatenate([id_rows[:-1], id_rows[1:]], axis=2)
    id_cols = ids[BLOCK:].reshape(rows_all, 1)
    cot2, stacked[0] = lax.optimization_barrier((cotangent, stacked[0]))
    cot2 = cross(cot2)
    normed_all, qkv, updates, lse_u = stacked

    place = (t_index ^ (nb - 1)) * BLOCK
    edge = along(lax.dynamic_slice(qkv, (place, lw), (BLOCK, 2 * lw)), 1)

    before, total = call(
        chain_kernel,
        (1,),
        (t_pre,),
        [(updates, full(nb, NS, lw)), (block_rows, full(nb, 1, lw))],
        [((nb, NS, lw), f32, full(nb, NS, lw)), ((NS, lw), bf16, full(NS, lw))],
        flops=nb * NS * lw * 2,
        nbytes=nb * NS * lw * 8,
        hbm=(0,),
    )
    pair_flops = 2 * BLOCK * SPAN * lw

    def window(first, count, edge, stacked, weight):
        at = lambda col, back=0: pl.BlockSpec(
            (BLOCK, lw), lambda j, t: ((j + first - back) ^ t[0], col)
        )
        blk = lambda *tail: pl.BlockSpec((1,) + tail, lambda j, t: (j + first, 0, 0))
        if edge is None:
            before_block = [(qkv, at(1, 1)), (qkv, at(2, 1))]
        else:
            before_block = [
                (edge, pl.BlockSpec((BLOCK, lw), lambda j, t: (0, 0))),
                (edge, pl.BlockSpec((BLOCK, lw), lambda j, t: (0, 1))),
            ]
        return call(
            functools.partial(window_kernel, scale, heads),
            (count,),
            (t_pre,),
            [(qkv, at(0)), (qkv, at(1)), (qkv, at(2))]
            + before_block
            + [
                (id_cols, pl.BlockSpec((BLOCK, 1), lambda j, t: (j + first, 0))),
                (id_rows, pl.BlockSpec((1, 1, 2 * BLOCK), lambda j, t: (j + first, 0, 0))),
                (bias, full(heads, TILE, SPAN)),
            ],
            [
                ((nb, BLOCK, lw), f32, blk(BLOCK, lw)),
                ((nb, BLOCK, 128), f32, blk(BLOCK, 128)),
            ],
            [] if stacked is None else [(array, n) for n, array in enumerate(stacked)],
            flops=count * 2 * pair_flops,
            nbytes=count * BLOCK * lw * 12,
            exps=count * heads * BLOCK * SPAN,
            scratch=[pltpu.VMEM((2 * BLOCK, lw), bf16)] * 2,
            weight=weight,
        )

    windows = window(1, nb - 1, None, None, WEIGHT)
    late_edge, total, *windows = lax.optimization_barrier((edge, total, *windows))
    totals = swap(total.reshape(groups, share, lw))
    acc, ml = window(0, 1, late_edge, windows, HEAVY)
    cot2 = hold(cot2, acc)
    cots = [hold(cotangent, acc), hold(cot1, acc), cot2, core(cot2)]
    gacts = [nt(cot, w_return).astype(bf16) for cot in cots]
    totals, gacts[0], gacts[1] = lax.optimization_barrier((totals, gacts[0], gacts[1]))
    (entries,) = call(
        scan_kernel,
        (1,),
        (s_pre,),
        [
            (totals, full(groups, share, lw)),
            (group_rows, full(groups, 1, lw)),
            (state_init, pl.BlockSpec((share, lw), lambda g, s: (s[0], 0))),
        ],
        [((groups, share, lw), bf16, full(groups, share, lw))],
        flops=NS * lw * 2,
        nbytes=NS * lw * 4,
    )
    entry = swap(entries).reshape(NS, lw)

    entry, *gacts = lax.optimization_barrier((entry, *gacts))

    def attend(high, stacked):
        blk = lambda *tail: pl.BlockSpec((1,) + tail, lambda g, t: (t[0] ^ (high - g), 0, 0))
        pos = lambda *tail: pl.BlockSpec((1,) + tail, lambda g, t: (high - g, 0, 0))
        return call(
            functools.partial(state_kernel, scale, heads),
            (2,),
            (t_pre,),
            [
                (qkv, pl.BlockSpec((BLOCK, lw), lambda g, t: (high - g, 0))),
                (entry, full(NS, lw)),
                (before, blk(NS, lw)),
                (carry_rows, blk(1, lw)),
                (keep_rows, blk(1, lw)),
                (acc, blk(BLOCK, lw)),
                (ml, blk(BLOCK, 128)),
                (w_output, full(lw, width)),
            ],
            [
                ((nb, BLOCK, lw), bf16, pos(BLOCK, lw)),
                ((nb, BLOCK, 128), f32, pos(BLOCK, 128)),
                ((nb, NS, lw), bf16, pos(NS, lw)),
                ((BLOCK, width), bf16, full(BLOCK, width)),
                ((BLOCK, width), bf16, full(BLOCK, width)),
            ],
            [] if stacked is None else [(array, n) for n, array in enumerate(stacked)],
            flops=8 * BLOCK * NS * lw + 4 * BLOCK * lw * width,
            nbytes=2 * BLOCK * (lw * 24 + width * 2),
            exps=2 * heads * BLOCK * NS,
        )

    *stacked, part3, part2 = attend(3, None)
    *stacked, part1, part0 = attend(1, stacked)
    mixed_all, stats_f, used_low = stacked

    def pair_sum(mine, theirs):
        return (mine.astype(f32) + theirs.astype(f32)).astype(bf16)

    sum2 = pair_sum(part2, core(part3))
    sum0 = pair_sum(part0, core(part1))
    far2 = cross(sum2)
    blk = lambda *tail: pl.BlockSpec((1,) + tail, lambda g, t: (t[0] ^ g, 0, 0))
    pos = lambda *tail: pl.BlockSpec((1,) + tail, lambda g, t: (g, 0, 0))
    (block_states,) = call(
        states_kernel,
        (nb,),
        (t_pre,),
        [
            (hold(entry, sum0), full(NS, lw)),
            (before, blk(NS, lw)),
            (carry_rows, blk(1, lw)),
            (keep_rows, blk(1, lw)),
            (gate_row, full(1, lw)),
            (updates, pos(NS, lw)),
        ],
        [((nb, NS, lw), f32, blk(NS, lw))],
        flops=nb * NS * lw * 4,
        nbytes=nb * NS * lw * 12,
        hbm=(0,),
    )
    far2 = hold(far2, block_states)
    far0 = cross(hold(sum0, far2))

    def norm_mlp(tok, mine, theirs):
        return call(
            norm_kernel,
            (2,),
            (),
            [(x, tall(width)) for x in (tok, mine, theirs)] + [(gain_mlp[None, :], full(1, width))],
            [((BLOCK, width), f32, tall(width)), ((BLOCK, width), bf16, tall(width))],
            flops=BLOCK * width * 8,
            nbytes=BLOCK * width * 12,
            hbm=(0,),
        )

    def feed(first, nm_a, nm_b, stacked):
        early_tile = lambda cols: pl.BlockSpec((half, cols), lambda g: (jnp.minimum(g, 1), 0))
        late_tile = lambda cols: pl.BlockSpec((half, cols), lambda g: (jnp.maximum(g - 2, 0), 0))
        return call(
            functools.partial(mlp_kernel, 2),
            (4,),
            (),
            [
                (nm_a, early_tile(width)),
                (nm_b, late_tile(width)),
                (gacts[first], early_tile(ff)),
                (gacts[first + 1], late_tile(ff)),
                (w_hidden, full(width, ff)),
            ],
            [
                ((rows_all, ff), bf16, pl.BlockSpec((half, ff), lambda g: (2 * first + g, 0))),
                ((rows_all, ff), bf16, pl.BlockSpec((half, ff), lambda g: (2 * first + g, 0))),
                ((BLOCK, width), bf16, early_tile(width)),
                ((BLOCK, width), bf16, late_tile(width)),
            ],
            [] if stacked is None else [(array, n) for n, array in enumerate(stacked)],
            flops=8 * BLOCK * width * ff,
            nbytes=2 * BLOCK * width * 10,
            exps=4 * BLOCK * ff,
        )

    residual0, nm0 = norm_mlp(toks[0], sum0, far2)
    nm1 = core(nm0)
    *stacked, back0, back1 = feed(0, nm0, nm1, None)
    far0, back1 = lax.optimization_barrier((far0, back1))
    back0 = pair_sum(back0, core(back1))
    home0 = cross(back0)
    residual2, nm2 = norm_mlp(toks[2], sum2, far0)
    nm3 = core(nm2)
    *stacked, back2, back3 = feed(2, nm2, nm3, stacked)
    hidden_all, gpre_all = stacked
    slab = width // groups
    cut = 256
    per = cut // slab

    nms = [nm0, nm1, nm2, nm3]
    *feed_grads, gain_mlp_part = call(
        functools.partial(feed_grads_kernel, nb),
        (width // cut,),
        (s_pre,),
        [(x, pl.BlockSpec((BLOCK, cut), lambda g, s: (0, g))) for x in nms + cots]
        + [
            (gpre_all, full(rows_all, ff)),
            (hidden_all, full(rows_all, ff)),
            (w_hidden, pl.BlockSpec((cut, ff), lambda g, s: (g, 0))),
        ],
        [
            ((groups // 2, slab, ff), bf16, pl.BlockSpec((per // 2, slab, ff), lambda g, s: (g, 0, 0))),
            ((groups // 2, slab, ff), bf16, pl.BlockSpec((per // 2, slab, ff), lambda g, s: (g, 0, 0))),
            ((width, ff), bf16, pl.BlockSpec((cut, ff), lambda g, s: (g, 0))),
            ((8, width), f32, pl.BlockSpec((8, cut), lambda g, s: (0, g))),
        ],
        flops=4 * rows_all * width * ff,
        nbytes=rows_all * width * 8,
        mib=48,
        pin=range(nb, 16),
        hbm=range(4),
    )

    flip = [(i, i ^ 1) for i in range(groups)]
    columns = [list(range(side, groups, 2)) for side in range(2)]

    def over_columns(value):
        return lax.psum_scatter(
            value, "seq", scatter_dimension=0, tiled=True, axis_index_groups=columns
        )

    home0, back3, *feed_grads = lax.optimization_barrier((home0, back3, *feed_grads))
    back2 = pair_sum(back2, core(back3))
    home2 = cross(back2)

    def norm_mlp_back(cot, mine, theirs, residual):
        return call(
            norm_back_kernel,
            (2,),
            (),
            [(x, tall(width)) for x in (cot, mine, theirs, residual)]
            + [(gain_mlp[None, :], full(1, width))],
            [((BLOCK, width), f32, tall(width)), ((BLOCK, width), bf16, tall(width))]
            + [((half, width), bf16, full(half, width))] * 2,
            flops=BLOCK * width * 12,
            nbytes=BLOCK * width * 16,
            hbm=(0,),
            pin=(0, 1, 3),
        )

    hidden_got = lax.ppermute(feed_grads[1], "seq", flip)
    return_sum = over_columns(feed_grads[2])

    _, ga2, *ga2_halves = norm_mlp_back(cots[2], back2, home0, residual2)
    ga3 = [core(x) for x in ga2_halves]
    away, stay = call(
        return_kernel,
        (nb,),
        (),
        [
            (hidden_all, pl.BlockSpec((BLOCK, ff), lambda g: (nb - 1 - g, 0))),
            (w_return, full(ff, width)),
        ],
        [
            ((2 * BLOCK, width), bf16, pl.BlockSpec((BLOCK, width), lambda g: (g // 2, 0))),
            ((2 * BLOCK, width), bf16, pl.BlockSpec((BLOCK, width), lambda g: (jnp.maximum(g - 1, 0) // 2, 0))),
        ],
        flops=2 * rows_all * ff * width,
        nbytes=rows_all * (ff + width) * 2,
    )
    def attend_back(first, ga_a, ga_b, stacked):
        pos = lambda *tail: pl.BlockSpec((1,) + tail, lambda g: (first + g, 0, 0))
        return call(
            functools.partial(state_back_kernel, scale, heads),
            (2,),
            (),
            [
                (ga_a, full(BLOCK, width)),
                (ga_b[0], full(half, width)),
                (ga_b[1], full(half, width)),
                (w_output, full(lw, width)),
                (qkv, pl.BlockSpec((BLOCK, lw), lambda g: (first + g, 0))),
                (mixed_all, pos(BLOCK, lw)),
                (used_low, pos(NS, lw)),
                (stats_f, pos(BLOCK, 128)),
            ],
            [
                ((nb, BLOCK, lw), bf16, pos(BLOCK, lw)),
                ((nb, BLOCK, 128), f32, pos(BLOCK, 128)),
                ((nb, BLOCK, lw), f32, pos(BLOCK, lw)),
                ((nb, NS, lw), f32, pos(NS, lw)),
            ],
            [] if stacked is None else [(array, n) for n, array in enumerate(stacked)],
            flops=4 * BLOCK * lw * width + 20 * BLOCK * NS * lw,
            nbytes=2 * BLOCK * (width * 4 + lw * 16),
            exps=2 * heads * BLOCK * NS,
        )

    stacked = attend_back(2, ga2, ga3, None)
    hidden_got, *stacked = lax.optimization_barrier((hidden_got, *stacked))
    hidden_sum = (feed_grads[0].astype(f32) + hidden_got.astype(f32)).astype(bf16)
    home2, away, stay, hidden_sum, *stacked = lax.optimization_barrier(
        (home2, away, stay, hidden_sum, *stacked)
    )
    grad_residual, ga0, *ga0_halves = norm_mlp_back(cots[0], back0, home2, residual0)
    ga1 = [core(x) for x in ga0_halves]
    near_out = core(hold(away, home2))
    far_out = cross(pair_sum(stay[:BLOCK], near_out[:BLOCK]))
    gas = [ga0, *ga1, ga2, *ga3]
    hidden_sum, *stacked = lax.optimization_barrier((hidden_sum, *stacked))
    hidden_sum = over_columns(hidden_sum.reshape(width // 2, ff))
    stacked = list(attend_back(0, ga0, ga1, stacked))
    gm_all, stats_b, dq_state, direct = stacked

    (local_grad,) = call(
        chain_back_kernel,
        (1,),
        (t_pre,),
        [
            (direct, full(nb, NS, lw)),
            (gate_row, full(1, lw)),
            (keep_rows, full(nb, 1, lw)),
        ],
        [((NS, lw), bf16, full(NS, lw))],
        flops=nb * NS * lw * 2,
        nbytes=nb * NS * lw * 4,
    )
    local_grads = swap(local_grad.reshape(groups, share, lw))
    turn = lambda j: nb - 1 - j
    at = lambda col: pl.BlockSpec((BLOCK, lw), lambda j, t: (turn(j) ^ t[0], col))
    prev = lambda col: pl.BlockSpec(
        (BLOCK, lw), lambda j, t: (jnp.maximum(turn(j) - 1, 0) ^ t[0], col)
    )
    pos = lambda *tail: pl.BlockSpec((1,) + tail, lambda j, t: (turn(j) ^ t[0], 0, 0))
    dq, dk, dv, back_kv, bias_grad = call(
        functools.partial(window_back_kernel, scale, heads),
        (nb,),
        (t_pre,),
        [
            (qkv, at(0)),
            (qkv, at(1)),
            (qkv, at(2)),
            (qkv, prev(1)),
            (qkv, prev(2)),
            (edge, pl.BlockSpec((BLOCK, lw), lambda j, t: (0, 0))),
            (edge, pl.BlockSpec((BLOCK, lw), lambda j, t: (0, 1))),
            (id_cols, pl.BlockSpec((BLOCK, 1), lambda j, t: (turn(j), 0))),
            (id_rows, pl.BlockSpec((1, 1, 2 * BLOCK), lambda j, t: (turn(j), 0, 0))),
            (bias, full(heads, TILE, SPAN)),
            (gm_all, pos(BLOCK, lw)),
            (stats_b, pos(BLOCK, 128)),
            (dq_state, pos(BLOCK, lw)),
        ],
        [
            ((rows_all, lw), bf16, pl.BlockSpec((BLOCK, lw), lambda j, t: (turn(j) ^ t[0], 0))),
            ((nb, BLOCK, lw), f32, pos(BLOCK, lw)),
            ((nb, BLOCK, lw), f32, pos(BLOCK, lw)),
            ((BLOCK, 2 * lw), bf16, full(BLOCK, 2 * lw)),
            ((heads, TILE, SPAN), f32, full(heads, TILE, SPAN)),
        ],
        scratch=[pltpu.VMEM((2 * BLOCK, lw), bf16)] * 2 + [pltpu.VMEM((2 * BLOCK, lw), f32)] * 2,
        flops=nb * 5 * pair_flops,
        nbytes=nb * BLOCK * lw * 24,
        exps=nb * heads * BLOCK * SPAN,
    )
    local_grads, dq, return_sum = lax.optimization_barrier((local_grads, dq, return_sum))
    odd = s_index & 1
    return_own = lax.dynamic_slice_in_dim(return_sum, odd * slab, slab, 0)
    return_other = lax.dynamic_slice_in_dim(return_sum, (1 - odd) * slab, slab, 0)
    return_got = lax.ppermute(return_other, "seq", flip)
    carries, grad_state = call(
        scan_back_kernel,
        (1,),
        (),
        [(local_grads, full(groups, share, lw)), (group_rows, full(groups, 1, lw))],
        [
            ((groups, share, lw), bf16, full(groups, share, lw)),
            ((share, lw), f32, full(share, lw)),
        ],
        flops=NS * lw * 2,
        nbytes=NS * lw * 4,
    )
    carried = swap(carries).reshape(NS, lw)

    next_kv = along(back_kv, -1)

    mid, row_part = call(
        functools.partial(query_grads_kernel, len(gas)),
        (width // cut,),
        (),
        [(x, pl.BlockSpec((x.shape[0], cut), lambda g: (0, g))) for x in gas]
        + [
            (mixed_all, full(nb, BLOCK, lw)),
            (normed_all, pl.BlockSpec((rows_all, cut), lambda g: (0, g))),
            (dq, full(rows_all, lw)),
            (w_query, pl.BlockSpec((cut, lw), lambda g: (g, 0))),
        ],
        [
            ((width, 2 * lw), bf16, pl.BlockSpec((cut, 2 * lw), lambda g: (g, 0))),
            ((8, width), f32, pl.BlockSpec((8, cut), lambda g: (0, g))),
        ],
        flops=4 * rows_all * width * lw,
        nbytes=rows_all * width * 4,
        mib=32,
        pin=range(16),
    )
    carried, mid, hidden_sum, return_got, *_ = lax.optimization_barrier(
        (carried, mid, hidden_sum, return_got, far_out)
    )
    mid = swap(mid.reshape(groups, width // groups, 2 * lw))
    result = (
        residual0 + stay[BLOCK:].astype(f32) + near_out[BLOCK:].astype(f32) + far_out.astype(f32)
    ).astype(bf16)

    (gu_all,) = call(
        carry_kernel,
        (1,),
        (t_pre,),
        [
            (carried, full(NS, lw)),
            (direct, full(nb, NS, lw)),
            (keep_rows, full(nb, 1, lw)),
            (gate_row, full(1, lw)),
        ],
        [((nb, NS, lw), bf16, full(nb, NS, lw))],
        flops=nb * NS * lw * 4,
        nbytes=nb * NS * lw * 6,
    )

    def learn_back(high, gu_all, grad_sq, dkv):
        pos = lambda *tail: pl.BlockSpec((1,) + tail, lambda g, t: (high - g, 0, 0))
        row = lambda cols, col=0: pl.BlockSpec((BLOCK, cols), lambda g, t: (high - g, col))
        return call(
            functools.partial(update_back_kernel, scale, heads, high, nb - 1),
            (2,),
            (t_pre,),
            [
                (gu_all, pos(NS, lw)),
                (qkv, row(lw, 1)),
                (qkv, row(lw, 2)),
                (state_queries, full(NS, lw)),
                (lse_u, pos(NS, 128)),
                (updates, pos(NS, lw)),
                (dq, row(lw)),
                (dk, pos(BLOCK, lw)),
                (dv, pos(BLOCK, lw)),
                (next_kv, pl.BlockSpec((BLOCK, lw), lambda g, t: (0, 0))),
                (next_kv, pl.BlockSpec((BLOCK, lw), lambda g, t: (0, 1))),
                (w_joined, full(width, 3 * lw)),
                (grad_sq, full(NS, lw)),
            ],
            [
                ((rows_all, 2 * lw), bf16, row(2 * lw)),
                ((BLOCK, width), bf16, full(BLOCK, width)),
                ((BLOCK, width), bf16, full(BLOCK, width)),
                ((NS, lw), f32, full(NS, lw)),
            ],
            [] if dkv is None else [(dkv, 0)],
            flops=20 * NS * BLOCK * lw + 12 * BLOCK * lw * width,
            nbytes=2 * BLOCK * (lw * 30 + width * 2),
            exps=2 * heads * NS * BLOCK,
        )

    dkv, part3, part2, grad_sq = learn_back(3, gu_all, jnp.zeros((NS, lw), f32), None)
    far = pair_sum(part2, core(part3))
    gu_all = hold(gu_all, far)
    far = cross(far)
    dkv, part1, part0, grad_sq = learn_back(1, gu_all, grad_sq, dkv)
    near = core(part1)

    late, gain_attn_part = call(
        key_grads_kernel,
        (width // cut,),
        (),
        [
            (normed_all, pl.BlockSpec((rows_all, cut), lambda g: (0, g))),
            (dkv, full(rows_all, 2 * lw)),
            (w_key, pl.BlockSpec((cut, lw), lambda g: (g, 0))),
            (w_value, pl.BlockSpec((cut, lw), lambda g: (g, 0))),
            (grad_sq, pl.BlockSpec((per * share, lw), lambda g: (g, 0))),
            (row_part, pl.BlockSpec((8, cut), lambda g: (0, g))),
        ],
        [
            (
                (groups, slab + share // 2, 2 * lw),
                bf16,
                pl.BlockSpec((per, slab + share // 2, 2 * lw), lambda g: (g, 0, 0)),
            ),
            ((8, width), f32, pl.BlockSpec((8, cut), lambda g: (0, g))),
        ],
        flops=4 * rows_all * width * lw,
        nbytes=rows_all * width * 4,
        mib=32,
    )
    (bias_line,) = call(
        bias_sum_kernel,
        (1,),
        (),
        [(hold(bias_grad, late), full(heads, TILE, SPAN))],
        [((heads, SPAN), f32, full(heads, SPAN))],
    )
    (gate_sum,) = call(
        gate_kernel,
        (1,),
        (t_pre,),
        [
            (hold(carried, late), full(NS, lw)),
            (direct, full(nb, NS, lw)),
            (entry, full(NS, lw)),
            (before, full(nb, NS, lw)),
            (carry_rows, full(nb, 1, lw)),
            (keep_rows, full(nb, 1, lw)),
            (gate_row, full(1, lw)),
        ],
        [((1, lw), f32, full(1, lw))],
        flops=nb * NS * lw * 8,
        nbytes=nb * NS * lw * 10,
    )
    late, gate_sum, bias_line, *_ = lax.optimization_barrier((late, gate_sum, bias_line, far))
    late = swap(late)
    bias_local = jnp.dot(bias_line, onehot, precision=lax.Precision.HIGHEST)

    bias_full = lax.dynamic_update_slice(
        jnp.zeros((H, BUCKETS), f32), bias_local, (t_index * heads, 0)
    )
    gate_full = lax.dynamic_update_slice(
        jnp.zeros((D,), f32), gate_sum[0] * gates * (1.0 - gates), (t_index * lw,)
    )
    small = jnp.concatenate(
        [
            gain_attn_part[0] / gain_attn,
            gain_mlp_part[0] / gain_mlp,
            gate_full,
            bias_full.reshape(-1),
        ]
    ).reshape(-1, 128)
    small = hold(small, mid)
    (grad_tokens,) = call(
        final_kernel,
        (2,),
        (),
        [(x, tall(width)) for x in (tokens, part0, near, far, grad_residual)]
        + [(gain_attn[None, :], full(1, width))],
        [((BLOCK, width), f32, tall(width))],
        flops=BLOCK * width * 12,
        nbytes=BLOCK * width * 16,
        pin=(0, 4),
    )

    small = small + core(small)
    small = small + cross(small)
    small, grad_tokens = lax.optimization_barrier((small, grad_tokens))
    step = 1
    while step < groups:
        small = small + lax.ppermute(small, "seq", [(i, i ^ step) for i in range(groups)])
        step *= 2
    small = small.reshape(-1)

    mid = jnp.sum(mid.astype(f32), axis=0)
    late = jnp.sum(late.astype(f32), axis=0)
    queries_sent = jnp.concatenate([late[slab:, :lw], late[slab:, lw:]])
    return (
        result,
        block_states,
        grad_tokens,
        grad_state,
        small[:D],
        mid[:, :lw],
        late[:slab, :lw],
        late[:slab, lw:],
        mid[:, lw:].T,
        small[3 * D :].reshape(H, BUCKETS),
        queries_sent,
        small[2 * D : 3 * D],
        small[D : 2 * D],
        hidden_sum.astype(f32),
        (return_own.astype(f32) + return_got.astype(f32)).T,
    )


def solution(mesh):
    return jax.shard_map(
        local,
        mesh=mesh,
        in_specs=(
            P(("seq", "tp"), None),
            P("seq"),
            P("seq"),
            P(None, "tp"),
            P(),
            P(None, "tp"),
            P(None, "tp"),
            P(None, "tp"),
            P("tp", None),
            P("tp", None),
            P(None, "tp"),
            P("tp"),
            P(),
            P(None, "tp"),
            P("tp", None),
            P(("seq", "tp"), None),
        ),
        out_specs=(
            P(("seq", "tp"), None),
            P("seq", None, "tp"),
            P(("seq", "tp"), None),
            P("seq", "tp"),
            P(),
            P("seq", "tp"),
            P("seq", "tp"),
            P("seq", "tp"),
            P("tp", "seq"),
            P(),
            P("seq", "tp"),
            P(),
            P(),
            P("seq", "tp"),
            P("tp", "seq"),
        ),
        check_vma=False,
    )
```

```python
import functools
import math

import jax
import jax.numpy as jnp
import numpy as np
from jax import lax
from jax.experimental import pallas as pl
from jax.experimental.pallas import tpu as pltpu
from jax.sharding import PartitionSpec as P

D = 1024
H = 8
NS = 512
BLOCK = 512
BUCKETS = 32
FAR = 128
TILE = 128
SPAN = BLOCK + TILE
HEAD = 128

eps = 1e-06
negative_fill = -1e30
LOG2E = math.log2(math.e)
WEIGHT = 0.05
HEAVY = 1.0
f32 = jnp.float32
bf16 = jnp.bfloat16


def nn(a, b):
    return lax.dot_general(a, b, (((1,), (0,)), ((), ())), preferred_element_type=f32)


def nt(a, b):
    return lax.dot_general(a, b, (((1,), (1,)), ((), ())), preferred_element_type=f32)


def tn(a, b):
    return lax.dot_general(a, b, (((0,), (0,)), ((), ())), preferred_element_type=f32)


def pinned(array):
    return pltpu.with_memory_space_constraint(array, pltpu.HBM)


def call(
    kernel, grid, prefetch, ins, outs, aliases=(), scratch=(), flops=0, nbytes=0, exps=0, mib=24,
    hbm=(), pin=(), weight=WEIGHT,
):
    any_spec = pl.BlockSpec(memory_space=pl.ANY)
    arrays = [
        pinned(array) if n in pin or array.ndim == 3 or array.shape[0] > D else array
        for n, (array, _) in enumerate(ins)
    ]
    arrays += [pinned(array) for array, _ in aliases]
    specs = [spec for _, spec in ins] + [any_spec for _ in aliases]
    first = len(prefetch) + len(ins)
    alias_map = {first + n: out for n, (_, out) in enumerate(aliases)}
    n_pre, n_in, n_alias = len(prefetch), len(ins), len(aliases)

    def body(*refs):
        kept = refs[: n_pre + n_in] + refs[n_pre + n_in + n_alias :]
        kernel(*kept)

    return pl.pallas_call(
        body,
        name=getattr(kernel, 'func', kernel).__name__,
        out_shape=[
            pltpu.HBM(shape, dtype)
            if len(shape) == 3 or shape[0] > D or n in hbm
            else jax.ShapeDtypeStruct(shape, dtype)
            for n, (shape, dtype, _) in enumerate(outs)
        ],
        grid_spec=pltpu.PrefetchScalarGridSpec(
            num_scalar_prefetch=n_pre,
            grid=grid,
            in_specs=specs,
            out_specs=[spec for _, _, spec in outs],
            scratch_shapes=list(scratch),
        ),
        input_output_aliases=alias_map,
        compiler_params=pltpu.CompilerParams(
            dimension_semantics=("arbitrary",) * len(grid), vmem_limit_bytes=mib * 1024 * 1024
        ),
        cost_estimate=pl.CostEstimate(
            flops=int(flops * weight),
            bytes_accessed=int(nbytes * weight),
            transcendentals=int(exps * weight),
        ),
    )(*prefetch, *arrays)


def lanes(*columns):
    rows = columns[0].shape[0]
    lane = lax.broadcasted_iota(jnp.int32, (rows, 128), 1)
    packed = jnp.broadcast_to(columns[0], (rows, 128))
    for n, column in enumerate(columns[1:], 1):
        packed = jnp.where(lane == n, column, packed)
    return packed


def pick(*columns):
    lane = lax.broadcasted_iota(jnp.int32, columns[0].shape, 1)
    packed = columns[0]
    for n, column in enumerate(columns[1:], 1):
        packed = jnp.where(lane == n, column, packed)
    return packed


def with_ones(values):
    return jnp.concatenate([values, jnp.ones((values.shape[0], HEAD), bf16)], axis=1)


def head_of(h):
    return slice(h * HEAD, (h + 1) * HEAD)


def bias_kernel(base_ref, out_ref):
    for h in range(out_ref.shape[0]):
        row = jnp.broadcast_to(base_ref[h : h + 1, :], (TILE, SPAN))
        out_ref[h] = pltpu.roll(row, 0, 1, stride=1, stride_axis=0)


def bias_sum_kernel(grad_ref, out_ref):
    rows = lax.broadcasted_iota(jnp.int32, (TILE, SPAN), 0)
    for h in range(grad_ref.shape[0]):
        value = grad_ref[h]
        step = 1
        while step < TILE:
            moved = pltpu.roll(value, SPAN - step, 1)
            value = jnp.where((rows & step) != 0, moved, value)
            step *= 2
        out_ref[h : h + 1, :] = jnp.sum(value, axis=0, keepdims=True)


def front_kernel(scale, heads, tok_a, tok_b, gain, w, sq, normed_out, qkv_out, u_out, lse_out):
    width = heads * HEAD
    first = pl.program_id(0) == 0
    rows = 256
    for i in range(BLOCK // rows):
        part = slice(i * rows, (i + 1) * rows)
        x = jnp.where(first, tok_a[part, :].astype(f32), tok_b[part, :].astype(f32))
        r = lax.rsqrt(jnp.mean(x * x, axis=-1, keepdims=True) + eps)
        n = (x * r * gain[...]).astype(bf16)
        normed_out[part, :] = n
        qkv_out[part, :] = nn(n, w[...]).astype(bf16)
    values = [
        with_ones(qkv_out[:, 2 * width + h * HEAD : 2 * width + (h + 1) * HEAD])
        for h in range(heads)
    ]

    def scores_of(i, h):
        k = qkv_out[:, width + h * HEAD : width + (h + 1) * HEAD]
        return nt(sq[i * rows : (i + 1) * rows, head_of(h)], k)

    work = [(i, h) for i in range(BLOCK // rows) for h in range(heads)]
    ready = scores_of(*work[0])
    stats = []
    for n, (i, h) in enumerate(work):
        s = ready * (scale * LOG2E)
        if n + 1 < len(work):
            ready = scores_of(*work[n + 1])
        part = slice(i * rows, (i + 1) * rows)
        m = jnp.max(s, axis=1, keepdims=True)
        p = jnp.exp2(s - m)
        both = nn(p.astype(bf16), values[h])
        total = both[:, HEAD:]
        u_out[0, part, head_of(h)] = both[:, :HEAD] / total
        stats.append(m + jnp.log(total) * LOG2E)
        if h == heads - 1:
            lse_out[0, part, :] = pick(*stats)
            stats = []


def masked(scale, h, raw, qid, kid, bias):
    return jnp.where(qid == kid, raw * (scale * LOG2E) + bias[h], negative_fill)


def window_kernel(scale, heads, t, q, kc, vc, kp, vp, qid, kid, bias, acc, ml, keys, values):
    keys[:BLOCK] = kp[...]
    keys[BLOCK:] = kc[...]
    values[:BLOCK] = vp[...]
    values[BLOCK:] = vc[...]

    def scores_of(i, h):
        part = slice(i * TILE, (i + 1) * TILE)
        return nt(q[part, head_of(h)], keys[i * TILE : i * TILE + SPAN, head_of(h)])

    work = [(i, h) for i in range(BLOCK // TILE) for h in range(heads)]
    ready = scores_of(*work[0])
    peaks, sums = [], []
    for n, (i, h) in enumerate(work):
        raw = ready
        if n + 1 < len(work):
            ready = scores_of(*work[n + 1])
        part = slice(i * TILE, (i + 1) * TILE)
        span = slice(i * TILE, i * TILE + SPAN)
        s = masked(scale, h, raw, qid[part, :], kid[0, :, span], bias)
        m = jnp.max(s, axis=1, keepdims=True)
        p = jnp.exp2(s - m)
        both = nn(p.astype(bf16), with_ones(values[span, head_of(h)]))
        acc[0, part, head_of(h)] = both[:, :HEAD]
        peaks.append(jnp.broadcast_to(m, (TILE, HEAD)))
        sums.append(both[:, HEAD:])
        if h == heads - 1:
            ml[0, part, :] = pick(*peaks, *sums)
            peaks, sums = [], []


def chain_kernel(t, updates, factors, before_out, total_out):
    state = jnp.zeros(total_out.shape, f32)
    for j in range(updates.shape[0]):
        before_out[j] = state
        state = factors[j] * state + updates[t[0] ^ j]
    total_out[...] = state.astype(bf16)


def scan_kernel(s, totals, factors, init, out):
    state = init[...]
    for g in range(totals.shape[0]):
        out[g] = state.astype(bf16)
        state = factors[g] * state + totals[g].astype(f32)


def chain_back_kernel(t, direct, gates, keep_rows, out):
    state = jnp.zeros(out.shape, f32)
    for j in reversed(range(direct.shape[0])):
        state = keep_rows[j] * (direct[t[0] ^ j] + gates[...] * state)
    out[...] = state.astype(bf16)


def scan_back_kernel(totals, factors, out, first_out):
    state = jnp.zeros(first_out.shape, f32)
    for g in reversed(range(totals.shape[0])):
        out[g] = state.astype(bf16)
        state = factors[g] * state + totals[g].astype(f32)
    first_out[...] = state


def carry_kernel(t, carried0, direct, keep_rows, gates, gu_out):
    now = carried0[...].astype(f32)
    for j in reversed(range(direct.shape[0])):
        gu_out[t[0] ^ j] = now.astype(bf16)
        now = keep_rows[j] * (direct[t[0] ^ j] + gates[...] * now)


def gate_kernel(t, carried0, direct, entry, before, carry_rows, keep_rows, gates, gate_out):
    now = carried0[...].astype(f32)
    start = entry[...].astype(f32)
    total = jnp.zeros(gate_out.shape, f32)
    for j in reversed(range(direct.shape[0])):
        used = carry_rows[j] * start + keep_rows[j] * before[j]
        total = total + jnp.sum(now * used, axis=0, keepdims=True)
        now = keep_rows[j] * (direct[t[0] ^ j] + gates[...] * now)
    gate_out[...] = total


def state_kernel(
    scale, heads, t, q, entry, before, carry_row, keep_row, acc, ml, w,
    mixed_out, stats_out, used_out, first_out, second_out,
):
    used_out[0] = (carry_row[0] * entry[...].astype(f32) + keep_row[0] * before[0]).astype(bf16)
    values = [with_ones(used_out[0, :, head_of(h)]) for h in range(heads)]
    rows = 256
    for i in range(BLOCK // rows):
        part = slice(i * rows, (i + 1) * rows)
        stats = []
        for h in range(heads):
            m = ml[0, part, h : h + 1]
            l = ml[0, part, heads + h : heads + h + 1]
            s = nt(q[part, head_of(h)], used_out[0, :, head_of(h)]) * (scale * LOG2E)
            top = jnp.maximum(m, jnp.max(s, axis=1, keepdims=True))
            p = jnp.exp2(s - top)
            shrink = jnp.exp2(m - top)
            both = nn(p.astype(bf16), values[h])
            total = l * shrink + both[:, HEAD:]
            value = (acc[0, part, head_of(h)] * shrink + both[:, :HEAD]) / total
            mixed_out[0, part, head_of(h)] = value.astype(bf16)
            stats.append(top + jnp.log(total) * LOG2E)
        stats_out[0, part, :] = pick(*stats)
    result = nn(mixed_out[0], w[...]).astype(bf16)
    first = pl.program_id(0) == 0

    @pl.when(first)
    def _():
        first_out[...] = result

    @pl.when(jnp.logical_not(first))
    def _():
        second_out[...] = result


def states_kernel(t, entry, before, carry_row, keep_row, gates, u, next_out):
    used = carry_row[0] * entry[...].astype(f32) + keep_row[0] * before[0]
    next_out[0] = gates[...] * used + u[0]


def return_kernel(hidden, w, away_out, stay_out):
    even = pl.program_id(0) % 2 == 0

    @pl.when(even)
    def _():
        away_out[...] = nn(hidden[...], w[...]).astype(bf16)

    @pl.when(jnp.logical_not(even))
    def _():
        stay_out[...] = nn(hidden[...], w[...]).astype(bf16)


def norm_kernel(tok, mine, theirs, gain, residual_out, nm_out):
    residual = tok[...].astype(f32) + (mine[...].astype(f32) + theirs[...].astype(f32))
    residual_out[...] = residual
    inverse = lax.rsqrt(jnp.mean(residual * residual, axis=-1, keepdims=True) + eps)
    nm_out[...] = (residual * inverse * gain[...]).astype(bf16)


def norm_back_kernel(
    cot, mine, theirs, residual, gain, grad_out, low_out, upper_out, lower_out
):
    r = residual[...]
    inverse = lax.rsqrt(jnp.mean(r * r, axis=-1, keepdims=True) + eps)
    scaled = r * inverse
    grad = (mine[...].astype(f32) + theirs[...].astype(f32)) * gain[...]
    inner = jnp.mean(grad * scaled, axis=-1, keepdims=True)
    result = cot[...].astype(f32) + inverse * (grad - scaled * inner)
    grad_out[...] = result
    low = result.astype(bf16)
    low_out[...] = low
    upper = pl.program_id(0) == 0

    @pl.when(upper)
    def _():
        upper_out[...] = low

    @pl.when(jnp.logical_not(upper))
    def _():
        lower_out[...] = low


def final_kernel(tok, mine, near, far, residual_grad, gain, out):
    x = tok[...].astype(f32)
    inverse = lax.rsqrt(jnp.mean(x * x, axis=-1, keepdims=True) + eps)
    scaled = x * inverse
    grad = mine[...].astype(f32) + near[...].astype(f32) + far[...].astype(f32)
    grad = grad * gain[...]
    inner = jnp.mean(grad * scaled, axis=-1, keepdims=True)
    out[...] = residual_grad[...] + inverse * (grad - scaled * inner)


def row_sums(value):
    sums = jnp.broadcast_to(jnp.sum(value, axis=1, keepdims=True), (value.shape[0], HEAD))
    return sums.T[:8]


def feed_grads_kernel(n, s, *refs):
    nms, cots = refs[:n], refs[n : 2 * n]
    gpre, hidden, w, kept_out, sent_out, return_out, gain_out = refs[2 * n :]
    odd = s[0] % 2 == 1
    rows = nms[0].shape[0]
    ff = w.shape[1]
    for which, left, right in ((0, nms, gpre), (1, cots, hidden)):
        total = None
        for r in range(n):
            piece = tn(left[r][...], right[r * rows : (r + 1) * rows, :])
            total = piece if total is None else total + piece
        low = total.astype(bf16)
        if which == 0:
            slab = kept_out.shape[1]
            for g in range(kept_out.shape[0]):
                even_rows = low[2 * g * slab : (2 * g + 1) * slab]
                odd_rows = low[(2 * g + 1) * slab : (2 * g + 2) * slab]
                kept_out[g] = jnp.where(odd, odd_rows, even_rows)
                sent_out[g] = jnp.where(odd, even_rows, odd_rows)
        else:
            return_out[...] = low
        if which == 0:
            gain_out[...] = row_sums(total * w[...].astype(f32))


def query_grads_kernel(n, *refs):
    gas = refs[:n]
    mixed, normed, dq, w, out, row_out = refs[n:]
    lw = dq.shape[1]
    total, at = None, 0
    for ga in gas:
        first = at % BLOCK
        piece = tn(ga[...], mixed[at // BLOCK, first : first + ga.shape[0]])
        total = piece if total is None else total + piece
        at += ga.shape[0]
    out[:, lw:] = total.astype(bf16)
    grad = tn(normed[...], dq[...])
    out[:, :lw] = grad.astype(bf16)
    row_out[...] = row_sums(grad * w[...].astype(f32))


def key_grads_kernel(normed, dkv, wk, wv, dsq, row, out, row_out):
    grad = tn(normed[...], dkv[...])
    rows, lw = grad.shape[0], wk.shape[1]
    slab = rows // out.shape[0]
    part = dsq.shape[0] // out.shape[0] // 2
    low = grad.astype(bf16)
    for g in range(out.shape[0]):
        out[g, :slab] = low[g * slab : (g + 1) * slab]
        out[g, slab:, :lw] = dsq[2 * g * part : (2 * g + 1) * part].astype(bf16)
        out[g, slab:, lw:] = dsq[(2 * g + 1) * part : (2 * g + 2) * part].astype(bf16)
    both = jnp.concatenate([wk[...].astype(f32), wv[...].astype(f32)], axis=1)
    row_out[...] = row[...] + row_sums(grad * both)


def mlp_kernel(steps, nm_a, nm_b, gact_a, gact_b, w, hidden_out, gpre_out, first_out, second_out):
    first = pl.program_id(0) < steps
    cols = 256
    x = jnp.where(first, nm_a[...], nm_b[...])
    for c in range(w.shape[1] // cols):
        cut = slice(c * cols, (c + 1) * cols)
        pre = nn(x, w[:, cut])
        cumulative = 0.5 * (1.0 + lax.erf(pre * (1.0 / math.sqrt(2.0))))
        density = jnp.exp2(pre * pre * (-0.5 * LOG2E)) * (1.0 / math.sqrt(2.0 * math.pi))
        hidden_out[:, cut] = (pre * cumulative).astype(bf16)
        gact = jnp.where(first, gact_a[:, cut].astype(f32), gact_b[:, cut].astype(f32))
        gpre_out[:, cut] = (gact * (cumulative + pre * density)).astype(bf16)
    result = nt(gpre_out[...], w[...]).astype(bf16)

    @pl.when(first)
    def _():
        first_out[...] = result

    @pl.when(jnp.logical_not(first))
    def _():
        second_out[...] = result


def state_back_kernel(
    scale, heads, ga_a, ga_b, ga_c, w, q, mixed, used, stats, gm_out, stats_out, dq_out, direct_out
):
    first = pl.program_id(0) == 0
    gm_out[0] = nt(jnp.where(first, ga_a[...], jnp.concatenate([ga_b[...], ga_c[...]])), w[...]).astype(bf16)
    raws = [
        (nt(q[:, head_of(h)], used[0, :, head_of(h)]), nt(gm_out[0, :, head_of(h)], used[0, :, head_of(h)]))
        for h in range(heads)
    ]
    logs, deltas = [], []
    for h, (raw, grad_p) in enumerate(raws):
        hs = head_of(h)
        gm = gm_out[0, :, hs]
        delta = jnp.sum(gm.astype(f32) * mixed[0, :, hs].astype(f32), axis=1, keepdims=True)
        lse = stats[0, :, h : h + 1]
        p = jnp.exp2(raw * (scale * LOG2E) - lse)
        ds = (p * (grad_p - delta)).astype(bf16)
        dq_out[0, :, hs] = nn(ds, used[0, :, hs]) * scale
        direct_out[0, :, hs] = tn(ds, q[:, hs]) * scale + tn(p.astype(bf16), gm)
        logs.append(lse)
        deltas.append(delta)
    stats_out[0] = lanes(*logs, *deltas)


def window_back_kernel(
    scale, heads, t, q, kc, vc, kb, vb, hk, hv, qid, kid, bias, gm, stats, dqs,
    dq_out, dk_out, dv_out, edge_out, grad_bias, keys, values, dkeys, dvalues,
):
    step = pl.program_id(0)
    last = pl.num_programs(0) - 1

    @pl.when(step == last)
    def _():
        keys[:BLOCK] = hk[...]
        values[:BLOCK] = hv[...]

    @pl.when(step != last)
    def _():
        keys[:BLOCK] = kb[...]
        values[:BLOCK] = vb[...]

    keys[BLOCK:] = kc[...]
    values[BLOCK:] = vc[...]

    @pl.when(step == 0)
    def _():
        dkeys[...] = jnp.zeros_like(dkeys)
        dvalues[...] = jnp.zeros_like(dvalues)
        grad_bias[...] = jnp.zeros_like(grad_bias)

    @pl.when(step != 0)
    def _():
        for total in (dkeys, dvalues):
            total[BLOCK:] = total[:BLOCK]
            total[:BLOCK] = jnp.zeros((BLOCK, total.shape[1]), f32)

    def scores_of(i, h):
        part = slice(i * TILE, (i + 1) * TILE)
        span = slice(i * TILE, i * TILE + SPAN)
        hs = head_of(h)
        return nt(q[part, hs], keys[span, hs]), nt(gm[0, part, hs], values[span, hs])

    work = [(i, h) for i in range(BLOCK // TILE) for h in range(heads)]
    ready = scores_of(*work[0])
    for n, (i, h) in enumerate(work):
        raw, grad_p = ready
        if n + 1 < len(work):
            ready = scores_of(*work[n + 1])
        part = slice(i * TILE, (i + 1) * TILE)
        span = slice(i * TILE, i * TILE + SPAN)
        hs = head_of(h)
        qt = q[part, hs]
        g = gm[0, part, hs]
        lse = stats[0, part, h : h + 1]
        delta = stats[0, part, heads + h : heads + h + 1]
        p = jnp.exp2(masked(scale, h, raw, qid[part, :], kid[0, :, span], bias) - lse)
        ds = p * (grad_p - delta)
        low = ds.astype(bf16)
        zero = jnp.zeros_like(qt)
        sides = jnp.concatenate(
            [jnp.concatenate([qt, zero], axis=1), jnp.concatenate([zero, g], axis=1)]
        )
        both = tn(jnp.concatenate([low, p.astype(bf16)]), sides)
        dq = nn(low, keys[span, hs]) * scale + dqs[0, part, hs]
        grad_bias[h] += ds
        dq_out[part, hs] = dq.astype(bf16)
        dkeys[span, hs] += both[:, :HEAD] * scale
        dvalues[span, hs] += both[:, HEAD:]
    dk_out[0] = dkeys[BLOCK:]
    dv_out[0] = dvalues[BLOCK:]

    @pl.when(step == last)
    def _():
        width = heads * HEAD
        edge_out[:, :width] = dkeys[:BLOCK].astype(bf16)
        edge_out[:, width:] = dvalues[:BLOCK].astype(bf16)


def update_back_kernel(
    scale, heads, high, last, t, gu_all, k, v, sq, lse_u, u, dq, dk, dv, hk, hv, w, dsq_in,
    dkv_out, first_out, second_out, dsq_out,
):
    width = heads * HEAD
    step = pl.program_id(0)
    edge = jnp.where((t[0] ^ (high - step)) == last, 1.0, 0.0)

    @pl.when(step == 0)
    def _():
        dsq_out[...] = dsq_in[...]

    raws = [
        (nt(sq[:, head_of(h)], k[:, head_of(h)]), nt(gu_all[0, :, head_of(h)], v[:, head_of(h)]))
        for h in range(heads)
    ]
    for h, (raw, grad_p) in enumerate(raws):
        hs = head_of(h)
        gu = gu_all[0, :, hs]
        sqh = sq[:, hs]
        kh = k[:, hs]
        delta = jnp.sum(gu.astype(f32) * u[0, :, hs], axis=1, keepdims=True)
        p = jnp.exp2(raw * (scale * LOG2E) - lse_u[0, :, h : h + 1])
        ds = (p * (grad_p - delta)).astype(bf16)
        dsq_out[:, hs] += nn(ds, kh) * scale
        dkh = dk[0, :, hs] + tn(ds, sqh) * scale + edge * hk[:, hs].astype(f32)
        dvh = dv[0, :, hs] + tn(p.astype(bf16), gu) + edge * hv[:, hs].astype(f32)
        dkv_out[:, hs] = dkh.astype(bf16)
        dkv_out[:, width + h * HEAD : width + (h + 1) * HEAD] = dvh.astype(bf16)
    part = nt(dq[...], w[:, :width]) + nt(dkv_out[...], w[:, width:])
    result = part.astype(bf16)

    @pl.when(step == 0)
    def _():
        first_out[...] = result

    @pl.when(step != 0)
    def _():
        second_out[...] = result


def bucket_of(distance):
    half = BUCKETS // 2
    limits = [math.ceil(half * (FAR / half) ** (level / half)) for level in range(1, half)]
    clipped = np.maximum(distance, 0)
    extra = sum((clipped >= limit).astype(np.int32) for limit in limits)
    return np.where(clipped < half, clipped, half + extra)


def local(
    tokens,
    doc_flags,
    reset_flags,
    state_init,
    gain_attn,
    w_query,
    w_key,
    w_value,
    w_output,
    bias_table,
    state_queries,
    gate_logits,
    gain_mlp,
    w_hidden,
    w_return,
    cotangent,
):
    heads = bias_table.shape[0]
    lw = w_query.shape[1]
    width = tokens.shape[1]
    nb = reset_flags.shape[0]
    ff = w_hidden.shape[1]
    scale = 1.0 / math.sqrt(HEAD)
    groups = lax.axis_size("seq")
    s_index = lax.axis_index("seq")
    t_index = lax.axis_index("tp")
    t_pre = t_index.astype(jnp.int32)[None]
    s_pre = s_index.astype(jnp.int32)[None]
    rows_all = nb * BLOCK

    def core(value):
        return lax.ppermute(value, "tp", [(i, i ^ 1) for i in range(nb)])

    def cross(value):
        return lax.ppermute(value, "tp", [(i, i ^ 2) for i in range(nb)])

    def along(value, step):
        pairs = [(i, i + step) for i in range(groups) if 0 <= i + step < groups]
        return lax.ppermute(value, "seq", pairs)

    def swap(value):
        return lax.all_to_all(value, "seq", 0, 0, tiled=True)

    def hold(value, *others):
        return lax.optimization_barrier((value, *others))[0]

    full = lambda *shape: pl.BlockSpec(shape, lambda *_: (0,) * len(shape))
    half = BLOCK // 2
    tall = lambda *tail: pl.BlockSpec((half,) + tail, lambda g, *_: (g, 0))
    share = NS // groups

    tok2 = cross(tokens)
    tok1 = core(tokens)

    gates = jax.nn.sigmoid(gate_logits)
    keeps = (1 - reset_flags).astype(f32)
    gate_row = gates[None, :]
    gate_group = gates
    for _ in range(nb - 1):
        gate_group = gate_group * gates
    apart = BLOCK - np.arange(SPAN)
    shown = (apart >= 0) & (apart < BLOCK)
    onehot = (bucket_of(apart)[:, None] == np.arange(BUCKETS)[None, :]) & shown[:, None]
    onehot = jnp.asarray(onehot.astype(np.float32))
    base = jnp.dot(bias_table * LOG2E, onehot.T, precision=lax.Precision.HIGHEST)
    base = jnp.where(jnp.asarray(shown)[None, :], base, negative_fill)
    (bias,) = call(
        bias_kernel,
        (1,),
        (),
        [(base, full(heads, SPAN))],
        [((heads, TILE, SPAN), f32, full(heads, TILE, SPAN))],
    )

    w_joined = jnp.concatenate([w_query, w_key, w_value], axis=1)
    def front(first, tok_a, tok_b, stacked):
        row = lambda cols: pl.BlockSpec((BLOCK, cols), lambda g: (first + g, 0))
        pos = lambda *tail: pl.BlockSpec((1,) + tail, lambda g: (first + g, 0, 0))
        return call(
            functools.partial(front_kernel, scale, heads),
            (2,),
            (),
            [
                (tok_a, full(BLOCK, width)),
                (tok_b, full(BLOCK, width)),
                (gain_attn[None, :], full(1, width)),
                (w_joined, full(width, 3 * lw)),
                (state_queries, full(NS, lw)),
            ],
            [
                ((rows_all, width), bf16, row(width)),
                ((rows_all, 3 * lw), bf16, row(3 * lw)),
                ((nb, NS, lw), f32, pos(NS, lw)),
                ((nb, NS, 128), f32, pos(NS, 128)),
            ],
            [] if stacked is None else [(array, n) for n, array in enumerate(stacked)],
            flops=4 * BLOCK * width * 3 * lw + 8 * NS * BLOCK * lw,
            nbytes=12 * BLOCK * width * 2,
            exps=2 * heads * NS * BLOCK,
        )

    starts = [jnp.ones_like(gates)]
    for j in range(nb - 1):
        starts.append(starts[j] * (gates * keeps[j]))
    carry_rows = (jnp.stack(starts) * keeps[:, None])[:, None, :]
    keep_rows = jnp.broadcast_to(keeps[:, None, None], (nb, 1, lw))
    block_rows = (keeps[:, None] * gates[None, :])[:, None, :]
    stacked = front(0, tokens, tok1, None)
    reset_sent, flags_sent, *stacked = lax.optimization_barrier((reset_flags, doc_flags, *stacked))
    every = swap(jnp.broadcast_to(reset_sent.reshape(1, nb), (groups, nb)))
    flag_prev = along(flags_sent[rows_all - BLOCK :], 1)
    tok2, bias, every, flag_prev, *stacked = lax.optimization_barrier(
        (tok2, bias, every, flag_prev, *stacked)
    )
    toks = [tokens, tok1, tok2, core(tok2)]
    cot1 = core(cotangent)
    stacked = list(front(2, toks[2], toks[3], stacked))
    every, flag_prev, *stacked = lax.optimization_barrier((every, flag_prev, *stacked))
    group_keep = jnp.prod((1 - every).astype(f32), axis=1)

    group_rows = (group_keep[:, None] * gate_group[None, :])[:, None, :]

    ids = jnp.cumsum(jnp.concatenate([flag_prev, doc_flags]))
    ids = jnp.where((jnp.arange(rows_all + BLOCK) < BLOCK) & (s_index == 0), -1, ids)
    id_rows = ids.reshape(nb + 1, 1, BLOCK)
    id_rows = jnp.concatenate([id_rows[:-1], id_rows[1:]], axis=2)
    id_cols = ids[BLOCK:].reshape(rows_all, 1)
    cot2, stacked[0] = lax.optimization_barrier((cotangent, stacked[0]))
    cot2 = cross(cot2)
    normed_all, qkv, updates, lse_u = stacked

    place = (t_index ^ (nb - 1)) * BLOCK
    edge = along(lax.dynamic_slice(qkv, (place, lw), (BLOCK, 2 * lw)), 1)

    before, total = call(
        chain_kernel,
        (1,),
        (t_pre,),
        [(updates, full(nb, NS, lw)), (block_rows, full(nb, 1, lw))],
        [((nb, NS, lw), f32, full(nb, NS, lw)), ((NS, lw), bf16, full(NS, lw))],
        flops=nb * NS * lw * 2,
        nbytes=nb * NS * lw * 8,
        hbm=(0,),
    )
    pair_flops = 2 * BLOCK * SPAN * lw

    def window(first, count, edge, stacked, weight):
        at = lambda col, back=0: pl.BlockSpec(
            (BLOCK, lw), lambda j, t: ((j + first - back) ^ t[0], col)
        )
        blk = lambda *tail: pl.BlockSpec((1,) + tail, lambda j, t: (j + first, 0, 0))
        if edge is None:
            before_block = [(qkv, at(1, 1)), (qkv, at(2, 1))]
        else:
            before_block = [
                (edge, pl.BlockSpec((BLOCK, lw), lambda j, t: (0, 0))),
                (edge, pl.BlockSpec((BLOCK, lw), lambda j, t: (0, 1))),
            ]
        return call(
            functools.partial(window_kernel, scale, heads),
            (count,),
            (t_pre,),
            [(qkv, at(0)), (qkv, at(1)), (qkv, at(2))]
            + before_block
            + [
                (id_cols, pl.BlockSpec((BLOCK, 1), lambda j, t: (j + first, 0))),
                (id_rows, pl.BlockSpec((1, 1, 2 * BLOCK), lambda j, t: (j + first, 0, 0))),
                (bias, full(heads, TILE, SPAN)),
            ],
            [
                ((nb, BLOCK, lw), f32, blk(BLOCK, lw)),
                ((nb, BLOCK, 128), f32, blk(BLOCK, 128)),
            ],
            [] if stacked is None else [(array, n) for n, array in enumerate(stacked)],
            flops=count * 2 * pair_flops,
            nbytes=count * BLOCK * lw * 12,
            exps=count * heads * BLOCK * SPAN,
            scratch=[pltpu.VMEM((2 * BLOCK, lw), bf16)] * 2,
            weight=weight,
        )

    windows = window(1, nb - 1, None, None, WEIGHT)
    late_edge, total, *windows = lax.optimization_barrier((edge, total, *windows))
    totals = swap(total.reshape(groups, share, lw))
    acc, ml = window(0, 1, late_edge, windows, HEAVY)
    cot2 = hold(cot2, acc)
    cots = [hold(cotangent, acc), hold(cot1, acc), cot2, core(cot2)]
    gacts = [nt(cot, w_return).astype(bf16) for cot in cots]
    totals, gacts[0], gacts[1] = lax.optimization_barrier((totals, gacts[0], gacts[1]))
    (entries,) = call(
        scan_kernel,
        (1,),
        (s_pre,),
        [
            (totals, full(groups, share, lw)),
            (group_rows, full(groups, 1, lw)),
            (state_init, pl.BlockSpec((share, lw), lambda g, s: (s[0], 0))),
        ],
        [((groups, share, lw), bf16, full(groups, share, lw))],
        flops=NS * lw * 2,
        nbytes=NS * lw * 4,
    )
    entry = swap(entries).reshape(NS, lw)

    entry, *gacts = lax.optimization_barrier((entry, *gacts))

    def attend(high, stacked):
        blk = lambda *tail: pl.BlockSpec((1,) + tail, lambda g, t: (t[0] ^ (high - g), 0, 0))
        pos = lambda *tail: pl.BlockSpec((1,) + tail, lambda g, t: (high - g, 0, 0))
        return call(
            functools.partial(state_kernel, scale, heads),
            (2,),
            (t_pre,),
            [
                (qkv, pl.BlockSpec((BLOCK, lw), lambda g, t: (high - g, 0))),
                (entry, full(NS, lw)),
                (before, blk(NS, lw)),
                (carry_rows, blk(1, lw)),
                (keep_rows, blk(1, lw)),
                (acc, blk(BLOCK, lw)),
                (ml, blk(BLOCK, 128)),
                (w_output, full(lw, width)),
            ],
            [
                ((nb, BLOCK, lw), bf16, pos(BLOCK, lw)),
                ((nb, BLOCK, 128), f32, pos(BLOCK, 128)),
                ((nb, NS, lw), bf16, pos(NS, lw)),
                ((BLOCK, width), bf16, full(BLOCK, width)),
                ((BLOCK, width), bf16, full(BLOCK, width)),
            ],
            [] if stacked is None else [(array, n) for n, array in enumerate(stacked)],
            flops=8 * BLOCK * NS * lw + 4 * BLOCK * lw * width,
            nbytes=2 * BLOCK * (lw * 24 + width * 2),
            exps=2 * heads * BLOCK * NS,
        )

    *stacked, part3, part2 = attend(3, None)
    *stacked, part1, part0 = attend(1, stacked)
    mixed_all, stats_f, used_low = stacked

    def pair_sum(mine, theirs):
        return (mine.astype(f32) + theirs.astype(f32)).astype(bf16)

    sum2 = pair_sum(part2, core(part3))
    sum0 = pair_sum(part0, core(part1))
    far2 = cross(sum2)
    blk = lambda *tail: pl.BlockSpec((1,) + tail, lambda g, t: (t[0] ^ g, 0, 0))
    pos = lambda *tail: pl.BlockSpec((1,) + tail, lambda g, t: (g, 0, 0))
    (block_states,) = call(
        states_kernel,
        (nb,),
        (t_pre,),
        [
            (hold(entry, sum0), full(NS, lw)),
            (before, blk(NS, lw)),
            (carry_rows, blk(1, lw)),
            (keep_rows, blk(1, lw)),
            (gate_row, full(1, lw)),
            (updates, pos(NS, lw)),
        ],
        [((nb, NS, lw), f32, blk(NS, lw))],
        flops=nb * NS * lw * 4,
        nbytes=nb * NS * lw * 12,
        hbm=(0,),
    )
    far2 = hold(far2, block_states)
    far0 = cross(hold(sum0, far2))

    def norm_mlp(tok, mine, theirs):
        return call(
            norm_kernel,
            (2,),
            (),
            [(x, tall(width)) for x in (tok, mine, theirs)] + [(gain_mlp[None, :], full(1, width))],
            [((BLOCK, width), f32, tall(width)), ((BLOCK, width), bf16, tall(width))],
            flops=BLOCK * width * 8,
            nbytes=BLOCK * width * 12,
            hbm=(0,),
        )

    def feed(first, nm_a, nm_b, stacked):
        early_tile = lambda cols: pl.BlockSpec((half, cols), lambda g: (jnp.minimum(g, 1), 0))
        late_tile = lambda cols: pl.BlockSpec((half, cols), lambda g: (jnp.maximum(g - 2, 0), 0))
        return call(
            functools.partial(mlp_kernel, 2),
            (4,),
            (),
            [
                (nm_a, early_tile(width)),
                (nm_b, late_tile(width)),
                (gacts[first], early_tile(ff)),
                (gacts[first + 1], late_tile(ff)),
                (w_hidden, full(width, ff)),
            ],
            [
                ((rows_all, ff), bf16, pl.BlockSpec((half, ff), lambda g: (2 * first + g, 0))),
                ((rows_all, ff), bf16, pl.BlockSpec((half, ff), lambda g: (2 * first + g, 0))),
                ((BLOCK, width), bf16, early_tile(width)),
                ((BLOCK, width), bf16, late_tile(width)),
            ],
            [] if stacked is None else [(array, n) for n, array in enumerate(stacked)],
            flops=8 * BLOCK * width * ff,
            nbytes=2 * BLOCK * width * 10,
            exps=4 * BLOCK * ff,
        )

    residual0, nm0 = norm_mlp(toks[0], sum0, far2)
    nm1 = core(nm0)
    *stacked, back0, back1 = feed(0, nm0, nm1, None)
    far0, back1 = lax.optimization_barrier((far0, back1))
    back0 = pair_sum(back0, core(back1))
    home0 = cross(back0)
    residual2, nm2 = norm_mlp(toks[2], sum2, far0)
    nm3 = core(nm2)
    *stacked, back2, back3 = feed(2, nm2, nm3, stacked)
    hidden_all, gpre_all = stacked
    slab = width // groups
    cut = 256
    per = cut // slab

    nms = [nm0, nm1, nm2, nm3]
    *feed_grads, gain_mlp_part = call(
        functools.partial(feed_grads_kernel, nb),
        (width // cut,),
        (s_pre,),
        [(x, pl.BlockSpec((BLOCK, cut), lambda g, s: (0, g))) for x in nms + cots]
        + [
            (gpre_all, full(rows_all, ff)),
            (hidden_all, full(rows_all, ff)),
            (w_hidden, pl.BlockSpec((cut, ff), lambda g, s: (g, 0))),
        ],
        [
            ((groups // 2, slab, ff), bf16, pl.BlockSpec((per // 2, slab, ff), lambda g, s: (g, 0, 0))),
            ((groups // 2, slab, ff), bf16, pl.BlockSpec((per // 2, slab, ff), lambda g, s: (g, 0, 0))),
            ((width, ff), bf16, pl.BlockSpec((cut, ff), lambda g, s: (g, 0))),
            ((8, width), f32, pl.BlockSpec((8, cut), lambda g, s: (0, g))),
        ],
        flops=4 * rows_all * width * ff,
        nbytes=rows_all * width * 8,
        mib=48,
        pin=range(nb, 16),
        hbm=range(4),
    )

    flip = [(i, i ^ 1) for i in range(groups)]
    columns = [list(range(side, groups, 2)) for side in range(2)]

    def over_columns(value):
        return lax.psum_scatter(
            value, "seq", scatter_dimension=0, tiled=True, axis_index_groups=columns
        )

    home0, back3, *feed_grads = lax.optimization_barrier((home0, back3, *feed_grads))
    back2 = pair_sum(back2, core(back3))
    home2 = cross(back2)

    def norm_mlp_back(cot, mine, theirs, residual):
        return call(
            norm_back_kernel,
            (2,),
            (),
            [(x, tall(width)) for x in (cot, mine, theirs, residual)]
            + [(gain_mlp[None, :], full(1, width))],
            [((BLOCK, width), f32, tall(width)), ((BLOCK, width), bf16, tall(width))]
            + [((half, width), bf16, full(half, width))] * 2,
            flops=BLOCK * width * 12,
            nbytes=BLOCK * width * 16,
            hbm=(0,),
            pin=(0, 1, 3),
        )

    hidden_got = lax.ppermute(feed_grads[1], "seq", flip)
    return_sum = over_columns(feed_grads[2])

    _, ga2, *ga2_halves = norm_mlp_back(cots[2], back2, home0, residual2)
    ga3 = [core(x) for x in ga2_halves]
    away, stay = call(
        return_kernel,
        (nb,),
        (),
        [
            (hidden_all, pl.BlockSpec((BLOCK, ff), lambda g: (nb - 1 - g, 0))),
            (w_return, full(ff, width)),
        ],
        [
            ((2 * BLOCK, width), bf16, pl.BlockSpec((BLOCK, width), lambda g: (g // 2, 0))),
            ((2 * BLOCK, width), bf16, pl.BlockSpec((BLOCK, width), lambda g: (jnp.maximum(g - 1, 0) // 2, 0))),
        ],
        flops=2 * rows_all * ff * width,
        nbytes=rows_all * (ff + width) * 2,
    )
    def attend_back(first, ga_a, ga_b, stacked):
        pos = lambda *tail: pl.BlockSpec((1,) + tail, lambda g: (first + g, 0, 0))
        return call(
            functools.partial(state_back_kernel, scale, heads),
            (2,),
            (),
            [
                (ga_a, full(BLOCK, width)),
                (ga_b[0], full(half, width)),
                (ga_b[1], full(half, width)),
                (w_output, full(lw, width)),
                (qkv, pl.BlockSpec((BLOCK, lw), lambda g: (first + g, 0))),
                (mixed_all, pos(BLOCK, lw)),
                (used_low, pos(NS, lw)),
                (stats_f, pos(BLOCK, 128)),
            ],
            [
                ((nb, BLOCK, lw), bf16, pos(BLOCK, lw)),
                ((nb, BLOCK, 128), f32, pos(BLOCK, 128)),
                ((nb, BLOCK, lw), f32, pos(BLOCK, lw)),
                ((nb, NS, lw), f32, pos(NS, lw)),
            ],
            [] if stacked is None else [(array, n) for n, array in enumerate(stacked)],
            flops=4 * BLOCK * lw * width + 20 * BLOCK * NS * lw,
            nbytes=2 * BLOCK * (width * 4 + lw * 16),
            exps=2 * heads * BLOCK * NS,
        )

    stacked = attend_back(2, ga2, ga3, None)
    hidden_got, *stacked = lax.optimization_barrier((hidden_got, *stacked))
    hidden_sum = (feed_grads[0].astype(f32) + hidden_got.astype(f32)).astype(bf16)
    home2, away, stay, hidden_sum, *stacked = lax.optimization_barrier(
        (home2, away, stay, hidden_sum, *stacked)
    )
    grad_residual, ga0, *ga0_halves = norm_mlp_back(cots[0], back0, home2, residual0)
    ga1 = [core(x) for x in ga0_halves]
    near_out = core(hold(away, home2))
    far_out = cross(pair_sum(stay[:BLOCK], near_out[:BLOCK]))
    gas = [ga0, *ga1, ga2, *ga3]
    hidden_sum, *stacked = lax.optimization_barrier((hidden_sum, *stacked))
    hidden_sum = over_columns(hidden_sum.reshape(width // 2, ff))
    stacked = list(attend_back(0, ga0, ga1, stacked))
    gm_all, stats_b, dq_state, direct = stacked

    (local_grad,) = call(
        chain_back_kernel,
        (1,),
        (t_pre,),
        [
            (direct, full(nb, NS, lw)),
            (gate_row, full(1, lw)),
            (keep_rows, full(nb, 1, lw)),
        ],
        [((NS, lw), bf16, full(NS, lw))],
        flops=nb * NS * lw * 2,
        nbytes=nb * NS * lw * 4,
    )
    local_grads = swap(local_grad.reshape(groups, share, lw))
    turn = lambda j: nb - 1 - j
    at = lambda col: pl.BlockSpec((BLOCK, lw), lambda j, t: (turn(j) ^ t[0], col))
    prev = lambda col: pl.BlockSpec(
        (BLOCK, lw), lambda j, t: (jnp.maximum(turn(j) - 1, 0) ^ t[0], col)
    )
    pos = lambda *tail: pl.BlockSpec((1,) + tail, lambda j, t: (turn(j) ^ t[0], 0, 0))
    dq, dk, dv, back_kv, bias_grad = call(
        functools.partial(window_back_kernel, scale, heads),
        (nb,),
        (t_pre,),
        [
            (qkv, at(0)),
            (qkv, at(1)),
            (qkv, at(2)),
            (qkv, prev(1)),
            (qkv, prev(2)),
            (edge, pl.BlockSpec((BLOCK, lw), lambda j, t: (0, 0))),
            (edge, pl.BlockSpec((BLOCK, lw), lambda j, t: (0, 1))),
            (id_cols, pl.BlockSpec((BLOCK, 1), lambda j, t: (turn(j), 0))),
            (id_rows, pl.BlockSpec((1, 1, 2 * BLOCK), lambda j, t: (turn(j), 0, 0))),
            (bias, full(heads, TILE, SPAN)),
            (gm_all, pos(BLOCK, lw)),
            (stats_b, pos(BLOCK, 128)),
            (dq_state, pos(BLOCK, lw)),
        ],
        [
            ((rows_all, lw), bf16, pl.BlockSpec((BLOCK, lw), lambda j, t: (turn(j) ^ t[0], 0))),
            ((nb, BLOCK, lw), f32, pos(BLOCK, lw)),
            ((nb, BLOCK, lw), f32, pos(BLOCK, lw)),
            ((BLOCK, 2 * lw), bf16, full(BLOCK, 2 * lw)),
            ((heads, TILE, SPAN), f32, full(heads, TILE, SPAN)),
        ],
        scratch=[pltpu.VMEM((2 * BLOCK, lw), bf16)] * 2 + [pltpu.VMEM((2 * BLOCK, lw), f32)] * 2,
        flops=nb * 5 * pair_flops,
        nbytes=nb * BLOCK * lw * 24,
        exps=nb * heads * BLOCK * SPAN,
    )
    local_grads, dq, return_sum = lax.optimization_barrier((local_grads, dq, return_sum))
    odd = s_index & 1
    return_own = lax.dynamic_slice_in_dim(return_sum, odd * slab, slab, 0)
    return_other = lax.dynamic_slice_in_dim(return_sum, (1 - odd) * slab, slab, 0)
    return_got = lax.ppermute(return_other, "seq", flip)
    carries, grad_state = call(
        scan_back_kernel,
        (1,),
        (),
        [(local_grads, full(groups, share, lw)), (group_rows, full(groups, 1, lw))],
        [
            ((groups, share, lw), bf16, full(groups, share, lw)),
            ((share, lw), f32, full(share, lw)),
        ],
        flops=NS * lw * 2,
        nbytes=NS * lw * 4,
    )
    carried = swap(carries).reshape(NS, lw)

    next_kv = along(back_kv, -1)

    mid, row_part = call(
        functools.partial(query_grads_kernel, len(gas)),
        (width // cut,),
        (),
        [(x, pl.BlockSpec((x.shape[0], cut), lambda g: (0, g))) for x in gas]
        + [
            (mixed_all, full(nb, BLOCK, lw)),
            (normed_all, pl.BlockSpec((rows_all, cut), lambda g: (0, g))),
            (dq, full(rows_all, lw)),
            (w_query, pl.BlockSpec((cut, lw), lambda g: (g, 0))),
        ],
        [
            ((width, 2 * lw), bf16, pl.BlockSpec((cut, 2 * lw), lambda g: (g, 0))),
            ((8, width), f32, pl.BlockSpec((8, cut), lambda g: (0, g))),
        ],
        flops=4 * rows_all * width * lw,
        nbytes=rows_all * width * 4,
        mib=32,
        pin=range(16),
    )
    carried, mid, hidden_sum, return_got, *_ = lax.optimization_barrier(
        (carried, mid, hidden_sum, return_got, far_out)
    )
    mid = swap(mid.reshape(groups, width // groups, 2 * lw))
    result = (
        residual0 + stay[BLOCK:].astype(f32) + near_out[BLOCK:].astype(f32) + far_out.astype(f32)
    ).astype(bf16)

    (gu_all,) = call(
        carry_kernel,
        (1,),
        (t_pre,),
        [
            (carried, full(NS, lw)),
            (direct, full(nb, NS, lw)),
            (keep_rows, full(nb, 1, lw)),
            (gate_row, full(1, lw)),
        ],
        [((nb, NS, lw), bf16, full(nb, NS, lw))],
        flops=nb * NS * lw * 4,
        nbytes=nb * NS * lw * 6,
    )

    def learn_back(high, gu_all, grad_sq, dkv):
        pos = lambda *tail: pl.BlockSpec((1,) + tail, lambda g, t: (high - g, 0, 0))
        row = lambda cols, col=0: pl.BlockSpec((BLOCK, cols), lambda g, t: (high - g, col))
        return call(
            functools.partial(update_back_kernel, scale, heads, high, nb - 1),
            (2,),
            (t_pre,),
            [
                (gu_all, pos(NS, lw)),
                (qkv, row(lw, 1)),
                (qkv, row(lw, 2)),
                (state_queries, full(NS, lw)),
                (lse_u, pos(NS, 128)),
                (updates, pos(NS, lw)),
                (dq, row(lw)),
                (dk, pos(BLOCK, lw)),
                (dv, pos(BLOCK, lw)),
                (next_kv, pl.BlockSpec((BLOCK, lw), lambda g, t: (0, 0))),
                (next_kv, pl.BlockSpec((BLOCK, lw), lambda g, t: (0, 1))),
                (w_joined, full(width, 3 * lw)),
                (grad_sq, full(NS, lw)),
            ],
            [
                ((rows_all, 2 * lw), bf16, row(2 * lw)),
                ((BLOCK, width), bf16, full(BLOCK, width)),
                ((BLOCK, width), bf16, full(BLOCK, width)),
                ((NS, lw), f32, full(NS, lw)),
            ],
            [] if dkv is None else [(dkv, 0)],
            flops=20 * NS * BLOCK * lw + 12 * BLOCK * lw * width,
            nbytes=2 * BLOCK * (lw * 30 + width * 2),
            exps=2 * heads * NS * BLOCK,
        )

    dkv, part3, part2, grad_sq = learn_back(3, gu_all, jnp.zeros((NS, lw), f32), None)
    far = pair_sum(part2, core(part3))
    gu_all = hold(gu_all, far)
    far = cross(far)
    dkv, part1, part0, grad_sq = learn_back(1, gu_all, grad_sq, dkv)
    near = core(part1)

    late, gain_attn_part = call(
        key_grads_kernel,
        (width // cut,),
        (),
        [
            (normed_all, pl.BlockSpec((rows_all, cut), lambda g: (0, g))),
            (dkv, full(rows_all, 2 * lw)),
            (w_key, pl.BlockSpec((cut, lw), lambda g: (g, 0))),
            (w_value, pl.BlockSpec((cut, lw), lambda g: (g, 0))),
            (grad_sq, pl.BlockSpec((per * share, lw), lambda g: (g, 0))),
            (row_part, pl.BlockSpec((8, cut), lambda g: (0, g))),
        ],
        [
            (
                (groups, slab + share // 2, 2 * lw),
                bf16,
                pl.BlockSpec((per, slab + share // 2, 2 * lw), lambda g: (g, 0, 0)),
            ),
            ((8, width), f32, pl.BlockSpec((8, cut), lambda g: (0, g))),
        ],
        flops=4 * rows_all * width * lw,
        nbytes=rows_all * width * 4,
        mib=32,
    )
    (bias_line,) = call(
        bias_sum_kernel,
        (1,),
        (),
        [(hold(bias_grad, late), full(heads, TILE, SPAN))],
        [((heads, SPAN), f32, full(heads, SPAN))],
    )
    (gate_sum,) = call(
        gate_kernel,
        (1,),
        (t_pre,),
        [
            (hold(carried, late), full(NS, lw)),
            (direct, full(nb, NS, lw)),
            (entry, full(NS, lw)),
            (before, full(nb, NS, lw)),
            (carry_rows, full(nb, 1, lw)),
            (keep_rows, full(nb, 1, lw)),
            (gate_row, full(1, lw)),
        ],
        [((1, lw), f32, full(1, lw))],
        flops=nb * NS * lw * 8,
        nbytes=nb * NS * lw * 10,
    )
    late, gate_sum, bias_line, *_ = lax.optimization_barrier((late, gate_sum, bias_line, far))
    late = swap(late)
    bias_local = jnp.dot(bias_line, onehot, precision=lax.Precision.HIGHEST)

    bias_full = lax.dynamic_update_slice(
        jnp.zeros((H, BUCKETS), f32), bias_local, (t_index * heads, 0)
    )
    gate_full = lax.dynamic_update_slice(
        jnp.zeros((D,), f32), gate_sum[0] * gates * (1.0 - gates), (t_index * lw,)
    )
    small = jnp.concatenate(
        [
            gain_attn_part[0] / gain_attn,
            gain_mlp_part[0] / gain_mlp,
            gate_full,
            bias_full.reshape(-1),
        ]
    ).reshape(-1, 128)
    small = hold(small, mid)
    (grad_tokens,) = call(
        final_kernel,
        (2,),
        (),
        [(x, tall(width)) for x in (tokens, part0, near, far, grad_residual)]
        + [(gain_attn[None, :], full(1, width))],
        [((BLOCK, width), f32, tall(width))],
        flops=BLOCK * width * 12,
        nbytes=BLOCK * width * 16,
        pin=(0, 4),
    )

    small = small + core(small)
    small = small + cross(small)
    step = 1
    while step < groups:
        small = small + lax.ppermute(small, "seq", [(i, i ^ step) for i in range(groups)])
        if step == 1:
            small, grad_tokens = lax.optimization_barrier((small, grad_tokens))
        step *= 2
    small = small.reshape(-1)

    mid = jnp.sum(mid.astype(f32), axis=0)
    late = jnp.sum(late.astype(f32), axis=0)
    queries_sent = jnp.concatenate([late[slab:, :lw], late[slab:, lw:]])
    return (
        result,
        block_states,
        grad_tokens,
        grad_state,
        small[:D],
        mid[:, :lw],
        late[:slab, :lw],
        late[:slab, lw:],
        mid[:, lw:].T,
        small[3 * D :].reshape(H, BUCKETS),
        queries_sent,
        small[2 * D : 3 * D],
        small[D : 2 * D],
        hidden_sum.astype(f32),
        (return_own.astype(f32) + return_got.astype(f32)).T,
    )


def solution(mesh):
    return jax.shard_map(
        local,
        mesh=mesh,
        in_specs=(
            P(("seq", "tp"), None),
            P("seq"),
            P("seq"),
            P(None, "tp"),
            P(),
            P(None, "tp"),
            P(None, "tp"),
            P(None, "tp"),
            P("tp", None),
            P("tp", None),
            P(None, "tp"),
            P("tp"),
            P(),
            P(None, "tp"),
            P("tp", None),
            P(("seq", "tp"), None),
        ),
        out_specs=(
            P(("seq", "tp"), None),
            P("seq", None, "tp"),
            P(("seq", "tp"), None),
            P("seq", "tp"),
            P(),
            P("seq", "tp"),
            P("seq", "tp"),
            P("seq", "tp"),
            P("tp", "seq"),
            P(),
            P("seq", "tp"),
            P(),
            P(),
            P("seq", "tp"),
            P("tp", "seq"),
        ),
        check_vma=False,
    )
```
